32 devices in a mesh: groups: 2 (over y), feat: 4 (over z), layer: 2 (over x), row: 2 (over core).
Axes of the slice: x: 2, y: 2, z: 4, core: 2. Of those that a mesh axis runs over, the one named last changes fastest.
Arguments:
- resid_buf: bfloat16 [512, 2, 4608], P(('groups', 'feat', 'row')), parts along dimension 0, may hold values from -6 to 6
- shuffle: int32 [512], P('groups'), parts along dimension 0, may hold values from 0 to 255, each once
- mlp_out: bfloat16 [512, 2, 4608], P(('groups', 'feat', 'row')), parts along dimension 0, may hold values from -5 to 5
- enc_weight: bfloat16 [2, 8192, 4608], P('layer', 'feat', 'row'), may hold values from -0.09375 to 0.09375
- dec_weight: bfloat16 [2, 8192, 2, 4608], P('layer', 'feat', None, 'row'), may hold values from -0.0625 to 0.0625
- enc_bias: float32 [2, 8192], P('layer', 'feat'), may hold values from -0.5 to 0.5
- dec_bias: float32 [2, 4608], replicated, may hold values from -3 to 3
Outputs:
- rebuilt: bfloat16 [512, 2, 4608], P(('groups', 'feat', 'row')), parts along dimension 0
- enc_grad: bfloat16 [4, 8192, 4608], P(('groups', 'layer'), 'feat', 'row'), parts along dimension 0
- dec_grad: bfloat16 [4, 8192, 2, 4608], P(('groups', 'layer'), 'feat', None, 'row'), parts along dimension 0
- bias_grad: float32 [4, 8192], P(('groups', 'layer'), 'feat'), parts along dimension 0
The draws below stay inside these ranges and needn't reach their ends.
There are 2 independent parts, one for each index of `groups`. The reference program is written for one: setup_inputs(seed, part) draws one part's arguments, and reference() takes and returns one part's arrays. A program takes and returns all parts, laid end to end along the dimension named above; an argument that names none is the same for every part. Nothing has to cross between parts.
Inputs may be any that keep to these rules, and one draw needn't show every extreme that they name: `shuffle`: a permutation of the 256 buffer rows.
All inputs are finite; a program needn't handle non-finite values.
Results may differ from the reference program's by a relative error of at most 0.04.
Values may be sent and summed in bfloat16 or wider, within the bound.
A program may use at most 128 MiB of HBM per device.

```python
import jax
import jax.numpy as jnp

D = 4608
F = 8192
LAYERS = 2
ROWS = 256
FSEC = 8192
N_LAYER = 2


def steps_of(rng, shape, pieces, smallest, largest):
    def one(position, shards_of):
        steps = jax.random.uniform(jax.random.fold_in(jax.random.fold_in(rng, 6), position), (shards_of,), jnp.float32, smallest / len(pieces), largest / len(pieces))
        return jnp.repeat(jnp.exp(steps), shape[position] // shards_of).reshape((-1,) + (1,) * (len(shape) - position - 1))

    gain = one(*pieces[0])
    for cut in pieces[1:]:
        gain = gain * one(*cut)
    return gain


def centred(rng, shape, scale, limit, pieces=(), held_as=jnp.bfloat16):
    array = jax.random.normal(rng, shape, jnp.float32) * scale
    if len(pieces) > 0:
        array = steps_of(rng, shape, pieces, -0.22, 0.18) * array
    return jnp.clip(array, min=-limit, max=limit).astype(held_as)


def setup_inputs(seed: int = 0, part: int = 0) -> dict:
    seeds = jax.random.split(jax.random.key(seed), 8)
    own_keys = jax.random.split(jax.random.fold_in(seeds[7], part), 8)
    resid_buf = centred(own_keys[0], (ROWS, LAYERS, D), 1.0, 6.0, ((0, 8),))
    shuffle = jax.random.permutation(own_keys[1], ROWS).astype(jnp.int32)
    mlp_out = centred(own_keys[2], (ROWS, LAYERS, D), 0.7, 5.0, ((0, 8),))
    enc_weight = centred(seeds[3], (N_LAYER, FSEC, D), D ** -0.5, 0.09375, ((0, 2), (1, 4), (2, 2)))
    dec_weight = centred(seeds[4], (N_LAYER, FSEC, 2, D), F ** -0.5, 0.0625, ((0, 2), (1, 4), (3, 2)))
    enc_bias = jnp.clip(jax.random.uniform(seeds[5], (N_LAYER, FSEC), jnp.float32, -0.5, 0.5) * steps_of(seeds[5], (N_LAYER, FSEC), ((0, 2), (1, 4)), -0.4, 0.0), -0.5, 0.5)
    dec_bias = centred(seeds[6], (LAYERS, D), 0.5, 3.0, (), jnp.float32)
    return {"resid_buf": resid_buf, "shuffle": shuffle, "mlp_out": mlp_out, "enc_weight": enc_weight, "dec_weight": dec_weight, "enc_bias": enc_bias, "dec_bias": dec_bias}


def reference(resid_buf, shuffle, mlp_out, enc_weight, dec_weight, enc_bias, dec_bias):
    encoders = enc_weight.reshape(LAYERS, F, D)
    decoders = dec_weight.reshape(LAYERS, F, 2, D)
    biases = enc_bias.reshape(LAYERS, F)
    inputs = jnp.take(resid_buf, shuffle.astype(jnp.int32), axis=0)
    loss_scale = float(ROWS) ** -0.5
    pre_list = []
    feature_list = []
    for source in range(LAYERS):
        pre_act = jnp.dot(inputs[:, source], encoders[source].T, preferred_element_type=jnp.float32) + biases[source]
        pre_list.append(pre_act)
        feature_list.append(jnp.maximum(pre_act, 0.0).astype(jnp.bfloat16))
    rebuilt_list = []
    for target in range(LAYERS):
        total = jnp.zeros((ROWS, D), jnp.float32) + dec_bias[target]
        for source in range(target + 1):
            total = total + jnp.dot(feature_list[source], decoders[source, :, target - source], preferred_element_type=jnp.float32)
        rebuilt_list.append(total)
    recon_sum = jnp.stack(rebuilt_list, axis=1)
    errors = (recon_sum - mlp_out.astype(jnp.float32)).astype(jnp.bfloat16)
    enc_list = []
    dec_list = []
    bias_list = []
    for source in range(LAYERS):
        own_err = errors[:, source]
        grad_feats = jnp.dot(own_err, decoders[source, :, 0].T, preferred_element_type=jnp.float32)
        own_dec = loss_scale * jnp.dot(feature_list[source].T, own_err, preferred_element_type=jnp.float32)
        if source + 1 < LAYERS:
            next_err = errors[:, source + 1]
            grad_feats = grad_feats + jnp.dot(next_err, decoders[source, :, 1].T, preferred_element_type=jnp.float32)
            next_dec = loss_scale * jnp.dot(feature_list[source].T, next_err, preferred_element_type=jnp.float32)
        else:
            next_dec = jnp.zeros((F, D), jnp.float32)
        grad_feats = grad_feats * loss_scale
        grad_pre = jnp.where(pre_list[source] > 0, grad_feats, 0.0).astype(jnp.bfloat16)
        enc_list.append(jnp.dot(grad_pre.T, inputs[:, source], preferred_element_type=jnp.float32).astype(jnp.bfloat16))
        dec_list.append(jnp.stack([own_dec, next_dec], axis=1).astype(jnp.bfloat16))
        bias_list.append(jnp.sum(grad_pre.astype(jnp.float32), axis=0))
    enc_grad = jnp.stack(enc_list, axis=0).reshape(N_LAYER, FSEC, D)
    dec_grad = jnp.stack(dec_list, axis=0).reshape(N_LAYER, FSEC, 2, D)
    bias_grad = jnp.stack(bias_list, axis=0).reshape(N_LAYER, FSEC)
    return (recon_sum.astype(jnp.bfloat16), enc_grad, dec_grad, bias_grad)
```

```python
import functools

import jax
import jax.numpy as jnp
from jax import lax
from jax.experimental import pallas as pl
from jax.experimental.pallas import tpu as pltpu
from jax.sharding import PartitionSpec as P

LAYERS = 2


def from_behind(block, axis, distance):
    devices = range(lax.axis_size(axis))
    route = [(i - distance, i) for i in devices if i - distance in devices]
    return lax.ppermute(block, axis, route)


def dot_last(left, right):
    return lax.dot_general(
        left, right, (((1,), (1,)), ((), ())), preferred_element_type=jnp.float32
    )


def dot_first(left, right):
    return lax.dot_general(
        left, right, (((0,), (0,)), ((), ())), preferred_element_type=jnp.float32
    )


def on_device(resid_buf, shuffle, mlp_out, enc_weight, dec_weight, enc_bias, dec_bias):
    feat_count = lax.axis_size("feat")
    row_count = lax.axis_size("row")
    sub_blocks = lax.axis_size("layer") // LAYERS
    layer_pos = lax.axis_index("layer")
    row_pos = lax.axis_index("row")
    source = layer_pos // sub_blocks
    rows_each = resid_buf.shape[0]
    width = dec_bias.shape[1]
    half_width = enc_weight.shape[2]
    local_rows = rows_each * feat_count
    total_rows = local_rows * row_count
    loss_scale = float(total_rows) ** (-0.5)
    own_layer = lax.dynamic_index_in_dim(resid_buf, source, axis=1, keepdims=False)
    buffer_all = lax.all_gather(own_layer, ("feat", "row"), axis=0, tiled=True)
    batch_rows = jnp.take(buffer_all, shuffle, axis=0)
    blocks = batch_rows.reshape(feat_count, row_count, rows_each, width)
    inputs_half = lax.dynamic_slice_in_dim(
        jnp.swapaxes(blocks, 0, 1), row_pos * half_width, half_width, axis=3
    )
    inputs_half = inputs_half.reshape(total_rows, half_width)
    own_half_dec = dec_weight[0][:, 0]
    next_half_dec = dec_weight[0][:, 1]
    pre_all = lax.psum(dot_last(inputs_half, enc_weight[0]), "row") + enc_bias[0]
    features_all = jnp.maximum(pre_all, 0.0).astype(jnp.bfloat16)
    own_part = jnp.dot(features_all, own_half_dec, preferred_element_type=jnp.float32)
    next_part = jnp.dot(features_all, next_half_dec, preferred_element_type=jnp.float32)
    carried = from_behind(next_part, "layer", sub_blocks)
    spread = (own_part + carried).reshape(row_count, local_rows, half_width)
    halves = lax.psum_scatter(spread, "feat", scatter_dimension=1, tiled=True)
    joined = lax.all_to_all(halves, "row", split_axis=0, concat_axis=2, tiled=True)
    section_sum = joined.reshape(rows_each, width)
    target_ids = jnp.arange(LAYERS, dtype=jnp.int32)
    target_slots = jnp.where((target_ids == source)[:, None, None], section_sum[None], 0.0)
    totals = lax.psum(target_slots, "layer")
    recon_sum = jnp.swapaxes(totals, 0, 1) + dec_bias[None]
    errors = (recon_sum - mlp_out.astype(jnp.float32)).astype(jnp.bfloat16)
    gathered = lax.all_gather(errors, ("feat", "row"), axis=0, tiled=True)
    error_grid = gathered.reshape(feat_count, row_count, rows_each, LAYERS, width)
    errors_mine = lax.dynamic_index_in_dim(error_grid, row_pos, axis=1, keepdims=False)
    errors_mine = errors_mine.reshape(local_rows, LAYERS, width)
    errors_half = lax.dynamic_slice_in_dim(
        jnp.swapaxes(error_grid, 0, 1), row_pos * half_width, half_width, axis=4
    )
    errors_half = errors_half.reshape(total_rows, LAYERS, half_width)
    live_next = source + 1 < LAYERS
    next_index = jnp.minimum(source + 1, LAYERS - 1)
    half_own = lax.dynamic_index_in_dim(errors_half, source, axis=1, keepdims=False)
    half_next = lax.dynamic_index_in_dim(errors_half, next_index, axis=1, keepdims=False)
    half_next = jnp.where(live_next, half_next, jnp.zeros_like(half_next))
    half_terms = dot_last(half_own, own_half_dec) + dot_last(half_next, next_half_dec)
    grad_feats = lax.psum(half_terms, "row") * loss_scale
    grad_all = jnp.where(pre_all > 0, grad_feats, 0.0).astype(jnp.bfloat16)
    grad_own = loss_scale * dot_first(features_all, half_own)
    grad_next = loss_scale * dot_first(features_all, half_next)
    enc_grad = dot_first(grad_all, inputs_half).astype(jnp.bfloat16)
    dec_grad = jnp.stack([grad_own, grad_next], axis=1).astype(jnp.bfloat16)
    bias_grad = jnp.sum(grad_all.astype(jnp.float32), axis=0)
    return (recon_sum.astype(jnp.bfloat16), enc_grad[None], dec_grad[None], bias_grad[None])

KC = 256
DC = 128
MESH = pl.DeviceIdType.MESH
VMEM_LIMIT = 67043328
BF = jnp.bfloat16


def pick(rows, cols, stride, offset):
    r = lax.broadcasted_iota(jnp.int32, (rows, cols), 0)
    c = lax.broadcasted_iota(jnp.int32, (rows, cols), 1)
    return (c == stride * r + offset).astype(BF)


def spread_to(offset):
    r = lax.broadcasted_iota(jnp.int32, (2 * DC, DC), 0)
    c = lax.broadcasted_iota(jnp.int32, (2 * DC, DC), 1)
    return (r == 2 * c + offset).astype(BF)


def mm(left, right):
    return jnp.dot(left, right, preferred_element_type=jnp.float32)


def step_kernel(
    n, J, res, shuf, mlp, enc, dec, bias, dbias,
    fx, xs, errs, gpre, parts,
    feats, enc_v, wv, raw, xsend, xg, mlpx, msend, pre_own, pre_send, pre_recv, fall,
    nsend, nrecv, facc, osend, rrecv, e0, e1, rc, rb, g_own, g_send, g_recv, gall,
    sem_l, sem_raw, x_s, x_r, m_s, m_r, p_s, p_r, f_s, f_r, n_s, n_r, r_s, r_r,
    e_s, e_r, t_s, t_r, b_s, b_r, g_s, g_r, q_s, q_r, y_s, w_s,
):
    z = lax.axis_index("feat")
    x = lax.axis_index("layer")
    c = lax.axis_index("row")
    R, H = xsend.shape[1:]
    F = enc_v.shape[0]
    T = xs.shape[0]
    T2, CR, NC = T // 2, 2 * R, H // J
    nk = F // KC
    scale = float(T) ** (-0.5)
    other_c, other_x = 1 - c, 1 - x

    def far(dz):
        return lax.rem(z + dz, n)

    def back(dz):
        return lax.rem(z + n - dz, n)

    def remote(src, dst, send, recv, **where):
        return pltpu.make_async_remote_copy(
            src_ref=src, dst_ref=dst, send_sem=send, recv_sem=recv,
            device_id=where, device_id_type=MESH)

    line = n == 4

    def unless_ends(dz, act):
        if line and dz == n - 1:
            pl.when(z != 0)(act)
        elif line and dz == 1:
            pl.when(z != n - 1)(act)
        else:
            act()

    def relays(act):
        if line:
            pl.when(z == 2)(lambda: act(1, 3))
            pl.when(z == 1)(lambda: act(3, 1))

    orders = (2, 1, 3) if line else tuple(range(1, n))

    enc_copy = pltpu.make_async_copy(enc, enc_v, sem_l)
    enc_copy.start()

    def raw_copy(i, slot):
        return pltpu.make_async_copy(
            dec.reshape(2 * F, H).at[pl.ds(pl.multiple_of(i * 2 * DC, 2 * DC), 2 * DC)], raw.at[slot], sem_raw.at[slot])

    raw_copy(0, 0).start()

    barrier = pltpu.get_barrier_semaphore()
    for dz in range(n):
        if dz:
            pl.semaphore_signal(barrier, inc=1, device_id={"feat": far(dz), "row": c}, device_id_type=MESH)
        pl.semaphore_signal(barrier, inc=1, device_id={"feat": far(dz), "row": other_c}, device_id_type=MESH)
    for cc in (c, other_c):
        pl.semaphore_signal(barrier, inc=1, device_id={"layer": other_x, "row": cc}, device_id_type=MESH)

    own_x = mm(pick(R, 2 * R, 2, x), res.reshape(2 * R, 2 * H)[...]).astype(BF)
    x_mine = jnp.where(c == 0, own_x[:, :H], own_x[:, H:])
    xsend[0] = x_mine
    xsend[1] = jnp.where(c == 0, own_x[:, H:], own_x[:, :H])
    xg[z, c] = x_mine
    own_m = mm(pick(R, 2 * R, 2, x), mlp.reshape(2 * R, 2 * H)[...]).astype(BF)
    mlpx[c] = jnp.where(c == 0, own_m[:, :H], own_m[:, H:])
    msend[...] = jnp.where(c == 0, own_m[:, H:], own_m[:, :H])

    pl.semaphore_wait(barrier, 2 * n + 1)

    def x_copy(dz, k):
        return remote(xsend.at[k], xg.at[z, c], x_s.at[dz, k], x_r.at[dz, k],
                      feat=far(dz), row=c if k == 0 else other_c)

    x_list = [(dz, k) for dz in orders for k in range(2)] + [(0, 1)]
    for dz, k in x_list:
        unless_ends(dz, lambda: x_copy(dz, k).start())

    def y_copy(k, to, at):
        cc = c if k == 0 else other_c
        return remote(xg.at[back(2), cc], xg.at[back(2), cc], y_s.at[k], x_r.at[at, k], feat=far(to))

    m_copy = remote(msend, mlpx.at[c], m_s, m_r, row=other_c)
    m_copy.start()

    apart = jnp.concatenate([pick(DC, 2 * DC, 2, 0), pick(DC, 2 * DC, 2, 1)], axis=0)
    nd = F // DC

    def split_body(i, carry):
        slot = lax.rem(i, 2)

        @pl.when(i + 1 < nd)
        def _():
            raw_copy(i + 1, 1 - slot).start()

        raw_copy(i, slot).wait()
        both = mm(apart, raw[slot]).astype(BF)
        rows = pl.ds(pl.multiple_of(i * DC, DC), DC)
        wv[0, rows, :] = both[:DC]
        wv[1, rows, :] = both[DC:]
        return carry

    lax.fori_loop(0, nd // 2, split_body, 0)
    if line:
        for k in range(2):
            x_copy(2, k).wait_recv()
            relays(lambda to, at: y_copy(k, to, at).start())
    lax.fori_loop(nd // 2, nd, split_body, 0)

    for dz, k in x_list:
        if not line or dz != 2:
            x_copy(dz, k).wait_recv()
    perm = (lax.broadcasted_iota(jnp.int32, (T, T), 0) == shuf[...]).astype(BF)

    def perm_body(q, carry):
        cols = pl.ds(pl.multiple_of(q * KC, KC), KC)
        xs[:, cols] = dot_first(perm, xg[:, :, :, cols].reshape(T, KC)).astype(BF)
        return carry

    lax.fori_loop(0, H // KC, perm_body, 0)
    enc_copy.wait()

    def cols_of(k):
        return pl.ds(pl.multiple_of(k * KC, KC), KC)

    def keep_and_send(v, k, own, send):
        top, bot = v[:T2], v[T2:]
        own[k] = jnp.where(c == 0, top, bot)
        send[k] = jnp.where(c == 0, bot, top)

    def p_copy(k):
        return remote(pre_send.at[k], pre_recv.at[k], p_s.at[k], p_r.at[k], row=other_c)

    def f_copy(k):
        return remote(fall.at[c, k], fall.at[c, k], f_s.at[k], f_r.at[k], row=other_c)

    def pre_body(k, carry):
        keep_and_send(dot_last(xs[...], enc_v[cols_of(k), :]), k, pre_own, pre_send)
        p_copy(k).start()
        return carry

    lax.fori_loop(0, nk, pre_body, 0)

    def feat_body(k, carry):
        p_copy(k).wait_recv()
        v = pre_own[k] + pre_recv[k] + bias[:, cols_of(k)]
        fall[c, k] = jnp.maximum(v, 0.0).astype(BF)
        f_copy(k).start()
        return carry

    lax.fori_loop(0, nk, feat_body, 0)

    def join_body(k, carry):
        f_copy(k).wait_recv()
        feats[:, cols_of(k)] = jnp.concatenate([fall[0, k], fall[1, k]], axis=0)
        return carry

    lax.fori_loop(0, nk, join_body, 0)

    up0, up1 = spread_to(0), spread_to(1)

    def expand_body(b, carry):
        rows = pl.ds(pl.multiple_of(b * 2 * DC, 2 * DC), 2 * DC)
        turned = feats[:, pl.ds(pl.multiple_of(b * DC, DC), DC)].T
        fx[rows, :T] = mm(up0, turned).astype(BF)
        fx[rows, T:] = mm(up1, turned).astype(BF)
        return carry

    def n_copy(j):
        return remote(nsend.at[j], nrecv.at[j], n_s.at[j], n_r.at[j], layer=other_x)

    def r_copy(j, dz):
        return remote(osend.at[j, far(dz)], rrecv.at[j, dz - 1], r_s.at[j, dz], r_r.at[j, dz], feat=far(dz))

    def e_copy(j, dz):
        return remote(e0.at[j, z], e0.at[j, z], e_s.at[j, dz], e_r.at[j, dz], feat=far(dz))

    def w_copy(j, to, at):
        return remote(e0.at[j, back(2)], e0.at[j, back(2)], w_s.at[j], e_r.at[j, at], feat=far(to))

    def t_copy(j, dz):
        return remote(e0.at[j, back(dz)], e1.at[j, back(dz)], t_s.at[j, dz], t_r.at[j, dz], layer=other_x)

    def spots(j, q):
        wide = pl.ds(pl.multiple_of(j * NC + q * KC, KC), KC)
        return wide, pl.ds(pl.multiple_of(q * KC, KC), KC)

    @pl.when(x == 0)
    def _():
        for j in range(J):
            def next_body(q, carry):
                wide, near = spots(j, q)
                nsend[j, :, near] = mm(feats[...], wv[1, :, wide]).astype(BF)
                return carry

            lax.fori_loop(0, NC // KC, next_body, 0)
            n_copy(j).start()

            def own_body(q, carry):
                wide, near = spots(j, q)
                v = mm(feats[...], wv[0, :, wide]).reshape(n, CR, KC)
                facc[:, :, wide] = v
                osend[j, :, :, near] = v.astype(BF)
                return carry

            lax.fori_loop(0, NC // KC, own_body, 0)
            for dz in range(1, n):
                r_copy(j, dz).start()

    @pl.when(x == 1)
    def _():
        for j in range(J):
            def own_body(q, carry):
                wide, near = spots(j, q)
                facc[:, :, wide] = mm(feats[...], wv[0, :, wide]).reshape(n, CR, KC)
                return carry

            lax.fori_loop(0, NC // KC, own_body, 0)
        for j in range(J):
            n_copy(j).wait_recv()

            def add_body(q, carry):
                wide, near = spots(j, q)
                v = facc[:, :, wide] + nrecv[j, :, near].astype(jnp.float32).reshape(n, CR, KC)
                facc[:, :, wide] = v
                osend[j, :, :, near] = v.astype(BF)
                return carry

            lax.fori_loop(0, NC // KC, add_body, 0)
            for dz in range(1, n):
                r_copy(j, dz).start()

    lax.fori_loop(0, F // DC, expand_body, 0)
    m_copy.wait_recv()

    def reduce_chunk(j):
        for dz in range(1, n):
            r_copy(j, dz).wait_recv()
        wide = pl.ds(j * NC, NC)
        total = facc[z, :, wide]
        for dz in range(1, n):
            total = total + rrecv[j, dz - 1].astype(jnp.float32)
        d = jnp.where(
            x == 0,
            jnp.where(c == 0, dbias[0:1, j * NC:(j + 1) * NC], dbias[0:1, H + j * NC:H + (j + 1) * NC]),
            jnp.where(c == 0, dbias[1:2, j * NC:(j + 1) * NC], dbias[1:2, H + j * NC:H + (j + 1) * NC]))
        total = total + d
        e0[j, z] = (total - mlpx[:, :, wide].reshape(CR, NC).astype(jnp.float32)).astype(BF)
        for dz in orders:
            unless_ends(dz, lambda: e_copy(j, dz).start())

        @pl.when(x == 1)
        def _():
            t_copy(j, 0).start()

        rc[:, j] = total.astype(BF).reshape(2, R, NC)

    def pass_chunk(j):
        for dz in orders:
            e_copy(j, dz).wait_recv()
            if line and dz == 2:
                relays(lambda to, at: w_copy(j, to, at).start())

            @pl.when(x == 1)
            def _():
                t_copy(j, dz).start()

    for j in range(J):
        reduce_chunk(j)
        if j:
            pass_chunk(j - 1)
    pass_chunk(J - 1)

    def b_copy(k):
        dx, dc = k // 2, k % 2
        to_x = other_x if dx else x
        to_c = other_c if dc else c
        return remote(rc.at[to_c], rb.at[x, c], b_s.at[k], b_r.at[k], layer=to_x, row=to_c)

    for k in range(1, 4):
        b_copy(k).start()
    rb[x, c] = rc[c]

    for j in range(J):
        errs[0, :, j * NC:(j + 1) * NC] = e0[j].reshape(T, NC)

    @pl.when(x == 0)
    def _():
        for j in range(J):
            for dz in range(n):
                t_copy(j, dz).wait_recv()
            errs[1, :, j * NC:(j + 1) * NC] = e1[j].reshape(T, NC)

    @pl.when(x == 1)
    def _():
        errs[1] = jnp.zeros((T, H), BF)

    def g_copy(k):
        return remote(g_send.at[k], g_recv.at[k], g_s.at[k], g_r.at[k], row=other_c)

    def q_copy(k):
        return remote(gall.at[c, k], gall.at[c, k], q_s.at[k], q_r.at[k], row=other_c)

    @pl.when(x == 0)
    def _():
        def grad_body(k, carry):
            v = dot_last(errs[0], wv[0, cols_of(k), :]) + dot_last(errs[1], wv[1, cols_of(k), :])
            keep_and_send(v, k, g_own, g_send)
            g_copy(k).start()
            return carry

        lax.fori_loop(0, nk, grad_body, 0)

    @pl.when(x == 1)
    def _():
        def grad_body(k, carry):
            keep_and_send(dot_last(errs[0], wv[0, cols_of(k), :]), k, g_own, g_send)
            g_copy(k).start()
            return carry

        lax.fori_loop(0, nk, grad_body, 0)

    def mask_body(k, carry):
        g_copy(k).wait_recv()
        v = (g_own[k] + g_recv[k]) * scale
        gall[c, k] = jnp.where(fall[c, k].astype(jnp.float32) > 0, v, 0.0).astype(BF)
        q_copy(k).start()
        return carry

    lax.fori_loop(0, nk, mask_body, 0)

    for k in range(1, 4):
        b_copy(k).wait_recv()
    for h in range(2):
        for j in range(J):
            lo = h * H + j * NC
            parts[:, lo:lo + NC] = rb[:, h, j].reshape(2 * R, NC)

    def last_body(k, carry):
        q_copy(k).wait_recv()
        both = jnp.concatenate([gall[0, k], gall[1, k]], axis=0)
        gpre[:, cols_of(k)] = both
        p_copy(k).wait_send()
        f_copy(k).wait_send()
        g_copy(k).wait_send()
        q_copy(k).wait_send()
        return carry

    lax.fori_loop(0, nk, last_body, 0)

    for dz, k in x_list:
        unless_ends(dz, lambda: x_copy(dz, k).wait_send())
    for k in range(2):
        relays(lambda to, at: y_copy(k, to, at).wait_send())
    for j in range(J):
        relays(lambda to, at: w_copy(j, to, at).wait_send())
    m_copy.wait_send()
    for j in range(J):
        for dz in range(1, n):
            r_copy(j, dz).wait_send()
            unless_ends(dz, lambda: e_copy(j, dz).wait_send())
    for k in range(1, 4):
        b_copy(k).wait_send()

    @pl.when(x == 0)
    def _():
        for j in range(J):
            n_copy(j).wait_send()

    @pl.when(x == 1)
    def _():
        for j in range(J):
            for dz in range(n):
                t_copy(j, dz).wait_send()


def weight_kernel(scale, fx, gpre, errs, xs, parts, enc_grad, dec_grad, bgrad, rebuilt, dbuf, ebuf, dsem, esem):
    T, F = gpre.shape
    H = xs.shape[1]
    R2 = parts.shape[0]
    x = lax.axis_index("layer")
    nb = F // KC

    def d_copy(i, slot):
        rows = pl.ds(pl.multiple_of(i * 2 * KC, 2 * KC), 2 * KC)
        return pltpu.make_async_copy(dbuf.at[slot], dec_grad.reshape(2 * F, H).at[rows], dsem.at[slot])

    def e_copy(i, slot):
        rows = pl.ds(pl.multiple_of(i * KC, KC), KC)
        return pltpu.make_async_copy(ebuf.at[slot], enc_grad.at[rows], esem.at[slot])

    def block(i, carry):
        slot = lax.rem(i, 2)

        @pl.when(i >= 2)
        def _():
            d_copy(i - 2, slot).wait()
            e_copy(i - 2, slot).wait()

        rows = pl.ds(pl.multiple_of(i * 2 * KC, 2 * KC), 2 * KC)

        @pl.when(x == 0)
        def _():
            dbuf[slot] = (scale * mm(fx[rows, :], errs.reshape(2 * T, H)[...])).astype(BF)

        @pl.when(x == 1)
        def _():
            dbuf[slot] = (scale * mm(fx[rows, :T], errs[0])).astype(BF)

        d_copy(i, slot).start()
        cols = pl.ds(pl.multiple_of(i * KC, KC), KC)
        ebuf[slot] = dot_first(gpre[:, cols], xs[...]).astype(BF)
        e_copy(i, slot).start()
        return carry

    lax.fori_loop(0, nb, block, 0)
    bgrad[...] = jnp.sum(gpre[...].astype(jnp.float32), axis=0, keepdims=True)
    i = lax.broadcasted_iota(jnp.int32, (R2, R2), 0)
    j = lax.broadcasted_iota(jnp.int32, (R2, R2), 1)
    inter = (j == (i % 2) * (R2 // 2) + i // 2).astype(BF)
    rebuilt.reshape(R2, 2 * H)[...] = mm(inter, parts[...]).astype(BF)
    for k in range(max(nb - 2, 0), nb):
        d_copy(k, k % 2).wait()
        e_copy(k, k % 2).wait()


def fused(resid_buf, shuffle, mlp_out, enc_weight, dec_weight, enc_bias, dec_bias):
    n = lax.axis_size("feat")
    R = resid_buf.shape[0]
    F, H = enc_weight.shape[1:]
    T = R * n * 2
    T2, CR = T // 2, 2 * R
    J = H // KC
    NC, nk = H // J, F // KC
    f32 = jnp.float32
    vm = pl.BlockSpec(memory_space=pltpu.VMEM)
    hbm = pl.BlockSpec(memory_space=pl.ANY)
    dma = pltpu.SemaphoreType.DMA
    shape = jax.ShapeDtypeStruct
    outs = ((2 * F, 2 * T), (T, H), (2, T, H), (T, F), (2 * R, 2 * H))
    held = sum(2 * a[-1] * (a[0] * a[1] if len(a) == 3 else a[0]) for a in outs)
    fx, xs, errs, gpre, parts = pl.pallas_call(
        functools.partial(step_kernel, n, J),
        out_shape=tuple(pltpu.VMEM(a, BF) for a in outs),
        in_specs=[vm, vm, vm, hbm, hbm, vm, vm],
        out_specs=(vm,) * 5,
        scratch_shapes=[
            pltpu.VMEM((T, F), BF), pltpu.VMEM((F, H), BF), pltpu.VMEM((2, F, H), BF), pltpu.VMEM((2, 2 * DC, H), BF),
            pltpu.VMEM((2, R, H), BF), pltpu.VMEM((n, 2, R, H), BF),
            pltpu.VMEM((2, R, H), BF), pltpu.VMEM((R, H), BF),
            pltpu.VMEM((nk, T2, KC), f32), pltpu.VMEM((nk, T2, KC), f32), pltpu.VMEM((nk, T2, KC), f32),
            pltpu.VMEM((2, nk, T2, KC), BF),
            pltpu.VMEM((J, T, NC), BF), pltpu.VMEM((J, T, NC), BF), pltpu.VMEM((n, CR, H), f32),
            pltpu.VMEM((J, n, CR, NC), BF), pltpu.VMEM((J, n - 1, CR, NC), BF),
            pltpu.VMEM((J, n, CR, NC), BF), pltpu.VMEM((J, n, CR, NC), BF),
            pltpu.VMEM((2, J, R, NC), BF), pltpu.VMEM((2, 2, J, R, NC), BF),
            pltpu.VMEM((nk, T2, KC), f32), pltpu.VMEM((nk, T2, KC), f32), pltpu.VMEM((nk, T2, KC), f32),
            pltpu.VMEM((2, nk, T2, KC), BF),
            dma, dma((2,)), dma((n, 2)), dma((n, 2)), dma, dma, dma((nk,)), dma((nk,)),
            dma((nk,)), dma((nk,)), dma((J,)), dma((J,)), dma((J, n)), dma((J, n)),
            dma((J, n)), dma((J, n)), dma((J, n)), dma((J, n)), dma((4,)), dma((4,)),
            dma((nk,)), dma((nk,)), dma((nk,)), dma((nk,)), dma((2,)), dma((J,)),
        ],
        compiler_params=pltpu.CompilerParams(
            collective_id=0, has_side_effects=True, vmem_limit_bytes=VMEM_LIMIT - held),
    )(resid_buf, shuffle.reshape(1, T), mlp_out, enc_weight[0], dec_weight[0], enc_bias, dec_bias)
    enc_grad, dec_grad, bgrad, rebuilt = pl.pallas_call(
        functools.partial(weight_kernel, float(T) ** (-0.5)),
        out_shape=(
            shape((F, H), BF), shape((F, 2, H), BF), shape((1, F), f32), shape((R, 2, 2 * H), BF)),
        in_specs=[vm] * 5,
        out_specs=(hbm, hbm, vm, vm),
        scratch_shapes=[
            pltpu.VMEM((2, 2 * KC, H), BF), pltpu.VMEM((2, KC, H), BF), dma((2,)), dma((2,))],
        compiler_params=pltpu.CompilerParams(vmem_limit_bytes=VMEM_LIMIT // 2),
    )(fx, gpre, errs, xs, parts)
    return rebuilt, enc_grad[None], dec_grad[None], bgrad


def chosen(resid_buf, shuffle, mlp_out, enc_weight, dec_weight, enc_bias, dec_bias):
    args = (resid_buf, shuffle, mlp_out, enc_weight, dec_weight, enc_bias, dec_bias)
    rows, width = resid_buf.shape[0], enc_weight.shape[2]
    fits = (
        lax.axis_size("layer") == LAYERS == 2 and lax.axis_size("row") == 2
        and 1 < lax.axis_size("feat") <= 4 and rows % 16 == 0
        and width % KC == 0 and enc_weight.shape[1] % KC == 0)
    return fused(*args) if fits else on_device(*args)


def solution(mesh):
    return jax.shard_map(
        chosen,
        mesh=mesh,
        in_specs=(
            P(("groups", "feat", "row"), None, None),
            P("groups"),
            P(("groups", "feat", "row"), None, None),
            P("layer", "feat", "row"),
            P("layer", "feat", None, "row"),
            P("layer", "feat"),
            P(),
        ),
        out_specs=(
            P(("groups", "feat", "row"), None, None),
            P(("groups", "layer"), "feat", "row"),
            P(("groups", "layer"), "feat", None, "row"),
            P(("groups", "layer"), "feat"),
        ),
        check_vma=False,
    )
```

```python
import functools
import math

import jax
import jax.numpy as jnp
from jax import lax
from jax.experimental import pallas as pl
from jax.experimental.pallas import tpu as pltpu
from jax.sharding import PartitionSpec as P

LAYERS = 2


def from_behind(block, axis, distance):
    devices = range(lax.axis_size(axis))
    route = [(i - distance, i) for i in devices if i - distance in devices]
    return lax.ppermute(block, axis, route)


def dot_last(left, right):
    return lax.dot_general(
        left, right, (((1,), (1,)), ((), ())), preferred_element_type=jnp.float32
    )


def dot_first(left, right):
    return lax.dot_general(
        left, right, (((0,), (0,)), ((), ())), preferred_element_type=jnp.float32
    )


def on_device(resid_buf, shuffle, mlp_out, enc_weight, dec_weight, enc_bias, dec_bias):
    feat_count = lax.axis_size("feat")
    row_count = lax.axis_size("row")
    sub_blocks = lax.axis_size("layer") // LAYERS
    layer_pos = lax.axis_index("layer")
    row_pos = lax.axis_index("row")
    source = layer_pos // sub_blocks
    rows_each = resid_buf.shape[0]
    width = dec_bias.shape[1]
    half_width = enc_weight.shape[2]
    local_rows = rows_each * feat_count
    total_rows = local_rows * row_count
    loss_scale = float(total_rows) ** (-0.5)
    own_layer = lax.dynamic_index_in_dim(resid_buf, source, axis=1, keepdims=False)
    buffer_all = lax.all_gather(own_layer, ("feat", "row"), axis=0, tiled=True)
    batch_rows = jnp.take(buffer_all, shuffle, axis=0)
    blocks = batch_rows.reshape(feat_count, row_count, rows_each, width)
    inputs_half = lax.dynamic_slice_in_dim(
        jnp.swapaxes(blocks, 0, 1), row_pos * half_width, half_width, axis=3
    )
    inputs_half = inputs_half.reshape(total_rows, half_width)
    own_half_dec = dec_weight[0][:, 0]
    next_half_dec = dec_weight[0][:, 1]
    pre_all = lax.psum(dot_last(inputs_half, enc_weight[0]), "row") + enc_bias[0]
    features_all = jnp.maximum(pre_all, 0.0).astype(jnp.bfloat16)
    own_part = jnp.dot(features_all, own_half_dec, preferred_element_type=jnp.float32)
    next_part = jnp.dot(features_all, next_half_dec, preferred_element_type=jnp.float32)
    carried = from_behind(next_part, "layer", sub_blocks)
    spread = (own_part + carried).reshape(row_count, local_rows, half_width)
    halves = lax.psum_scatter(spread, "feat", scatter_dimension=1, tiled=True)
    joined = lax.all_to_all(halves, "row", split_axis=0, concat_axis=2, tiled=True)
    section_sum = joined.reshape(rows_each, width)
    target_ids = jnp.arange(LAYERS, dtype=jnp.int32)
    target_slots = jnp.where((target_ids == source)[:, None, None], section_sum[None], 0.0)
    totals = lax.psum(target_slots, "layer")
    recon_sum = jnp.swapaxes(totals, 0, 1) + dec_bias[None]
    errors = (recon_sum - mlp_out.astype(jnp.float32)).astype(jnp.bfloat16)
    gathered = lax.all_gather(errors, ("feat", "row"), axis=0, tiled=True)
    error_grid = gathered.reshape(feat_count, row_count, rows_each, LAYERS, width)
    errors_mine = lax.dynamic_index_in_dim(error_grid, row_pos, axis=1, keepdims=False)
    errors_mine = errors_mine.reshape(local_rows, LAYERS, width)
    errors_half = lax.dynamic_slice_in_dim(
        jnp.swapaxes(error_grid, 0, 1), row_pos * half_width, half_width, axis=4
    )
    errors_half = errors_half.reshape(total_rows, LAYERS, half_width)
    live_next = source + 1 < LAYERS
    next_index = jnp.minimum(source + 1, LAYERS - 1)
    half_own = lax.dynamic_index_in_dim(errors_half, source, axis=1, keepdims=False)
    half_next = lax.dynamic_index_in_dim(errors_half, next_index, axis=1, keepdims=False)
    half_next = jnp.where(live_next, half_next, jnp.zeros_like(half_next))
    half_terms = dot_last(half_own, own_half_dec) + dot_last(half_next, next_half_dec)
    grad_feats = lax.psum(half_terms, "row") * loss_scale
    grad_all = jnp.where(pre_all > 0, grad_feats, 0.0).astype(jnp.bfloat16)
    grad_own = loss_scale * dot_first(features_all, half_own)
    grad_next = loss_scale * dot_first(features_all, half_next)
    enc_grad = dot_first(grad_all, inputs_half).astype(jnp.bfloat16)
    dec_grad = jnp.stack([grad_own, grad_next], axis=1).astype(jnp.bfloat16)
    bias_grad = jnp.sum(grad_all.astype(jnp.float32), axis=0)
    return (recon_sum.astype(jnp.bfloat16), enc_grad[None], dec_grad[None], bias_grad[None])

KC = 256
DC = 128
MESH = pl.DeviceIdType.MESH
VMEM_LIMIT = 67043328
BF = jnp.bfloat16


def pick(rows, cols, stride, offset):
    r = lax.broadcasted_iota(jnp.int32, (rows, cols), 0)
    c = lax.broadcasted_iota(jnp.int32, (rows, cols), 1)
    return (c == stride * r + offset).astype(BF)


def spread_to(offset):
    r = lax.broadcasted_iota(jnp.int32, (2 * DC, DC), 0)
    c = lax.broadcasted_iota(jnp.int32, (2 * DC, DC), 1)
    return (r == 2 * c + offset).astype(BF)


def mm(left, right):
    return jnp.dot(left, right, preferred_element_type=jnp.float32)


def halves_of(width):
    return next(q for q in (3, 2, 1) if width % (q * DC) == 0)


def step_kernel(
    n, J, res, shuf, mlp, enc, dec, bias, dbias,
    fx, xs, e, gpre, parts,
    enc_v, wv, raw, xsend, xg, mlpx, msend, dsel, pre, pre_recv, feats,
    nsend, nrecv, facc, osend, rr, rl, rc, rb, gacc, g_recv,
    sem_l, sem_raw, x_s, x_r, y_s, m_s, m_r, p_s, p_r, f_s, f_r, n_s, n_r,
    rs_s, rs_r, a_s, a_r, t_s, t_r, b_s, b_r, g_s, g_r, q_s, q_r,
):
    z = lax.axis_index("feat")
    x = lax.axis_index("layer")
    c = lax.axis_index("row")
    Q, R, HX = xsend.shape[1:]
    F, H = enc_v.shape
    T = xs.shape[0]
    T2, CR, NC = T // 2, 2 * R, H // J
    nk, slots = F // KC, raw.shape[0]
    scale = float(T) ** (-0.5)
    other_c, other_x = 1 - c, 1 - x

    def far(dz):
        return lax.rem(z + dz, n)

    def back(dz):
        return lax.rem(z + n - dz, n)

    def remote(src, dst, send, recv, **where):
        return pltpu.make_async_remote_copy(
            src_ref=src, dst_ref=dst, send_sem=send, recv_sem=recv,
            device_id=where, device_id_type=MESH)

    def unless_ends(dz, act):
        if dz == n - 1:
            pl.when(z != 0)(act)
        elif dz == 1:
            pl.when(z != n - 1)(act)
        else:
            act()

    def relays(act):
        pl.when(z == 2)(lambda: act(1, 3))
        pl.when(z == 1)(lambda: act(3, 1))

    def raw_copy(i, slot):
        return pltpu.make_async_copy(
            dec.reshape(2 * F, H).at[pl.ds(pl.multiple_of(i * 2 * DC, 2 * DC), 2 * DC)], raw.at[slot], sem_raw.at[slot])

    nd = F // DC
    for i in range(slots - 1):
        raw_copy(i, i).start()
    enc_copy = pltpu.make_async_copy(enc, enc_v, sem_l)
    enc_copy.start()

    barrier = pltpu.get_barrier_semaphore()
    for dz in range(n):
        if dz:
            pl.semaphore_signal(barrier, inc=1, device_id={"feat": far(dz), "row": c}, device_id_type=MESH)
        pl.semaphore_signal(barrier, inc=1, device_id={"feat": far(dz), "row": other_c}, device_id_type=MESH)
    for cc in (c, other_c):
        pl.semaphore_signal(barrier, inc=1, device_id={"layer": other_x, "row": cc}, device_id_type=MESH)

    own_x = mm(pick(R, 2 * R, 2, x), res.reshape(2 * R, 2 * H)[...]).astype(BF)
    x_mine = jnp.where(c == 0, own_x[:, :H], own_x[:, H:])
    x_other = jnp.where(c == 0, own_x[:, H:], own_x[:, :H])
    for q in range(Q):
        xsend[0, q] = x_mine[:, q * HX:(q + 1) * HX]
        xsend[1, q] = x_other[:, q * HX:(q + 1) * HX]
        xg[z, c, q] = x_mine[:, q * HX:(q + 1) * HX]
    own_m = mm(pick(R, 2 * R, 2, x), mlp.reshape(2 * R, 2 * H)[...]).astype(BF)
    mlpx[c] = jnp.where(c == 0, own_m[:, :H], own_m[:, H:])
    msend[...] = jnp.where(c == 0, own_m[:, H:], own_m[:, :H])

    pl.semaphore_wait(barrier, 2 * n + 1)

    def x_copy(dz, k, q):
        return remote(xsend.at[k, q], xg.at[z, c, q], x_s.at[dz, k, q], x_r.at[dz, k, q],
                      feat=far(dz), row=c if k == 0 else other_c)

    x_list = [(dz, k) for dz in (2, 1, 3) for k in range(2)] + [(0, 1)]
    for q in range(Q):
        for dz, k in x_list:
            unless_ends(dz, lambda: x_copy(dz, k, q).start())

    def y_copy(k, q, to, at):
        cc = c if k == 0 else other_c
        return remote(xg.at[back(2), cc, q], xg.at[back(2), cc, q], y_s.at[k, q], x_r.at[at, k, q], feat=far(to))

    m_copy = remote(msend, mlpx.at[c], m_s, m_r, row=other_c)
    m_copy.start()
    d_all = jnp.where(x == 0, dbias[0:1, :], dbias[1:2, :])
    dsel[...] = jnp.where(c == 0, d_all[:, :H], d_all[:, H:])

    apart = jnp.concatenate([pick(DC, 2 * DC, 2, 0), pick(DC, 2 * DC, 2, 1)], axis=0)

    def split_body(i, carry):
        slot = lax.rem(i, slots)

        @pl.when(i + slots - 1 < nd)
        def _():
            raw_copy(i + slots - 1, lax.rem(i + slots - 1, slots)).start()

        raw_copy(i, slot).wait()
        both = mm(apart, raw[slot]).astype(BF)
        rows = pl.ds(pl.multiple_of(i * DC, DC), DC)
        wv[0, rows, :] = both[:DC]
        wv[1, rows, :] = both[DC:]
        return carry

    def pass_on(q):
        for k in range(2):
            x_copy(2, k, q).wait_recv()
            relays(lambda to, at: y_copy(k, q, to, at).start())

    perm = (lax.broadcasted_iota(jnp.int32, (T, T), 0) == shuf[...]).astype(BF)

    def p_copy(k):
        return remote(pre.at[k, pl.ds(pl.multiple_of(other_c * T2, T2), T2)], pre_recv.at[k], p_s.at[k], p_r.at[k], row=other_c)

    mine = pl.ds(pl.multiple_of(c * T2, T2), T2)

    def f_copy(k):
        return remote(feats.at[k, mine], feats.at[k, mine], f_s.at[k], f_r.at[k], row=other_c)

    lax.fori_loop(0, nd // 2, split_body, 0)
    pass_on(0)
    lax.fori_loop(nd // 2, nd, split_body, 0)
    enc_copy.wait()
    per = 2 if nk % 2 == 0 else 1
    for q in range(Q):
        if q:
            pass_on(q)
        for dz, k in x_list:
            if dz != 2:
                x_copy(dz, k, q).wait_recv()
        lo = q * HX
        xs[:, lo:lo + HX] = dot_first(perm, xg[:, :, q].reshape(T, HX)).astype(BF)

        def pre_body(i, carry):
            rows = pl.ds(pl.multiple_of(i * per * KC, KC), per * KC)
            v = dot_last(xs[:, lo:lo + HX], enc_v[rows, lo:lo + HX])
            for h in range(per):
                part = v[:, h * KC:(h + 1) * KC]
                k = i * per + h
                pre[k] = part if q == 0 else pre[k] + part
                if q == Q - 1:
                    p_copy(k).start()
            return carry

        lax.fori_loop(0, nk // per, pre_body, 0)

    def feat_body(k, carry):
        p_copy(k).wait_recv()
        cols = pl.ds(pl.multiple_of(k * KC, KC), KC)
        v = pre[k, mine, :] + pre_recv[k] + bias[:, cols]
        feats[k, mine, :] = jnp.maximum(v, 0.0).astype(BF)
        f_copy(k).start()
        return carry

    lax.fori_loop(0, nk, feat_body, 0)

    def zero_body(k, carry):
        gacc[k] = jnp.zeros((T, KC), jnp.float32)
        f_copy(k).wait_recv()
        return carry

    lax.fori_loop(0, nk, zero_body, 0)
    m_copy.wait_recv()
    up0, up1 = spread_to(0), spread_to(1)

    def expand(b):
        rows = pl.ds(pl.multiple_of(b * 2 * DC, 2 * DC), 2 * DC)
        turned = feats[b // (KC // DC), :, pl.ds(pl.multiple_of(lax.rem(b, KC // DC) * DC, DC), DC)].T
        fx[rows, :T] = mm(up0, turned).astype(BF)
        fx[rows, T:] = mm(up1, turned).astype(BF)

    def n_copy(j):
        return remote(nsend.at[j], nrecv.at[j], n_s.at[j], n_r.at[j], layer=other_x)

    def right_copy(j, k):
        some = pl.ds(k + 1, n - 1 - k)
        return remote(osend.at[j, some], rr.at[j, some], rs_s.at[j, 0], rs_r.at[j, 0], feat=k + 1)

    def left_copy(j, k):
        some = pl.ds(0, k)
        return remote(osend.at[j, some], rl.at[j, some], rs_s.at[j, 1], rs_r.at[j, 1], feat=k - 1)

    def wide(j):
        return pl.ds(pl.multiple_of(j * NC, NC), NC)

    def all_feats():
        return jnp.concatenate([feats[k] for k in range(nk)], axis=1)

    def front(j):
        @pl.when(x == 0)
        def _():
            nsend[j] = mm(all_feats(), wv[1, :, wide(j)]).astype(BF)
            n_copy(j).start()

        facc[j] = mm(all_feats(), wv[0, :, wide(j)]).reshape(n, CR, NC)

        @pl.when(x == 1)
        def _():
            n_copy(j).wait_recv()
            facc[j] = facc[j] + nrecv[j].astype(jnp.float32).reshape(n, CR, NC)

        @pl.when(z == 0)
        def _():
            osend[j, 1:] = facc[j, 1:].astype(BF)
            right_copy(j, 0).start()

        @pl.when(z == n - 1)
        def _():
            osend[j, :n - 1] = facc[j, :n - 1].astype(BF)
            left_copy(j, n - 1).start()

    def go_right(j, k):
        right_copy(j, k - 1).wait_recv()
        osend[j, k + 1:] = (facc[j, k + 1:] + rr[j, k + 1:].astype(jnp.float32)).astype(BF)
        right_copy(j, k).start()

    def go_left(j, k):
        left_copy(j, k + 1).wait_recv()
        osend[j, :k] = (facc[j, :k] + rl[j, :k].astype(jnp.float32)).astype(BF)
        left_copy(j, k).start()

    def relay_near(j):
        pl.when(z == 1)(lambda: go_right(j, 1))
        pl.when(z == 2)(lambda: go_left(j, 2))

    def relay_far(j):
        pl.when(z == 2)(lambda: go_right(j, 2))
        pl.when(z == 1)(lambda: go_left(j, 1))

    def a_copy(j, b, way):
        to = jnp.minimum(z + 1, n - 1) if way == 0 else jnp.maximum(z - 1, 0)
        return remote(e.at[j, 0, b], e.at[j, 0, b], a_s.at[j, way, b], a_r.at[j, b], feat=to)

    def t_copy(j, b):
        return remote(e.at[j, 0, b], e.at[j, 1, b], t_s.at[j, b], t_r.at[j, b], layer=other_x)

    def final(j):
        @pl.when(z == 0)
        def _():
            left_copy(j, 1).wait_recv()

        @pl.when(z == n - 1)
        def _():
            right_copy(j, n - 2).wait_recv()

        @pl.when(z > 0)
        def _():
            facc[j, z] = facc[j, z] + rr[j, z].astype(jnp.float32)

        @pl.when(z < n - 1)
        def _():
            facc[j, z] = facc[j, z] + rl[j, z].astype(jnp.float32)

        total = facc[j, z] + dsel[:, wide(j)]
        e[j, 0, z] = (total - mlpx[:, :, wide(j)].reshape(CR, NC).astype(jnp.float32)).astype(BF)
        pl.when(z < n - 1)(lambda: a_copy(j, z, 0).start())
        pl.when(z > 0)(lambda: a_copy(j, z, 1).start())
        pl.when(x == 1)(lambda: t_copy(j, z).start())
        kept = total.astype(BF).reshape(2, R, NC)
        rc[0, j] = kept[0]
        rc[1, j] = kept[1]

    def hop(j, h):
        @pl.when(z >= h)
        def _():
            a_copy(j, z - h, 0).wait_recv()
            pl.when(z < n - 1)(lambda: a_copy(j, z - h, 0).start())
            pl.when(x == 1)(lambda: t_copy(j, z - h).start())

        @pl.when(z + h < n)
        def _():
            a_copy(j, z + h, 1).wait_recv()
            pl.when(z > 0)(lambda: a_copy(j, z + h, 1).start())
            pl.when(x == 1)(lambda: t_copy(j, z + h).start())

    def g_copy(k):
        return remote(gacc.at[k, pl.ds(pl.multiple_of(other_c * T2, T2), T2)], g_recv.at[k], g_s.at[k], g_r.at[k], row=other_c)

    def grads(j):
        last = j == J - 1

        @pl.when(x == 0)
        def _():
            for b in range(n):
                t_copy(j, b).wait_recv()

            def body(k, carry):
                rows = pl.ds(pl.multiple_of(k * KC, KC), KC)
                gacc[k] = (gacc[k] + dot_last(e[j, 0].reshape(T, NC), wv[0, rows, wide(j)])
                           + dot_last(e[j, 1].reshape(T, NC), wv[1, rows, wide(j)]))
                pl.when(last)(lambda: g_copy(k).start())
                return carry

            lax.fori_loop(0, nk, body, 0)

        @pl.when(x == 1)
        def _():
            def body(k, carry):
                rows = pl.ds(pl.multiple_of(k * KC, KC), KC)
                gacc[k] = gacc[k] + dot_last(e[j, 0].reshape(T, NC), wv[0, rows, wide(j)])
                pl.when(last)(lambda: g_copy(k).start())
                return carry

            lax.fori_loop(0, nk, body, 0)

    def early_b(j):
        pl.when(j == JB - 1)(lambda: [b_copy(k, 0).start() for k in range(1, 4)] and None)

    JB = min(3, J - 1)

    def b_copy(k, late):
        dx, dc = k // 2, k % 2
        to_x = other_x if dx else x
        to_c = other_c if dc else c
        some = pl.ds(JB, J - JB) if late else pl.ds(0, JB)
        return remote(rc.at[to_c, some], rb.at[x, c, some], b_s.at[k, late], b_r.at[k, late], layer=to_x, row=to_c)

    stages = ((0, front), (1, relay_near), (2, relay_far), (3, final), (3, early_b),
              (4, lambda j: hop(j, 1)), (5, lambda j: hop(j, 2)), (6, lambda j: hop(j, 3)), (7, grads))
    steps = J + stages[-1][0]
    share = pl.cdiv(nd, steps)

    def pipe(s, carry):
        for lag, act in stages:
            pl.when(jnp.logical_and(s >= lag, s < J + lag))(functools.partial(act, s - lag))
        for i in range(share):
            pl.when(s * share + i < nd)(functools.partial(expand, s * share + i))
        return carry

    lax.fori_loop(0, steps, pipe, 0)
    for k in range(1, 4):
        b_copy(k, 1).start()

    def q_copy(k):
        return remote(gpre.at[k, mine], gpre.at[k, mine], q_s.at[k], q_r.at[k], row=other_c)

    def mask_body(k, carry):
        g_copy(k).wait_recv()
        v = (gacc[k, mine, :] + g_recv[k]) * scale
        gpre[k, mine, :] = jnp.where(feats[k, mine, :].astype(jnp.float32) > 0, v, 0.0).astype(BF)
        q_copy(k).start()
        return carry

    lax.fori_loop(0, nk, mask_body, 0)
    rb[x, c] = rc[c]

    def sent_body(k, carry):
        p_copy(k).wait_send()
        f_copy(k).wait_send()
        return carry

    lax.fori_loop(0, nk, sent_body, 0)
    for q in range(Q):
        for dz, k in x_list:
            unless_ends(dz, lambda: x_copy(dz, k, q).wait_send())
        for k in range(2):
            relays(lambda to, at: y_copy(k, q, to, at).wait_send())
    m_copy.wait_send()

    def sent_chunk(j, carry):
        for k in range(n):
            @pl.when(z == k)
            def _():
                if k < n - 1:
                    right_copy(j, k).wait_send()
                if k > 0:
                    left_copy(j, k).wait_send()

        for b in range(n):
            pl.when(jnp.logical_and(z >= b, z < n - 1))(lambda: a_copy(j, b, 0).wait_send())
            pl.when(jnp.logical_and(z <= b, z > 0))(lambda: a_copy(j, b, 1).wait_send())

        @pl.when(x == 0)
        def _():
            n_copy(j).wait_send()

        @pl.when(x == 1)
        def _():
            for b in range(n):
                t_copy(j, b).wait_send()

        return carry

    lax.fori_loop(0, J, sent_chunk, 0)
    for k in range(1, 4):
        for late in range(2):
            b_copy(k, late).wait_recv()
    for h in range(2):
        for j in range(J):
            lo = h * H + j * NC
            parts[:, lo:lo + NC] = rb[:, h, j].reshape(2 * R, NC)

    def last_body(k, carry):
        q_copy(k).wait_recv()
        g_copy(k).wait_send()
        q_copy(k).wait_send()
        return carry

    lax.fori_loop(0, nk, last_body, 0)
    for k in range(1, 4):
        for late in range(2):
            b_copy(k, late).wait_send()


def weight_kernel(scale, fx, gpre, e, xs, parts, enc_grad, dec_grad, bgrad, rebuilt, dbuf, ebuf, dsem, esem):
    nb, T, _ = gpre.shape
    H = xs.shape[1]
    J, NC = e.shape[0], e.shape[-1]
    R2 = parts.shape[0]
    x = lax.axis_index("layer")

    def d_copy(i, slot):
        rows = pl.ds(pl.multiple_of(i * 2 * KC, 2 * KC), 2 * KC)
        return pltpu.make_async_copy(dbuf.at[slot], dec_grad.reshape(2 * nb * KC, H).at[rows], dsem.at[slot])

    def e_copy(i, slot):
        rows = pl.ds(pl.multiple_of(i * KC, KC), KC)
        return pltpu.make_async_copy(ebuf.at[slot], enc_grad.at[rows], esem.at[slot])

    def block(i, carry):
        slot = lax.rem(i, 2)

        @pl.when(i >= 2)
        def _():
            d_copy(i - 2, slot).wait()
            e_copy(i - 2, slot).wait()

        rows = pl.ds(pl.multiple_of(i * 2 * KC, 2 * KC), 2 * KC)

        @pl.when(x == 0)
        def _():
            for j in range(J):
                dbuf[slot, :, j * NC:(j + 1) * NC] = (scale * mm(fx[rows, :], e[j].reshape(2 * T, NC))).astype(BF)

        @pl.when(x == 1)
        def _():
            for j in range(J):
                dbuf[slot, :, j * NC:(j + 1) * NC] = (scale * mm(fx[rows, :T], e[j, 0].reshape(T, NC))).astype(BF)

        d_copy(i, slot).start()
        ebuf[slot] = dot_first(gpre[i], xs[...]).astype(BF)
        e_copy(i, slot).start()
        bgrad[:, pl.ds(pl.multiple_of(i * KC, KC), KC)] = jnp.sum(gpre[i].astype(jnp.float32), axis=0, keepdims=True)
        return carry

    lax.fori_loop(0, nb, block, 0)
    i = lax.broadcasted_iota(jnp.int32, (R2, R2), 0)
    j = lax.broadcasted_iota(jnp.int32, (R2, R2), 1)
    inter = (j == (i % 2) * (R2 // 2) + i // 2).astype(BF)
    rebuilt.reshape(R2, 2 * H)[...] = mm(inter, parts[...]).astype(BF)
    for k in range(max(nb - 2, 0), nb):
        d_copy(k, k % 2).wait()
        e_copy(k, k % 2).wait()


def fused(resid_buf, shuffle, mlp_out, enc_weight, dec_weight, enc_bias, dec_bias):
    n = lax.axis_size("feat")
    R = resid_buf.shape[0]
    F, H = enc_weight.shape[1:]
    T = R * n * 2
    T2, CR = T // 2, 2 * R
    J = H // KC
    NC, nk = H // J, F // KC
    Q = halves_of(H)
    HX = H // Q
    f32 = jnp.float32
    vm = pl.BlockSpec(memory_space=pltpu.VMEM)
    hbm = pl.BlockSpec(memory_space=pl.ANY)
    dma = pltpu.SemaphoreType.DMA
    vmem = pltpu.VMEM
    shape = jax.ShapeDtypeStruct
    outs = ((2 * F, 2 * T), (T, H), (J, 2, n, CR, NC), (nk, T, KC), (2 * R, 2 * H))
    held = sum(2 * math.prod(a) for a in outs)
    fx, xs, e, gpre, parts = pl.pallas_call(
        functools.partial(step_kernel, n, J),
        out_shape=tuple(vmem(a, BF) for a in outs),
        in_specs=[vm, vm, vm, hbm, hbm, vm, vm],
        out_specs=(vm,) * 5,
        scratch_shapes=[
            vmem((F, H), BF), vmem((2, F, H), BF), vmem((4, 2 * DC, H), BF),
            vmem((2, Q, R, HX), BF), vmem((n, 2, Q, R, HX), BF),
            vmem((2, R, H), BF), vmem((R, H), BF), vmem((1, H), f32),
            vmem((nk, T, KC), f32), vmem((nk, T2, KC), f32), vmem((nk, T, KC), BF),
            vmem((J, T, NC), BF), vmem((J, T, NC), BF), vmem((J, n, CR, NC), f32),
            vmem((J, n, CR, NC), BF), vmem((J, n, CR, NC), BF), vmem((J, n, CR, NC), BF),
            vmem((2, J, R, NC), BF), vmem((2, 2, J, R, NC), BF),
            vmem((nk, T, KC), f32), vmem((nk, T2, KC), f32),
            dma, dma((4,)), dma((n, 2, Q)), dma((n, 2, Q)), dma((2, Q)), dma, dma,
            dma((nk,)), dma((nk,)), dma((nk,)), dma((nk,)), dma((J,)), dma((J,)),
            dma((J, 2)), dma((J, 2)), dma((J, 2, n)), dma((J, n)), dma((J, n)), dma((J, n)),
            dma((4, 2)), dma((4, 2)), dma((nk,)), dma((nk,)), dma((nk,)), dma((nk,)),
        ],
        compiler_params=pltpu.CompilerParams(
            collective_id=0, has_side_effects=True, vmem_limit_bytes=VMEM_LIMIT - held),
    )(resid_buf, shuffle.reshape(1, T), mlp_out, enc_weight[0], dec_weight[0], enc_bias, dec_bias)
    enc_grad, dec_grad, bgrad, rebuilt = pl.pallas_call(
        functools.partial(weight_kernel, float(T) ** (-0.5)),
        out_shape=(
            shape((F, H), BF), shape((F, 2, H), BF), shape((1, F), f32), shape((R, 2, 2 * H), BF)),
        in_specs=[vm] * 5,
        out_specs=(hbm, hbm, vm, vm),
        scratch_shapes=[
            vmem((2, 2 * KC, H), BF), vmem((2, KC, H), BF), dma((2,)), dma((2,))],
        compiler_params=pltpu.CompilerParams(vmem_limit_bytes=VMEM_LIMIT // 2),
    )(fx, gpre, e, xs, parts)
    return rebuilt, enc_grad[None], dec_grad[None], bgrad


def chosen(resid_buf, shuffle, mlp_out, enc_weight, dec_weight, enc_bias, dec_bias):
    args = (resid_buf, shuffle, mlp_out, enc_weight, dec_weight, enc_bias, dec_bias)
    rows, width = resid_buf.shape[0], enc_weight.shape[2]
    fits = (
        lax.axis_size("layer") == LAYERS == 2 and lax.axis_size("row") == 2
        and lax.axis_size("feat") == 4 and rows % 16 == 0
        and width % KC == 0 and enc_weight.shape[1] % KC == 0)
    return fused(*args) if fits else on_device(*args)


def solution(mesh):
    return jax.shard_map(
        chosen,
        mesh=mesh,
        in_specs=(
            P(("groups", "feat", "row"), None, None),
            P("groups"),
            P(("groups", "feat", "row"), None, None),
            P("layer", "feat", "row"),
            P("layer", "feat", None, "row"),
            P("layer", "feat"),
            P(),
        ),
        out_specs=(
            P(("groups", "feat", "row"), None, None),
            P(("groups", "layer"), "feat", "row"),
            P(("groups", "layer"), "feat", None, "row"),
            P(("groups", "layer"), "feat"),
        ),
        check_vma=False,
    )
```

```python
import functools
import math

import jax
import jax.numpy as jnp
from jax import lax
from jax.experimental import pallas as pl
from jax.experimental.pallas import tpu as pltpu
from jax.sharding import PartitionSpec as P

LAYERS = 2


def from_behind(block, axis, distance):
    devices = range(lax.axis_size(axis))
    route = [(i - distance, i) for i in devices if i - distance in devices]
    return lax.ppermute(block, axis, route)


def dot_last(left, right):
    return lax.dot_general(
        left, right, (((1,), (1,)), ((), ())), preferred_element_type=jnp.float32
    )


def dot_first(left, right):
    return lax.dot_general(
        left, right, (((0,), (0,)), ((), ())), preferred_element_type=jnp.float32
    )


def on_device(resid_buf, shuffle, mlp_out, enc_weight, dec_weight, enc_bias, dec_bias):
    feat_count = lax.axis_size("feat")
    row_count = lax.axis_size("row")
    sub_blocks = lax.axis_size("layer") // LAYERS
    layer_pos = lax.axis_index("layer")
    row_pos = lax.axis_index("row")
    source = layer_pos // sub_blocks
    rows_each = resid_buf.shape[0]
    width = dec_bias.shape[1]
    half_width = enc_weight.shape[2]
    local_rows = rows_each * feat_count
    total_rows = local_rows * row_count
    loss_scale = float(total_rows) ** (-0.5)
    own_layer = lax.dynamic_index_in_dim(resid_buf, source, axis=1, keepdims=False)
    buffer_all = lax.all_gather(own_layer, ("feat", "row"), axis=0, tiled=True)
    batch_rows = jnp.take(buffer_all, shuffle, axis=0)
    blocks = batch_rows.reshape(feat_count, row_count, rows_each, width)
    inputs_half = lax.dynamic_slice_in_dim(
        jnp.swapaxes(blocks, 0, 1), row_pos * half_width, half_width, axis=3
    )
    inputs_half = inputs_half.reshape(total_rows, half_width)
    own_half_dec = dec_weight[0][:, 0]
    next_half_dec = dec_weight[0][:, 1]
    pre_all = lax.psum(dot_last(inputs_half, enc_weight[0]), "row") + enc_bias[0]
    features_all = jnp.maximum(pre_all, 0.0).astype(jnp.bfloat16)
    own_part = jnp.dot(features_all, own_half_dec, preferred_element_type=jnp.float32)
    next_part = jnp.dot(features_all, next_half_dec, preferred_element_type=jnp.float32)
    carried = from_behind(next_part, "layer", sub_blocks)
    spread = (own_part + carried).reshape(row_count, local_rows, half_width)
    halves = lax.psum_scatter(spread, "feat", scatter_dimension=1, tiled=True)
    joined = lax.all_to_all(halves, "row", split_axis=0, concat_axis=2, tiled=True)
    section_sum = joined.reshape(rows_each, width)
    target_ids = jnp.arange(LAYERS, dtype=jnp.int32)
    target_slots = jnp.where((target_ids == source)[:, None, None], section_sum[None], 0.0)
    totals = lax.psum(target_slots, "layer")
    recon_sum = jnp.swapaxes(totals, 0, 1) + dec_bias[None]
    errors = (recon_sum - mlp_out.astype(jnp.float32)).astype(jnp.bfloat16)
    gathered = lax.all_gather(errors, ("feat", "row"), axis=0, tiled=True)
    error_grid = gathered.reshape(feat_count, row_count, rows_each, LAYERS, width)
    errors_mine = lax.dynamic_index_in_dim(error_grid, row_pos, axis=1, keepdims=False)
    errors_mine = errors_mine.reshape(local_rows, LAYERS, width)
    errors_half = lax.dynamic_slice_in_dim(
        jnp.swapaxes(error_grid, 0, 1), row_pos * half_width, half_width, axis=4
    )
    errors_half = errors_half.reshape(total_rows, LAYERS, half_width)
    live_next = source + 1 < LAYERS
    next_index = jnp.minimum(source + 1, LAYERS - 1)
    half_own = lax.dynamic_index_in_dim(errors_half, source, axis=1, keepdims=False)
    half_next = lax.dynamic_index_in_dim(errors_half, next_index, axis=1, keepdims=False)
    half_next = jnp.where(live_next, half_next, jnp.zeros_like(half_next))
    half_terms = dot_last(half_own, own_half_dec) + dot_last(half_next, next_half_dec)
    grad_feats = lax.psum(half_terms, "row") * loss_scale
    grad_all = jnp.where(pre_all > 0, grad_feats, 0.0).astype(jnp.bfloat16)
    grad_own = loss_scale * dot_first(features_all, half_own)
    grad_next = loss_scale * dot_first(features_all, half_next)
    enc_grad = dot_first(grad_all, inputs_half).astype(jnp.bfloat16)
    dec_grad = jnp.stack([grad_own, grad_next], axis=1).astype(jnp.bfloat16)
    bias_grad = jnp.sum(grad_all.astype(jnp.float32), axis=0)
    return (recon_sum.astype(jnp.bfloat16), enc_grad[None], dec_grad[None], bias_grad[None])

KC = 256
DC = 128
GC = 1024
LAG0 = 9
MESH = pl.DeviceIdType.MESH
VMEM_LIMIT = 67043328
BF = jnp.bfloat16


def pick(rows, cols, stride, offset):
    r = lax.broadcasted_iota(jnp.int32, (rows, cols), 0)
    c = lax.broadcasted_iota(jnp.int32, (rows, cols), 1)
    return (c == stride * r + offset).astype(BF)


def spread_to(offset):
    r = lax.broadcasted_iota(jnp.int32, (2 * DC, DC), 0)
    c = lax.broadcasted_iota(jnp.int32, (2 * DC, DC), 1)
    return (r == 2 * c + offset).astype(BF)


def mm(left, right):
    return jnp.dot(left, right, preferred_element_type=jnp.float32)


def halves_of(width):
    return next(q for q in (3, 2, 1) if width % (q * DC) == 0)


def step_kernel(
    n, J, res, shuf, mlp, enc, dec, bias, dbias,
    dg, xs, gt, parts,
    fx, e, enc_v, raw, xsend, xg, mlpx, msend, dsel, pre, pre_recv, feats,
    nsend, nrecv, facc, osend, rr, rl, rc, rb, gacc, g_recv,
    sem_l, sem_raw, x_s, x_r, y_s, m_s, m_r, p_s, p_r, f_s, f_r, n_s, n_r,
    rs_s, rs_r, a_s, a_r, t_s, t_r, b_s, b_r, g_s, g_r, q_s, q_r,
):
    z = lax.axis_index("feat")
    x = lax.axis_index("layer")
    c = lax.axis_index("row")
    Q, R, HX = xsend.shape[1:]
    F, H = enc_v.shape
    T = xs.shape[0]
    T2, CR, NC = T // 2, 2 * R, H // J
    nk, slots = F // KC, raw.shape[0]
    scale = float(T) ** (-0.5)
    other_c, other_x = 1 - c, 1 - x

    def far(dz):
        return lax.rem(z + dz, n)

    def back(dz):
        return lax.rem(z + n - dz, n)

    def remote(src, dst, send, recv, **where):
        return pltpu.make_async_remote_copy(
            src_ref=src, dst_ref=dst, send_sem=send, recv_sem=recv,
            device_id=where, device_id_type=MESH)

    def unless_ends(dz, act):
        if dz == n - 1:
            pl.when(z != 0)(act)
        elif dz == 1:
            pl.when(z != n - 1)(act)
        else:
            act()

    def relays(act):
        pl.when(z == 2)(lambda: act(1, 3))
        pl.when(z == 1)(lambda: act(3, 1))

    def raw_copy(i, slot):
        return pltpu.make_async_copy(
            dec.reshape(2 * F, H).at[pl.ds(pl.multiple_of(i * 2 * DC, 2 * DC), 2 * DC)], raw.at[slot], sem_raw.at[slot])

    nd = F // DC
    for i in range(slots - 1):
        raw_copy(i, i).start()
    enc_copy = pltpu.make_async_copy(enc, enc_v, sem_l)
    enc_copy.start()

    barrier = pltpu.get_barrier_semaphore()
    for dz in range(n):
        if dz:
            pl.semaphore_signal(barrier, inc=1, device_id={"feat": far(dz), "row": c}, device_id_type=MESH)
        pl.semaphore_signal(barrier, inc=1, device_id={"feat": far(dz), "row": other_c}, device_id_type=MESH)
    for cc in (c, other_c):
        pl.semaphore_signal(barrier, inc=1, device_id={"layer": other_x, "row": cc}, device_id_type=MESH)

    own_x = mm(pick(R, 2 * R, 2, x), res.reshape(2 * R, 2 * H)[...]).astype(BF)
    x_mine = jnp.where(c == 0, own_x[:, :H], own_x[:, H:])
    x_other = jnp.where(c == 0, own_x[:, H:], own_x[:, :H])
    for q in range(Q):
        xsend[0, q] = x_mine[:, q * HX:(q + 1) * HX]
        xsend[1, q] = x_other[:, q * HX:(q + 1) * HX]
        xg[z, c, q] = x_mine[:, q * HX:(q + 1) * HX]
    own_m = mm(pick(R, 2 * R, 2, x), mlp.reshape(2 * R, 2 * H)[...]).astype(BF)
    mlpx[c] = jnp.where(c == 0, own_m[:, :H], own_m[:, H:])
    msend[...] = jnp.where(c == 0, own_m[:, H:], own_m[:, :H])

    pl.semaphore_wait(barrier, 2 * n + 1)

    def x_copy(dz, k, q):
        return remote(xsend.at[k, q], xg.at[z, c, q], x_s.at[dz, k, q], x_r.at[dz, k, q],
                      feat=far(dz), row=c if k == 0 else other_c)

    x_list = [(dz, k) for dz in (2, 1, 3) for k in range(2)] + [(0, 1)]
    for q in range(Q):
        for dz, k in x_list:
            unless_ends(dz, lambda: x_copy(dz, k, q).start())

    def y_copy(k, q, to, at):
        cc = c if k == 0 else other_c
        return remote(xg.at[back(2), cc, q], xg.at[back(2), cc, q], y_s.at[k, q], x_r.at[at, k, q], feat=far(to))

    m_copy = remote(msend, mlpx.at[c], m_s, m_r, row=other_c)
    m_copy.start()
    d_all = jnp.where(x == 0, dbias[0:1, :], dbias[1:2, :])
    dsel[...] = jnp.where(c == 0, d_all[:, :H], d_all[:, H:])

    apart = jnp.concatenate([pick(DC, 2 * DC, 2, 0), pick(DC, 2 * DC, 2, 1)], axis=0)

    def split_body(i, carry):
        slot = lax.rem(i, slots)

        @pl.when(i + slots - 1 < nd)
        def _():
            raw_copy(i + slots - 1, lax.rem(i + slots - 1, slots)).start()

        raw_copy(i, slot).wait()
        both = mm(apart, raw[slot]).astype(BF)
        rows = pl.ds(pl.multiple_of(i * DC, DC), DC)
        dg[rows, :] = both[:DC]
        dg[pl.ds(pl.multiple_of(F + i * DC, DC), DC), :] = both[DC:]
        return carry

    def pass_on(q):
        for k in range(2):
            x_copy(2, k, q).wait_recv()
            relays(lambda to, at: y_copy(k, q, to, at).start())

    perm = (lax.broadcasted_iota(jnp.int32, (T, T), 0) == shuf[...]).astype(BF)

    def p_copy(k):
        return remote(pre.at[k, pl.ds(pl.multiple_of(other_c * T2, T2), T2)], pre_recv.at[k], p_s.at[k], p_r.at[k], row=other_c)

    mine = pl.ds(pl.multiple_of(c * T2, T2), T2)

    def f_copy(k):
        return remote(feats.at[k, mine], feats.at[k, mine], f_s.at[k], f_r.at[k], row=other_c)

    lax.fori_loop(0, nd // 2, split_body, 0)
    pass_on(0)
    lax.fori_loop(nd // 2, nd, split_body, 0)
    enc_copy.wait()
    per = 2 if nk % 2 == 0 else 1
    for q in range(Q):
        if q:
            pass_on(q)
        for dz, k in x_list:
            if dz != 2:
                x_copy(dz, k, q).wait_recv()
        lo = q * HX
        xs[:, lo:lo + HX] = dot_first(perm, xg[:, :, q].reshape(T, HX)).astype(BF)

        def pre_body(i, carry):
            rows = pl.ds(pl.multiple_of(i * per * KC, KC), per * KC)
            v = dot_last(xs[:, lo:lo + HX], enc_v[rows, lo:lo + HX])
            for h in range(per):
                part = v[:, h * KC:(h + 1) * KC]
                k = i * per + h
                pre[k] = part if q == 0 else pre[k] + part
                if q == Q - 1:
                    p_copy(k).start()
            return carry

        lax.fori_loop(0, nk // per, pre_body, 0)

    def feat_body(k, carry):
        p_copy(k).wait_recv()
        cols = pl.ds(pl.multiple_of(k * KC, KC), KC)
        v = pre[k, mine, :] + pre_recv[k] + bias[:, cols]
        feats[k, mine, :] = jnp.maximum(v, 0.0).astype(BF)
        f_copy(k).start()
        return carry

    lax.fori_loop(0, nk, feat_body, 0)

    def rows_of(k, size, base=0):
        return pl.ds(pl.multiple_of(base + k * size, KC), size)

    def zero_body(k, carry):
        gacc[:, rows_of(k, KC), :] = jnp.zeros((2, KC, T2), jnp.float32)
        f_copy(k).wait_recv()
        return carry

    lax.fori_loop(0, nk, zero_body, 0)
    m_copy.wait_recv()
    up0, up1 = spread_to(0), spread_to(1)

    def expand(b):
        rows = pl.ds(pl.multiple_of(b * 2 * DC, 2 * DC), 2 * DC)
        turned = feats[b // (KC // DC), :, pl.ds(pl.multiple_of(lax.rem(b, KC // DC) * DC, DC), DC)].T
        fx[rows, :T] = mm(up0, turned).astype(BF)
        fx[rows, T:] = mm(up1, turned).astype(BF)

    def n_copy(j):
        return remote(nsend.at[j], nrecv.at[j], n_s.at[j], n_r.at[j], layer=other_x)

    def right_copy(j, k):
        some = pl.ds(k + 1, n - 1 - k)
        return remote(osend.at[j, some], rr.at[j, some], rs_s.at[j, 0], rs_r.at[j, 0], feat=k + 1)

    def left_copy(j, k):
        some = pl.ds(0, k)
        return remote(osend.at[j, some], rl.at[j, some], rs_s.at[j, 1], rs_r.at[j, 1], feat=k - 1)

    def wide(j):
        return pl.ds(pl.multiple_of(j * NC, NC), NC)

    def all_feats():
        return jnp.concatenate([feats[k] for k in range(nk)], axis=1)

    def send_next(j):
        @pl.when(x == 0)
        def _():
            nsend[j] = mm(all_feats(), dg[pl.ds(F, F), wide(j)]).astype(BF)
            n_copy(j).start()

    def front(j):
        for i in range(2):
            pl.when(2 * j + i < J)(functools.partial(send_next, 2 * j + i))
        facc[j] = mm(all_feats(), dg[pl.ds(0, F), wide(j)]).reshape(n, CR, NC)

        @pl.when(x == 1)
        def _():
            n_copy(j).wait_recv()
            facc[j] = facc[j] + nrecv[j].astype(jnp.float32).reshape(n, CR, NC)

        @pl.when(z == 0)
        def _():
            osend[j, 1:] = facc[j, 1:].astype(BF)
            right_copy(j, 0).start()

        @pl.when(z == n - 1)
        def _():
            osend[j, :n - 1] = facc[j, :n - 1].astype(BF)
            left_copy(j, n - 1).start()

    def go_right(j, k):
        right_copy(j, k - 1).wait_recv()
        osend[j, k + 1:] = (facc[j, k + 1:] + rr[j, k + 1:].astype(jnp.float32)).astype(BF)
        right_copy(j, k).start()

    def go_left(j, k):
        left_copy(j, k + 1).wait_recv()
        osend[j, :k] = (facc[j, :k] + rl[j, :k].astype(jnp.float32)).astype(BF)
        left_copy(j, k).start()

    def relay_near(j):
        pl.when(z == 1)(lambda: go_right(j, 1))
        pl.when(z == 2)(lambda: go_left(j, 2))

    def relay_far(j):
        pl.when(z == 2)(lambda: go_right(j, 2))
        pl.when(z == 1)(lambda: go_left(j, 1))

    def a_copy(j, b, way):
        to = jnp.minimum(z + 1, n - 1) if way == 0 else jnp.maximum(z - 1, 0)
        return remote(e.at[j, 0, b], e.at[j, 0, b], a_s.at[j, way, b], a_r.at[j, b], feat=to)

    def t_copy(j, b):
        return remote(e.at[j, 0, b], e.at[j, 1, b], t_s.at[j, b], t_r.at[j, b], layer=other_x)

    def final(j):
        @pl.when(z == 0)
        def _():
            left_copy(j, 1).wait_recv()

        @pl.when(z == n - 1)
        def _():
            right_copy(j, n - 2).wait_recv()

        @pl.when(z > 0)
        def _():
            facc[j, z] = facc[j, z] + rr[j, z].astype(jnp.float32)

        @pl.when(z < n - 1)
        def _():
            facc[j, z] = facc[j, z] + rl[j, z].astype(jnp.float32)

        total = facc[j, z] + dsel[:, wide(j)]
        e[j, 0, z] = (total - mlpx[:, :, wide(j)].reshape(CR, NC).astype(jnp.float32)).astype(BF)
        pl.when(z < n - 1)(lambda: a_copy(j, z, 0).start())
        pl.when(z > 0)(lambda: a_copy(j, z, 1).start())
        pl.when(x == 1)(lambda: t_copy(j, z).start())
        kept = total.astype(BF).reshape(2, R, NC)
        rc[0, j] = kept[0]
        rc[1, j] = kept[1]

    def hop(j, h):
        @pl.when(z >= h)
        def _():
            a_copy(j, z - h, 0).wait_recv()
            pl.when(z < n - 1)(lambda: a_copy(j, z - h, 0).start())
            pl.when(x == 1)(lambda: t_copy(j, z - h).start())

        @pl.when(z + h < n)
        def _():
            a_copy(j, z + h, 1).wait_recv()
            pl.when(z > 0)(lambda: a_copy(j, z + h, 1).start())
            pl.when(x == 1)(lambda: t_copy(j, z + h).start())

    def g_copy(k):
        return remote(gacc.at[other_c, rows_of(k, GC)], g_recv.at[rows_of(k, GC)], g_s.at[k], g_r.at[k], row=other_c)

    def grads(j):
        last = j == J - 1

        def body(k, carry):
            rows = rows_of(k, GC)
            v = dot_last(dg[rows, wide(j)], e[j, 0].reshape(T, NC))
            gacc[0, rows, :] = gacc[0, rows, :] + v[:, :T2]
            gacc[1, rows, :] = gacc[1, rows, :] + v[:, T2:]
            pl.when(last)(lambda: g_copy(k).start())
            return carry

        lax.fori_loop(0, F // GC, body, 0)

    def both_grads(j):
        last = j == J - 1
        for b in range(n):
            t_copy(j, b).wait_recv()

        def body(k, carry):
            rows, below = rows_of(k, GC), rows_of(k, GC, F)
            v = dot_last(dg[rows, wide(j)], e[j, 0].reshape(T, NC)) + dot_last(dg[below, wide(j)], e[j, 1].reshape(T, NC))
            gacc[0, rows, :] = gacc[0, rows, :] + v[:, :T2]
            gacc[1, rows, :] = gacc[1, rows, :] + v[:, T2:]
            pl.when(last)(lambda: g_copy(k).start())
            return carry

        lax.fori_loop(0, F // GC, body, 0)

    def weights(j):
        def body(k, carry):
            rows = rows_of(k, 2 * GC)
            dg[rows, wide(j)] = (scale * mm(fx[rows, :T], e[j, 0].reshape(T, NC))).astype(BF)
            return carry

        lax.fori_loop(0, F // GC, body, 0)

    def both_weights(j):
        def body(k, carry):
            rows = rows_of(k, 2 * GC)
            dg[rows, wide(j)] = (scale * mm(fx[rows, :], e[j].reshape(2 * T, NC))).astype(BF)
            return carry

        lax.fori_loop(0, F // GC, body, 0)

    cuts = (0, J // 3, 2 * J // 3, J)

    def b_copy(k, p):
        dx, dc = k // 2, k % 2
        to_x = other_x if dx else x
        to_c = other_c if dc else c
        some = pl.ds(cuts[p], cuts[p + 1] - cuts[p])
        return remote(rc.at[to_c, some], rb.at[x, c, some], b_s.at[k, p], b_r.at[k, p], layer=to_x, row=to_c)

    def start_b(p):
        for k in range(1, 4):
            b_copy(k, p).start()

    def early_b(j):
        for p in range(2):
            pl.when(j == cuts[p + 1] - 1)(functools.partial(start_b, p))

    def late_b(j):
        pl.when(j == J - 1)(lambda: start_b(2))

    stages = (
        (0, None, front), (1, None, relay_near), (2, None, relay_far), (3, None, final), (3, None, early_b),
        (4, None, lambda j: hop(j, 1)), (5, None, lambda j: hop(j, 2)), (6, None, lambda j: hop(j, 3)), (6, None, late_b),
        (7, 1, grads), (LAG0, 0, both_grads), (8, 1, weights), (LAG0 + 1, 0, both_weights))
    steps = J + LAG0 + 1
    share = pl.cdiv(nd, 8)

    def pipe(s, carry):
        for lag, side, act in stages:
            live = jnp.logical_and(s >= lag, s < J + lag)
            if side is not None:
                live = jnp.logical_and(live, x == side)
            pl.when(live)(functools.partial(act, s - lag))
        for i in range(share):
            pl.when(s * share + i < nd)(functools.partial(expand, s * share + i))
        return carry

    lax.fori_loop(0, steps, pipe, 0)

    def q_copy(k):
        return remote(gt.at[c, rows_of(k, GC)], gt.at[c, rows_of(k, GC)], q_s.at[k], q_r.at[k], row=other_c)

    def mask_body(k, carry):
        g_copy(k).wait_recv()
        rows = rows_of(k, GC)
        seen = jnp.concatenate([feats[k * (GC // KC) + i, mine, :] for i in range(GC // KC)], axis=1).T
        v = (gacc[c, rows, :] + g_recv[rows, :]) * scale
        gt[c, rows, :] = jnp.where(seen.astype(jnp.float32) > 0, v, 0.0).astype(BF)
        q_copy(k).start()
        return carry

    lax.fori_loop(0, F // GC, mask_body, 0)
    rb[x, c] = rc[c]

    def sent_body(k, carry):
        p_copy(k).wait_send()
        f_copy(k).wait_send()
        return carry

    lax.fori_loop(0, nk, sent_body, 0)
    for q in range(Q):
        for dz, k in x_list:
            unless_ends(dz, lambda: x_copy(dz, k, q).wait_send())
        for k in range(2):
            relays(lambda to, at: y_copy(k, q, to, at).wait_send())
    m_copy.wait_send()

    def sent_chunk(j, carry):
        for k in range(n):
            @pl.when(z == k)
            def _():
                if k < n - 1:
                    right_copy(j, k).wait_send()
                if k > 0:
                    left_copy(j, k).wait_send()

        for b in range(n):
            pl.when(jnp.logical_and(z >= b, z < n - 1))(lambda: a_copy(j, b, 0).wait_send())
            pl.when(jnp.logical_and(z <= b, z > 0))(lambda: a_copy(j, b, 1).wait_send())

        @pl.when(x == 0)
        def _():
            n_copy(j).wait_send()

        @pl.when(x == 1)
        def _():
            for b in range(n):
                t_copy(j, b).wait_send()

        return carry

    lax.fori_loop(0, J, sent_chunk, 0)
    for k in range(1, 4):
        for p in range(3):
            b_copy(k, p).wait_recv()
    for h in range(2):
        for j in range(J):
            lo = h * H + j * NC
            parts[:, lo:lo + NC] = rb[:, h, j].reshape(2 * R, NC)
    for k in range(1, 4):
        for p in range(3):
            b_copy(k, p).wait_send()

    def last_body(k, carry):
        q_copy(k).wait_recv()
        g_copy(k).wait_send()
        q_copy(k).wait_send()
        return carry

    lax.fori_loop(0, F // GC, last_body, 0)


def weight_kernel(dg, gt, xs, parts, enc_grad, dec_grad, bgrad, rebuilt, ebuf, bbuf, rbuf, dsem, esem, bsem, rsem):
    F, T2 = gt.shape[1:]
    H = xs.shape[1]
    R2 = parts.shape[0]
    nb = F // KC

    def rows_of(i, size):
        return pl.ds(pl.multiple_of(i * size, size), size)

    def d_copy(i):
        rows = rows_of(i, 2 * KC)
        return pltpu.make_async_copy(dg.at[rows], dec_grad.reshape(2 * F, H).at[rows], dsem.at[i])

    def e_copy(i):
        rows = rows_of(i, KC)
        return pltpu.make_async_copy(ebuf.at[rows], enc_grad.at[rows], esem.at[i])

    b_copy = pltpu.make_async_copy(bbuf, bgrad, bsem)
    r_copy = pltpu.make_async_copy(rbuf, rebuilt.reshape(R2, 2 * H), rsem)
    for i in range(nb):
        d_copy(i).start()
    i = lax.broadcasted_iota(jnp.int32, (R2, R2), 0)
    j = lax.broadcasted_iota(jnp.int32, (R2, R2), 1)
    inter = (j == (i % 2) * (R2 // 2) + i // 2).astype(BF)
    rbuf[...] = mm(inter, parts[...]).astype(BF)
    r_copy.start()
    ones = jnp.ones((8, 2 * T2), BF)

    def block(i, carry):
        rows = rows_of(i, KC)
        g = jnp.concatenate([gt[0, rows, :], gt[1, rows, :]], axis=1)
        ebuf[rows, :] = mm(g, xs[...]).astype(BF)
        e_copy(i).start()
        bbuf[:, rows] = dot_last(ones, g)[0:1]
        return carry

    lax.fori_loop(0, nb, block, 0)
    b_copy.start()
    for i in range(nb):
        d_copy(i).wait()
        e_copy(i).wait()
    r_copy.wait()
    b_copy.wait()


def fused(resid_buf, shuffle, mlp_out, enc_weight, dec_weight, enc_bias, dec_bias):
    n = lax.axis_size("feat")
    R = resid_buf.shape[0]
    F, H = enc_weight.shape[1:]
    T = R * n * 2
    T2, CR = T // 2, 2 * R
    J = H // KC
    NC, nk = H // J, F // KC
    Q = halves_of(H)
    HX = H // Q
    f32 = jnp.float32
    vm = pl.BlockSpec(memory_space=pltpu.VMEM)
    hbm = pl.BlockSpec(memory_space=pl.ANY)
    dma = pltpu.SemaphoreType.DMA
    vmem = pltpu.VMEM
    shape = jax.ShapeDtypeStruct
    outs = ((2 * F, H), (T, H), (2, F, T2), (2 * R, 2 * H))
    held = sum(2 * math.prod(a) for a in outs)
    dg, xs, gt, parts = pl.pallas_call(
        functools.partial(step_kernel, n, J),
        out_shape=tuple(vmem(a, BF) for a in outs),
        in_specs=[vm, vm, vm, hbm, hbm, vm, vm],
        out_specs=(vm,) * 4,
        scratch_shapes=[
            vmem((2 * F, 2 * T), BF), vmem((J, 2, n, CR, NC), BF), vmem((F, H), BF), vmem((4, 2 * DC, H), BF),
            vmem((2, Q, R, HX), BF), vmem((n, 2, Q, R, HX), BF),
            vmem((2, R, H), BF), vmem((R, H), BF), vmem((1, H), f32),
            vmem((nk, T, KC), f32), vmem((nk, T2, KC), f32), vmem((nk, T, KC), BF),
            vmem((J, T, NC), BF), vmem((J, T, NC), BF), vmem((J, n, CR, NC), f32),
            vmem((J, n, CR, NC), BF), vmem((J, n, CR, NC), BF), vmem((J, n, CR, NC), BF),
            vmem((2, J, R, NC), BF), vmem((2, 2, J, R, NC), BF),
            vmem((2, F, T2), f32), vmem((F, T2), f32),
            dma, dma((4,)), dma((n, 2, Q)), dma((n, 2, Q)), dma((2, Q)), dma, dma,
            dma((nk,)), dma((nk,)), dma((nk,)), dma((nk,)), dma((J,)), dma((J,)),
            dma((J, 2)), dma((J, 2)), dma((J, 2, n)), dma((J, n)), dma((J, n)), dma((J, n)),
            dma((4, 3)), dma((4, 3)), dma((nk,)), dma((nk,)), dma((nk,)), dma((nk,)),
        ],
        compiler_params=pltpu.CompilerParams(
            collective_id=0, has_side_effects=True, vmem_limit_bytes=VMEM_LIMIT - held),
    )(resid_buf, shuffle.reshape(1, T), mlp_out, enc_weight[0], dec_weight[0], enc_bias, dec_bias)
    enc_grad, dec_grad, bgrad, rebuilt = pl.pallas_call(
        weight_kernel,
        out_shape=(
            shape((F, H), BF), shape((F, 2, H), BF), shape((1, F), f32), shape((R, 2, 2 * H), BF)),
        in_specs=[vm] * 4,
        out_specs=(hbm,) * 4,
        scratch_shapes=[
            vmem((F, H), BF), vmem((1, F), f32), vmem((2 * R, 2 * H), BF), dma((nk,)), dma((nk,)), dma, dma],
        compiler_params=pltpu.CompilerParams(vmem_limit_bytes=VMEM_LIMIT // 3),
    )(dg, gt, xs, parts)
    return rebuilt, enc_grad[None], dec_grad[None], bgrad


def chosen(resid_buf, shuffle, mlp_out, enc_weight, dec_weight, enc_bias, dec_bias):
    args = (resid_buf, shuffle, mlp_out, enc_weight, dec_weight, enc_bias, dec_bias)
    rows, width = resid_buf.shape[0], enc_weight.shape[2]
    fits = (
        lax.axis_size("layer") == LAYERS == 2 and lax.axis_size("row") == 2
        and lax.axis_size("feat") == 4 and rows % 16 == 0
        and width % KC == 0 and width // KC >= 3 and enc_weight.shape[1] % GC == 0)
    return fused(*args) if fits else on_device(*args)


def solution(mesh):
    return jax.shard_map(
        chosen,
        mesh=mesh,
        in_specs=(
            P(("groups", "feat", "row"), None, None),
            P("groups"),
            P(("groups", "feat", "row"), None, None),
            P("layer", "feat", "row"),
            P("layer", "feat", None, "row"),
            P("layer", "feat"),
            P(),
        ),
        out_specs=(
            P(("groups", "feat", "row"), None, None),
            P(("groups", "layer"), "feat", "row"),
            P(("groups", "layer"), "feat", None, "row"),
            P(("groups", "layer"), "feat"),
        ),
        check_vma=False,
    )
```

```python
import functools
import math

import jax
import jax.numpy as jnp
from jax import lax
from jax.experimental import pallas as pl
from jax.experimental.pallas import tpu as pltpu
from jax.sharding import PartitionSpec as P

LAYERS = 2


def from_behind(block, axis, distance):
    devices = range(lax.axis_size(axis))
    route = [(i - distance, i) for i in devices if i - distance in devices]
    return lax.ppermute(block, axis, route)


def dot_last(left, right):
    return lax.dot_general(
        left, right, (((1,), (1,)), ((), ())), preferred_element_type=jnp.float32
    )


def dot_first(left, right):
    return lax.dot_general(
        left, right, (((0,), (0,)), ((), ())), preferred_element_type=jnp.float32
    )


def on_device(resid_buf, shuffle, mlp_out, enc_weight, dec_weight, enc_bias, dec_bias):
    feat_count = lax.axis_size("feat")
    row_count = lax.axis_size("row")
    sub_blocks = lax.axis_size("layer") // LAYERS
    layer_pos = lax.axis_index("layer")
    row_pos = lax.axis_index("row")
    source = layer_pos // sub_blocks
    rows_each = resid_buf.shape[0]
    width = dec_bias.shape[1]
    half_width = enc_weight.shape[2]
    local_rows = rows_each * feat_count
    total_rows = local_rows * row_count
    loss_scale = float(total_rows) ** (-0.5)
    own_layer = lax.dynamic_index_in_dim(resid_buf, source, axis=1, keepdims=False)
    buffer_all = lax.all_gather(own_layer, ("feat", "row"), axis=0, tiled=True)
    batch_rows = jnp.take(buffer_all, shuffle, axis=0)
    blocks = batch_rows.reshape(feat_count, row_count, rows_each, width)
    inputs_half = lax.dynamic_slice_in_dim(
        jnp.swapaxes(blocks, 0, 1), row_pos * half_width, half_width, axis=3
    )
    inputs_half = inputs_half.reshape(total_rows, half_width)
    own_half_dec = dec_weight[0][:, 0]
    next_half_dec = dec_weight[0][:, 1]
    pre_all = lax.psum(dot_last(inputs_half, enc_weight[0]), "row") + enc_bias[0]
    features_all = jnp.maximum(pre_all, 0.0).astype(jnp.bfloat16)
    own_part = jnp.dot(features_all, own_half_dec, preferred_element_type=jnp.float32)
    next_part = jnp.dot(features_all, next_half_dec, preferred_element_type=jnp.float32)
    carried = from_behind(next_part, "layer", sub_blocks)
    spread = (own_part + carried).reshape(row_count, local_rows, half_width)
    halves = lax.psum_scatter(spread, "feat", scatter_dimension=1, tiled=True)
    joined = lax.all_to_all(halves, "row", split_axis=0, concat_axis=2, tiled=True)
    section_sum = joined.reshape(rows_each, width)
    target_ids = jnp.arange(LAYERS, dtype=jnp.int32)
    target_slots = jnp.where((target_ids == source)[:, None, None], section_sum[None], 0.0)
    totals = lax.psum(target_slots, "layer")
    recon_sum = jnp.swapaxes(totals, 0, 1) + dec_bias[None]
    errors = (recon_sum - mlp_out.astype(jnp.float32)).astype(jnp.bfloat16)
    gathered = lax.all_gather(errors, ("feat", "row"), axis=0, tiled=True)
    error_grid = gathered.reshape(feat_count, row_count, rows_each, LAYERS, width)
    errors_mine = lax.dynamic_index_in_dim(error_grid, row_pos, axis=1, keepdims=False)
    errors_mine = errors_mine.reshape(local_rows, LAYERS, width)
    errors_half = lax.dynamic_slice_in_dim(
        jnp.swapaxes(error_grid, 0, 1), row_pos * half_width, half_width, axis=4
    )
    errors_half = errors_half.reshape(total_rows, LAYERS, half_width)
    live_next = source + 1 < LAYERS
    next_index = jnp.minimum(source + 1, LAYERS - 1)
    half_own = lax.dynamic_index_in_dim(errors_half, source, axis=1, keepdims=False)
    half_next = lax.dynamic_index_in_dim(errors_half, next_index, axis=1, keepdims=False)
    half_next = jnp.where(live_next, half_next, jnp.zeros_like(half_next))
    half_terms = dot_last(half_own, own_half_dec) + dot_last(half_next, next_half_dec)
    grad_feats = lax.psum(half_terms, "row") * loss_scale
    grad_all = jnp.where(pre_all > 0, grad_feats, 0.0).astype(jnp.bfloat16)
    grad_own = loss_scale * dot_first(features_all, half_own)
    grad_next = loss_scale * dot_first(features_all, half_next)
    enc_grad = dot_first(grad_all, inputs_half).astype(jnp.bfloat16)
    dec_grad = jnp.stack([grad_own, grad_next], axis=1).astype(jnp.bfloat16)
    bias_grad = jnp.sum(grad_all.astype(jnp.float32), axis=0)
    return (recon_sum.astype(jnp.bfloat16), enc_grad[None], dec_grad[None], bias_grad[None])

KC = 256
DC = 128
GC = 1024
LAG0 = 8
LAG1 = 7
MESH = pl.DeviceIdType.MESH
VMEM_LIMIT = 67043328
BF = jnp.bfloat16


def pick(rows, cols, stride, offset):
    r = lax.broadcasted_iota(jnp.int32, (rows, cols), 0)
    c = lax.broadcasted_iota(jnp.int32, (rows, cols), 1)
    return (c == stride * r + offset).astype(BF)


def spread_to(offset):
    r = lax.broadcasted_iota(jnp.int32, (2 * DC, DC), 0)
    c = lax.broadcasted_iota(jnp.int32, (2 * DC, DC), 1)
    return (r == 2 * c + offset).astype(BF)


def mm(left, right):
    return jnp.dot(left, right, preferred_element_type=jnp.float32)


def halves_of(width):
    return next(q for q in (3, 2, 1) if width % (q * DC) == 0)


def step_kernel(
    n, J, res, shuf, mlp, enc, dec, bias, dbias,
    dg, xs, gt, parts,
    fx, e, enc_v, raw, xsend, xg, mlpx, msend, dsel, pre, pre_recv, feats,
    nsend, nrecv, facc, osend, rr, rl, rc, rb, gacc, g_recv,
    sem_l, sem_raw, x_s, x_r, y_s, m_s, m_r, p_s, p_r, f_s, f_r, n_s, n_r,
    rs_s, rs_r, a_s, a_r, t_s, t_r, b_s, b_r, g_s, g_r, q_s, q_r,
):
    z = lax.axis_index("feat")
    x = lax.axis_index("layer")
    c = lax.axis_index("row")
    Q, R, HX = xsend.shape[1:]
    F, H = enc_v.shape
    T = xs.shape[0]
    T2, CR, NC = T // 2, 2 * R, H // J
    nk, slots = F // KC, raw.shape[0]
    scale = float(T) ** (-0.5)
    other_c, other_x = 1 - c, 1 - x

    def far(dz):
        return lax.rem(z + dz, n)

    def back(dz):
        return lax.rem(z + n - dz, n)

    def remote(src, dst, send, recv, **where):
        return pltpu.make_async_remote_copy(
            src_ref=src, dst_ref=dst, send_sem=send, recv_sem=recv,
            device_id=where, device_id_type=MESH)

    def unless_ends(dz, act):
        if dz == n - 1:
            pl.when(z != 0)(act)
        elif dz == 1:
            pl.when(z != n - 1)(act)
        else:
            act()

    def relays(act):
        pl.when(z == 2)(lambda: act(1, 3))
        pl.when(z == 1)(lambda: act(3, 1))

    def raw_copy(i, slot):
        return pltpu.make_async_copy(
            dec.reshape(2 * F, H).at[pl.ds(pl.multiple_of(i * 2 * DC, 2 * DC), 2 * DC)], raw.at[slot], sem_raw.at[slot])

    nd = F // DC
    for i in range(slots - 1):
        raw_copy(i, i).start()
    enc_copy = pltpu.make_async_copy(enc, enc_v, sem_l)
    enc_copy.start()

    barrier = pltpu.get_barrier_semaphore()
    for dz in range(n):
        if dz:
            pl.semaphore_signal(barrier, inc=1, device_id={"feat": far(dz), "row": c}, device_id_type=MESH)
        pl.semaphore_signal(barrier, inc=1, device_id={"feat": far(dz), "row": other_c}, device_id_type=MESH)
    for cc in (c, other_c):
        pl.semaphore_signal(barrier, inc=1, device_id={"layer": other_x, "row": cc}, device_id_type=MESH)

    own_x = mm(pick(R, 2 * R, 2, x), res.reshape(2 * R, 2 * H)[...]).astype(BF)
    x_mine = jnp.where(c == 0, own_x[:, :H], own_x[:, H:])
    x_other = jnp.where(c == 0, own_x[:, H:], own_x[:, :H])
    for q in range(Q):
        xsend[0, q] = x_mine[:, q * HX:(q + 1) * HX]
        xsend[1, q] = x_other[:, q * HX:(q + 1) * HX]
        xg[z, c, q] = x_mine[:, q * HX:(q + 1) * HX]
    own_m = mm(pick(R, 2 * R, 2, x), mlp.reshape(2 * R, 2 * H)[...]).astype(BF)
    mlpx[c] = jnp.where(c == 0, own_m[:, :H], own_m[:, H:])
    msend[...] = jnp.where(c == 0, own_m[:, H:], own_m[:, :H])

    pl.semaphore_wait(barrier, 2 * n + 1)

    def x_copy(dz, k, q):
        return remote(xsend.at[k, q], xg.at[z, c, q], x_s.at[dz, k], x_r.at[dz, k, q],
                      feat=far(dz), row=c if k == 0 else other_c)

    x_list = [(dz, k) for dz in (2, 1, 3) for k in range(2)] + [(0, 1)]
    for q in range(Q):
        for dz, k in x_list:
            unless_ends(dz, lambda: x_copy(dz, k, q).start())

    def y_copy(k, q, to, at):
        cc = c if k == 0 else other_c
        return remote(xg.at[back(2), cc, q], xg.at[back(2), cc, q], y_s.at[k], x_r.at[at, k, q], feat=far(to))

    m_copy = remote(msend, mlpx.at[c], m_s, m_r, row=other_c)
    m_copy.start()
    d_all = jnp.where(x == 0, dbias[0:1, :], dbias[1:2, :])
    dsel[...] = jnp.where(c == 0, d_all[:, :H], d_all[:, H:])

    apart = jnp.concatenate([pick(DC, 2 * DC, 2, 0), pick(DC, 2 * DC, 2, 1)], axis=0)

    def split_body(i, carry):
        slot = lax.rem(i, slots)

        @pl.when(i + slots - 1 < nd)
        def _():
            raw_copy(i + slots - 1, lax.rem(i + slots - 1, slots)).start()

        raw_copy(i, slot).wait()
        both = mm(apart, raw[slot]).astype(BF)
        rows = pl.ds(pl.multiple_of(i * DC, DC), DC)
        dg[rows, :] = both[:DC]
        dg[pl.ds(pl.multiple_of(F + i * DC, DC), DC), :] = both[DC:]
        return carry

    def pass_on(q):
        for k in range(2):
            x_copy(2, k, q).wait_recv()
            relays(lambda to, at: y_copy(k, q, to, at).start())

    perm = (lax.broadcasted_iota(jnp.int32, (T, T), 0) == shuf[...]).astype(BF)

    def p_copy(k):
        return remote(pre.at[k, pl.ds(pl.multiple_of(other_c * T2, T2), T2)], pre_recv.at[k], p_s, p_r.at[k], row=other_c)

    mine = pl.ds(pl.multiple_of(c * T2, T2), T2)

    def f_copy(k):
        return remote(feats.at[k, mine], feats.at[k, mine], f_s, f_r, row=other_c)

    lax.fori_loop(0, nd // 2, split_body, 0)
    pass_on(0)
    lax.fori_loop(nd // 2, nd, split_body, 0)
    enc_copy.wait()
    per = 2 if nk % 2 == 0 else 1
    for q in range(Q):
        if q:
            pass_on(q)
        for dz, k in x_list:
            if dz != 2:
                x_copy(dz, k, q).wait_recv()
        lo = q * HX
        xs[:, lo:lo + HX] = dot_first(perm, xg[:, :, q].reshape(T, HX)).astype(BF)

        def pre_body(i, carry):
            rows = pl.ds(pl.multiple_of(i * per * KC, KC), per * KC)
            v = dot_last(xs[:, lo:lo + HX], enc_v[rows, lo:lo + HX])
            for h in range(per):
                part = v[:, h * KC:(h + 1) * KC]
                k = i * per + h
                pre[k] = part if q == 0 else pre[k] + part
                if q == Q - 1:
                    p_copy(k).start()
            return carry

        lax.fori_loop(0, nk // per, pre_body, 0)

    def feat_body(k, carry):
        p_copy(k).wait_recv()
        cols = pl.ds(pl.multiple_of(k * KC, KC), KC)
        v = pre[k, mine, :] + pre_recv[k] + bias[:, cols]
        feats[k, mine, :] = jnp.maximum(v, 0.0).astype(BF)
        f_copy(k).start()
        return carry

    lax.fori_loop(0, nk, feat_body, 0)

    def rows_of(k, size, base=0):
        return pl.ds(pl.multiple_of(base + k * size, KC), size)

    def zero_body(k, carry):
        gacc[:, rows_of(k, KC), :] = jnp.zeros((2, KC, T2), jnp.float32)
        return carry

    lax.fori_loop(0, nk, zero_body, 0)
    all_f = remote(feats.at[:, mine], feats.at[:, mine], f_s, f_r, row=other_c)
    all_f.wait_recv()
    m_copy.wait_recv()
    up0, up1 = spread_to(0), spread_to(1)

    def expand(b):
        rows = pl.ds(pl.multiple_of(b * 2 * DC, 2 * DC), 2 * DC)
        turned = feats[b // (KC // DC), :, pl.ds(pl.multiple_of(lax.rem(b, KC // DC) * DC, DC), DC)].T
        fx[rows, :T] = mm(up0, turned).astype(BF)

        @pl.when(x == 0)
        def _():
            fx[rows, T:] = mm(up1, turned).astype(BF)

    def n_copy(j):
        return remote(nsend.at[j], nrecv.at[j], n_s, n_r.at[j], layer=other_x)

    def right_copy(j, k, onward):
        some = pl.ds(k + 2, n - 2 - k) if onward else pl.ds(k + 1, 1)
        return remote(osend.at[j, some], rr.at[j, some], rs_s.at[0], rs_r.at[j, 0, onward], feat=k + 1)

    def left_copy(j, k, onward):
        some = pl.ds(0, k - 1) if onward else pl.ds(k - 1, 1)
        return remote(osend.at[j, some], rl.at[j, some], rs_s.at[1], rs_r.at[j, 1, onward], feat=k - 1)

    def send_right(j, k):
        for lo, hi, onward in ((k + 2, n, 1), (k + 1, k + 2, 0)):
            if lo < hi:
                v = facc[j, lo:hi]
                if k > 0:
                    v = v + rr[j, lo:hi].astype(jnp.float32)
                osend[j, lo:hi] = v.astype(BF)
                right_copy(j, k, onward).start()

    def send_left(j, k):
        for lo, hi, onward in ((0, k - 1, 1), (k - 1, k, 0)):
            if lo < hi:
                v = facc[j, lo:hi]
                if k < n - 1:
                    v = v + rl[j, lo:hi].astype(jnp.float32)
                osend[j, lo:hi] = v.astype(BF)
                left_copy(j, k, onward).start()

    def wide(j):
        return pl.ds(pl.multiple_of(j * NC, NC), NC)

    def all_feats():
        return jnp.concatenate([feats[k] for k in range(nk)], axis=1)

    def send_next(j):
        @pl.when(x == 0)
        def _():
            nsend[j] = mm(all_feats(), dg[pl.ds(F, F), wide(j)]).astype(BF)
            n_copy(j).start()

    def front(j):
        for i in range(2):
            pl.when(2 * j + i < J)(functools.partial(send_next, 2 * j + i))
        facc[j] = mm(all_feats(), dg[pl.ds(0, F), wide(j)]).reshape(n, CR, NC)

        @pl.when(x == 1)
        def _():
            n_copy(j).wait_recv()
            facc[j] = facc[j] + nrecv[j].astype(jnp.float32).reshape(n, CR, NC)

        pl.when(z == 0)(lambda: send_right(j, 0))
        pl.when(z == n - 1)(lambda: send_left(j, n - 1))

    def go_right(j, k):
        right_copy(j, k - 1, 1).wait_recv()
        send_right(j, k)

    def go_left(j, k):
        left_copy(j, k + 1, 1).wait_recv()
        send_left(j, k)

    def relay_near(j):
        pl.when(z == 1)(lambda: go_right(j, 1))
        pl.when(z == 2)(lambda: go_left(j, 2))

    def relay_far(j):
        pl.when(z == 2)(lambda: go_right(j, 2))
        pl.when(z == 1)(lambda: go_left(j, 1))

    def a_copy(j, b, way):
        to = jnp.minimum(z + 1, n - 1) if way == 0 else jnp.maximum(z - 1, 0)
        return remote(e.at[j, 0, b], e.at[j, 0, b], a_s.at[way], a_r.at[j, b], feat=to)

    def t_copy(j, b):
        return remote(e.at[j, 0, b], e.at[j, 1, b], t_s, t_r.at[j], layer=other_x)

    def final(j):
        for k in range(n):
            @pl.when(z == k)
            def _():
                if k > 0:
                    right_copy(j, k - 1, 0).wait_recv()
                if k < n - 1:
                    left_copy(j, k + 1, 0).wait_recv()

        @pl.when(z > 0)
        def _():
            facc[j, z] = facc[j, z] + rr[j, z].astype(jnp.float32)

        @pl.when(z < n - 1)
        def _():
            facc[j, z] = facc[j, z] + rl[j, z].astype(jnp.float32)

        total = facc[j, z] + dsel[:, wide(j)]
        e[j, 0, z] = (total - mlpx[:, :, wide(j)].reshape(CR, NC).astype(jnp.float32)).astype(BF)
        pl.when(z < n - 1)(lambda: a_copy(j, z, 0).start())
        pl.when(z > 0)(lambda: a_copy(j, z, 1).start())
        pl.when(x == 1)(lambda: t_copy(j, z).start())
        kept = total.astype(BF).reshape(2, R, NC)
        rc[0, j] = kept[0]
        rc[1, j] = kept[1]

    def hop(j, h):
        @pl.when(z >= h)
        def _():
            a_copy(j, z - h, 0).wait_recv()
            pl.when(z < n - 1)(lambda: a_copy(j, z - h, 0).start())
            pl.when(x == 1)(lambda: t_copy(j, z - h).start())

        @pl.when(z + h < n)
        def _():
            a_copy(j, z + h, 1).wait_recv()
            pl.when(z > 0)(lambda: a_copy(j, z + h, 1).start())
            pl.when(x == 1)(lambda: t_copy(j, z + h).start())

    def g_copy(k):
        return remote(gacc.at[other_c, rows_of(k, GC)], g_recv.at[rows_of(k, GC)], g_s, g_r.at[k], row=other_c)

    def grads(j):
        last = j == J - 1

        def body(k, carry):
            rows = rows_of(k, GC)
            v = dot_last(dg[rows, wide(j)], e[j, 0].reshape(T, NC))
            gacc[0, rows, :] = gacc[0, rows, :] + v[:, :T2]
            gacc[1, rows, :] = gacc[1, rows, :] + v[:, T2:]
            pl.when(last)(lambda: g_copy(k).start())
            return carry

        lax.fori_loop(0, F // GC, body, 0)

    def both_grads(j):
        last = j == J - 1
        remote(e.at[j, 0], e.at[j, 1], t_s, t_r.at[j], layer=other_x).wait_recv()

        def body(k, carry):
            rows, below = rows_of(k, GC), rows_of(k, GC, F)
            v = dot_last(dg[rows, wide(j)], e[j, 0].reshape(T, NC)) + dot_last(dg[below, wide(j)], e[j, 1].reshape(T, NC))
            gacc[0, rows, :] = gacc[0, rows, :] + v[:, :T2]
            gacc[1, rows, :] = gacc[1, rows, :] + v[:, T2:]
            pl.when(last)(lambda: g_copy(k).start())
            return carry

        lax.fori_loop(0, F // GC, body, 0)

    def weights(j):
        def body(k, carry):
            rows = rows_of(k, 2 * GC)
            dg[rows, wide(j)] = (scale * mm(fx[rows, :T], e[j, 0].reshape(T, NC))).astype(BF)
            return carry

        lax.fori_loop(0, F // GC, body, 0)

    def both_weights(j):
        def body(k, carry):
            rows = rows_of(k, 2 * GC)
            dg[rows, wide(j)] = (scale * mm(fx[rows, :], e[j].reshape(2 * T, NC))).astype(BF)
            return carry

        lax.fori_loop(0, F // GC, body, 0)

    cuts = (0, J // 3, 2 * J // 3, J)

    def b_copy(k, p):
        dx, dc = k // 2, k % 2
        to_x = other_x if dx else x
        to_c = other_c if dc else c
        some = pl.ds(0, J) if p is None else pl.ds(cuts[p], cuts[p + 1] - cuts[p])
        return remote(rc.at[to_c, some], rb.at[x, c, some], b_s.at[k], b_r.at[k], layer=to_x, row=to_c)

    def start_b(p):
        for k in range(1, 4):
            b_copy(k, p).start()

    def early_b(j):
        for p in range(2):
            pl.when(j == cuts[p + 1] - 1)(functools.partial(start_b, p))

    def late_b(j):
        pl.when(j == J - 1)(lambda: start_b(2))

    stages = (
        (0, None, front), (1, None, relay_near), (2, None, relay_far), (3, None, final), (3, None, early_b),
        (4, None, lambda j: hop(j, 1)), (5, None, lambda j: hop(j, 2)), (6, None, lambda j: hop(j, 3)), (6, None, late_b),
        (LAG1, 1, grads), (LAG1 + 1, 1, weights), (LAG0, 0, both_grads), (LAG0, 0, both_weights))
    steps = J + max(LAG0, LAG1 + 1)
    share = pl.cdiv(nd, LAG0)

    def pipe(s, carry):
        for lag, side, act in stages:
            live = jnp.logical_and(s >= lag, s < J + lag)
            if side is not None:
                live = jnp.logical_and(live, x == side)
            pl.when(live)(functools.partial(act, s - lag))
        for i in range(share):
            pl.when(jnp.logical_and(x == 0, s * share + i < nd))(functools.partial(expand, s * share + i))
        return carry

    @pl.when(x == 1)
    def _():
        def body(b, carry):
            expand(b)
            return carry

        lax.fori_loop(0, nd, body, 0)

    lax.fori_loop(0, steps, pipe, 0)

    def q_copy(k):
        return remote(gt.at[c, rows_of(k, GC)], gt.at[c, rows_of(k, GC)], q_s, q_r.at[k], row=other_c)

    def mask_body(k, carry):
        g_copy(k).wait_recv()
        rows = rows_of(k, GC)
        seen = jnp.concatenate([feats[k * (GC // KC) + i, mine, :] for i in range(GC // KC)], axis=1).T
        v = (gacc[c, rows, :] + g_recv[rows, :]) * scale
        gt[c, rows, :] = jnp.where(seen.astype(jnp.float32) > 0, v, 0.0).astype(BF)
        q_copy(k).start()
        return carry

    lax.fori_loop(0, F // GC, mask_body, 0)
    rb[x, c] = rc[c]

    theirs = pl.ds(pl.multiple_of(other_c * T2, T2), T2)
    remote(pre.at[:, theirs], pre_recv, p_s, p_r.at[0], row=other_c).wait_send()
    all_f.wait_send()
    m_copy.wait_send()

    def x_all(dz, k):
        return remote(xsend.at[k], xg.at[z, c], x_s.at[dz, k], x_r.at[dz, k, 0], feat=far(dz), row=other_c)

    for dz, k in x_list:
        unless_ends(dz, lambda: x_all(dz, k).wait_send())

    def y_all(k, to, at):
        cc = c if k == 0 else other_c
        return remote(xg.at[back(2), cc], xg.at[back(2), cc], y_s.at[k], x_r.at[at, k, 0], feat=far(to))

    for k in range(2):
        relays(lambda to, at: y_all(k, to, at).wait_send())

    def sent(src, sem, **where):
        remote(src, src, sem, a_r.at[0, 0], **where).wait_send()

    for k in range(n):
        @pl.when(z == k)
        def _():
            if k < n - 1:
                sent(osend.at[:, pl.ds(k + 1, n - 1 - k)], rs_s.at[0], feat=k + 1)
                sent(e.at[:, 0, pl.ds(0, k + 1)], a_s.at[0], feat=k + 1)
            if k > 0:
                sent(osend.at[:, pl.ds(0, k)], rs_s.at[1], feat=k - 1)
                sent(e.at[:, 0, pl.ds(k, n - k)], a_s.at[1], feat=k - 1)

    pl.when(x == 0)(lambda: sent(nsend, n_s, layer=other_x))
    pl.when(x == 1)(lambda: sent(e.at[:, 0], t_s, layer=other_x))
    for k in range(1, 4):
        b_copy(k, None).wait_recv()
    for h in range(2):
        for j in range(J):
            lo = h * H + j * NC
            parts[:, lo:lo + NC] = rb[:, h, j].reshape(2 * R, NC)
    for k in range(1, 4):
        b_copy(k, None).wait_send()

    def last_body(k, carry):
        q_copy(k).wait_recv()
        return carry

    lax.fori_loop(0, F // GC, last_body, 0)
    sent(gacc.at[other_c], g_s, row=other_c)
    sent(gt.at[c], q_s, row=other_c)


def weight_kernel(dg, gt, xs, parts, enc_grad, dec_grad, bgrad, rebuilt, ebuf, bbuf, rbuf, dsem, esem, bsem, rsem):
    F, T2 = gt.shape[1:]
    H = xs.shape[1]
    R2 = parts.shape[0]
    nb = F // KC

    def rows_of(i, size):
        return pl.ds(pl.multiple_of(i * size, size), size)

    def d_copy(i):
        rows = rows_of(i, 2 * KC)
        return pltpu.make_async_copy(dg.at[rows], dec_grad.reshape(2 * F, H).at[rows], dsem.at[i])

    def e_copy(i):
        rows = rows_of(i, KC)
        return pltpu.make_async_copy(ebuf.at[rows], enc_grad.at[rows], esem.at[i])

    b_copy = pltpu.make_async_copy(bbuf, bgrad, bsem)
    r_copy = pltpu.make_async_copy(rbuf, rebuilt.reshape(R2, 2 * H), rsem)
    for i in range(nb):
        d_copy(i).start()
    i = lax.broadcasted_iota(jnp.int32, (R2, R2), 0)
    j = lax.broadcasted_iota(jnp.int32, (R2, R2), 1)
    inter = (j == (i % 2) * (R2 // 2) + i // 2).astype(BF)
    rbuf[...] = mm(inter, parts[...]).astype(BF)
    r_copy.start()
    ones = jnp.ones((8, 2 * T2), BF)

    def block(i, carry):
        rows = rows_of(i, KC)
        g = jnp.concatenate([gt[0, rows, :], gt[1, rows, :]], axis=1)
        ebuf[rows, :] = mm(g, xs[...]).astype(BF)
        e_copy(i).start()
        bbuf[:, rows] = dot_last(ones, g)[0:1]
        return carry

    lax.fori_loop(0, nb, block, 0)
    b_copy.start()
    for i in range(nb):
        d_copy(i).wait()
        e_copy(i).wait()
    r_copy.wait()
    b_copy.wait()


def fused(resid_buf, shuffle, mlp_out, enc_weight, dec_weight, enc_bias, dec_bias):
    n = lax.axis_size("feat")
    R = resid_buf.shape[0]
    F, H = enc_weight.shape[1:]
    T = R * n * 2
    T2, CR = T // 2, 2 * R
    J = H // KC
    NC, nk = H // J, F // KC
    Q = halves_of(H)
    HX = H // Q
    f32 = jnp.float32
    vm = pl.BlockSpec(memory_space=pltpu.VMEM)
    hbm = pl.BlockSpec(memory_space=pl.ANY)
    dma = pltpu.SemaphoreType.DMA
    vmem = pltpu.VMEM
    shape = jax.ShapeDtypeStruct
    outs = ((2 * F, H), (T, H), (2, F, T2), (2 * R, 2 * H))
    held = sum(2 * math.prod(a) for a in outs)
    dg, xs, gt, parts = pl.pallas_call(
        functools.partial(step_kernel, n, J),
        out_shape=tuple(vmem(a, BF) for a in outs),
        in_specs=[vm, vm, vm, hbm, hbm, vm, vm],
        out_specs=(vm,) * 4,
        scratch_shapes=[
            vmem((2 * F, 2 * T), BF), vmem((J, 2, n, CR, NC), BF), vmem((F, H), BF), vmem((4, 2 * DC, H), BF),
            vmem((2, Q, R, HX), BF), vmem((n, 2, Q, R, HX), BF),
            vmem((2, R, H), BF), vmem((R, H), BF), vmem((1, H), f32),
            vmem((nk, T, KC), f32), vmem((nk, T2, KC), f32), vmem((nk, T, KC), BF),
            vmem((J, T, NC), BF), vmem((J, T, NC), BF), vmem((J, n, CR, NC), f32),
            vmem((J, n, CR, NC), BF), vmem((J, n, CR, NC), BF), vmem((J, n, CR, NC), BF),
            vmem((2, J, R, NC), BF), vmem((2, 2, J, R, NC), BF),
            vmem((2, F, T2), f32), vmem((F, T2), f32),
            dma, dma((4,)), dma((n, 2)), dma((n, 2, Q)), dma((2,)), dma, dma,
            dma, dma((nk,)), dma, dma, dma, dma((J,)),
            dma((2,)), dma((J, 2, 2)), dma((2,)), dma((J, n)), dma, dma((J,)),
            dma((4,)), dma((4,)), dma, dma((F // GC,)), dma, dma((F // GC,)),
        ],
        compiler_params=pltpu.CompilerParams(
            collective_id=0, has_side_effects=True, vmem_limit_bytes=VMEM_LIMIT - held),
    )(resid_buf, shuffle.reshape(1, T), mlp_out, enc_weight[0], dec_weight[0], enc_bias, dec_bias)
    enc_grad, dec_grad, bgrad, rebuilt = pl.pallas_call(
        weight_kernel,
        out_shape=(
            shape((F, H), BF), shape((F, 2, H), BF), shape((1, F), f32), shape((R, 2, 2 * H), BF)),
        in_specs=[vm] * 4,
        out_specs=(hbm,) * 4,
        scratch_shapes=[
            vmem((F, H), BF), vmem((1, F), f32), vmem((2 * R, 2 * H), BF), dma((nk,)), dma((nk,)), dma, dma],
        compiler_params=pltpu.CompilerParams(vmem_limit_bytes=VMEM_LIMIT // 3),
    )(dg, gt, xs, parts)
    return rebuilt, enc_grad[None], dec_grad[None], bgrad


def chosen(resid_buf, shuffle, mlp_out, enc_weight, dec_weight, enc_bias, dec_bias):
    args = (resid_buf, shuffle, mlp_out, enc_weight, dec_weight, enc_bias, dec_bias)
    rows, width = resid_buf.shape[0], enc_weight.shape[2]
    fits = (
        lax.axis_size("layer") == LAYERS == 2 and lax.axis_size("row") == 2
        and lax.axis_size("feat") == 4 and rows % 16 == 0
        and width % KC == 0 and width // KC >= 3 and enc_weight.shape[1] % GC == 0)
    return fused(*args) if fits else on_device(*args)


def solution(mesh):
    return jax.shard_map(
        chosen,
        mesh=mesh,
        in_specs=(
            P(("groups", "feat", "row"), None, None),
            P("groups"),
            P(("groups", "feat", "row"), None, None),
            P("layer", "feat", "row"),
            P("layer", "feat", None, "row"),
            P("layer", "feat"),
            P(),
        ),
        out_specs=(
            P(("groups", "feat", "row"), None, None),
            P(("groups", "layer"), "feat", "row"),
            P(("groups", "layer"), "feat", None, "row"),
            P(("groups", "layer"), "feat"),
        ),
        check_vma=False,
    )
```

```python
import functools
import math

import jax
import jax.numpy as jnp
from jax import lax
from jax.experimental import pallas as pl
from jax.experimental.pallas import tpu as pltpu
from jax.sharding import PartitionSpec as P

LAYERS = 2


def from_behind(block, axis, distance):
    devices = range(lax.axis_size(axis))
    route = [(i - distance, i) for i in devices if i - distance in devices]
    return lax.ppermute(block, axis, route)


def dot_last(left, right):
    return lax.dot_general(
        left, right, (((1,), (1,)), ((), ())), preferred_element_type=jnp.float32
    )


def dot_first(left, right):
    return lax.dot_general(
        left, right, (((0,), (0,)), ((), ())), preferred_element_type=jnp.float32
    )


def on_device(resid_buf, shuffle, mlp_out, enc_weight, dec_weight, enc_bias, dec_bias):
    feat_count = lax.axis_size("feat")
    row_count = lax.axis_size("row")
    sub_blocks = lax.axis_size("layer") // LAYERS
    layer_pos = lax.axis_index("layer")
    row_pos = lax.axis_index("row")
    source = layer_pos // sub_blocks
    rows_each = resid_buf.shape[0]
    width = dec_bias.shape[1]
    half_width = enc_weight.shape[2]
    local_rows = rows_each * feat_count
    total_rows = local_rows * row_count
    loss_scale = float(total_rows) ** (-0.5)
    own_layer = lax.dynamic_index_in_dim(resid_buf, source, axis=1, keepdims=False)
    buffer_all = lax.all_gather(own_layer, ("feat", "row"), axis=0, tiled=True)
    batch_rows = jnp.take(buffer_all, shuffle, axis=0)
    blocks = batch_rows.reshape(feat_count, row_count, rows_each, width)
    inputs_half = lax.dynamic_slice_in_dim(
        jnp.swapaxes(blocks, 0, 1), row_pos * half_width, half_width, axis=3
    )
    inputs_half = inputs_half.reshape(total_rows, half_width)
    own_half_dec = dec_weight[0][:, 0]
    next_half_dec = dec_weight[0][:, 1]
    pre_all = lax.psum(dot_last(inputs_half, enc_weight[0]), "row") + enc_bias[0]
    features_all = jnp.maximum(pre_all, 0.0).astype(jnp.bfloat16)
    own_part = jnp.dot(features_all, own_half_dec, preferred_element_type=jnp.float32)
    next_part = jnp.dot(features_all, next_half_dec, preferred_element_type=jnp.float32)
    carried = from_behind(next_part, "layer", sub_blocks)
    spread = (own_part + carried).reshape(row_count, local_rows, half_width)
    halves = lax.psum_scatter(spread, "feat", scatter_dimension=1, tiled=True)
    joined = lax.all_to_all(halves, "row", split_axis=0, concat_axis=2, tiled=True)
    section_sum = joined.reshape(rows_each, width)
    target_ids = jnp.arange(LAYERS, dtype=jnp.int32)
    target_slots = jnp.where((target_ids == source)[:, None, None], section_sum[None], 0.0)
    totals = lax.psum(target_slots, "layer")
    recon_sum = jnp.swapaxes(totals, 0, 1) + dec_bias[None]
    errors = (recon_sum - mlp_out.astype(jnp.float32)).astype(jnp.bfloat16)
    gathered = lax.all_gather(errors, ("feat", "row"), axis=0, tiled=True)
    error_grid = gathered.reshape(feat_count, row_count, rows_each, LAYERS, width)
    errors_mine = lax.dynamic_index_in_dim(error_grid, row_pos, axis=1, keepdims=False)
    errors_mine = errors_mine.reshape(local_rows, LAYERS, width)
    errors_half = lax.dynamic_slice_in_dim(
        jnp.swapaxes(error_grid, 0, 1), row_pos * half_width, half_width, axis=4
    )
    errors_half = errors_half.reshape(total_rows, LAYERS, half_width)
    live_next = source + 1 < LAYERS
    next_index = jnp.minimum(source + 1, LAYERS - 1)
    half_own = lax.dynamic_index_in_dim(errors_half, source, axis=1, keepdims=False)
    half_next = lax.dynamic_index_in_dim(errors_half, next_index, axis=1, keepdims=False)
    half_next = jnp.where(live_next, half_next, jnp.zeros_like(half_next))
    half_terms = dot_last(half_own, own_half_dec) + dot_last(half_next, next_half_dec)
    grad_feats = lax.psum(half_terms, "row") * loss_scale
    grad_all = jnp.where(pre_all > 0, grad_feats, 0.0).astype(jnp.bfloat16)
    grad_own = loss_scale * dot_first(features_all, half_own)
    grad_next = loss_scale * dot_first(features_all, half_next)
    enc_grad = dot_first(grad_all, inputs_half).astype(jnp.bfloat16)
    dec_grad = jnp.stack([grad_own, grad_next], axis=1).astype(jnp.bfloat16)
    bias_grad = jnp.sum(grad_all.astype(jnp.float32), axis=0)
    return (recon_sum.astype(jnp.bfloat16), enc_grad[None], dec_grad[None], bias_grad[None])

KC = 256
DC = 128
GC = 2048
LC = 1024
LAG0 = 8
LATE = 3
LAG1 = 7
MESH = pl.DeviceIdType.MESH
VMEM_LIMIT = 67043328
BF = jnp.bfloat16


def pick(rows, cols, stride, offset):
    r = lax.broadcasted_iota(jnp.int32, (rows, cols), 0)
    c = lax.broadcasted_iota(jnp.int32, (rows, cols), 1)
    return (c == stride * r + offset).astype(BF)


def spread_to(offset):
    r = lax.broadcasted_iota(jnp.int32, (2 * DC, DC), 0)
    c = lax.broadcasted_iota(jnp.int32, (2 * DC, DC), 1)
    return (r == 2 * c + offset).astype(BF)


def mm(left, right):
    return jnp.dot(left, right, preferred_element_type=jnp.float32)


def halves_of(width):
    return next(q for q in (3, 2, 1) if width % (q * DC) == 0)


def step_kernel(
    n, J, res, shuf, mlp, enc, dec, bias, dbias,
    dg, xs, gt, parts,
    fx, e, enc_v, raw, xsend, xg, mlpx, msend, dsel, pre, pre_recv, feats,
    nsend, nrecv, facc, osend, rr, rl, rc, rb, gacc, g_send, g_recv,
    sem_l, sem_raw, x_s, x_r, y_s, m_s, m_r, p_s, p_r, f_s, f_r, n_s, n_r,
    rs_s, rs_r, a_s, a_r, t_s, t_r, b_s, b_r, g_s, g_r,
):
    z = lax.axis_index("feat")
    x = lax.axis_index("layer")
    c = lax.axis_index("row")
    Q, R, HX = xsend.shape[1:]
    F, H = enc_v.shape
    T = xs.shape[0]
    T2, CR, NC = T // 2, 2 * R, H // J
    nk, slots = F // KC, raw.shape[0]
    scale = float(T) ** (-0.5)
    other_c, other_x = 1 - c, 1 - x

    def far(dz):
        return lax.rem(z + dz, n)

    def back(dz):
        return lax.rem(z + n - dz, n)

    def remote(src, dst, send, recv, **where):
        return pltpu.make_async_remote_copy(
            src_ref=src, dst_ref=dst, send_sem=send, recv_sem=recv,
            device_id=where, device_id_type=MESH)

    def unless_ends(dz, act):
        if dz == n - 1:
            pl.when(z != 0)(act)
        elif dz == 1:
            pl.when(z != n - 1)(act)
        else:
            act()

    def relays(act):
        pl.when(z == 2)(lambda: act(1, 3))
        pl.when(z == 1)(lambda: act(3, 1))

    def raw_copy(i, slot):
        return pltpu.make_async_copy(
            dec.reshape(2 * F, H).at[pl.ds(pl.multiple_of(i * 2 * DC, 2 * DC), 2 * DC)], raw.at[slot], sem_raw.at[slot])

    nd = F // DC
    for i in range(slots - 1):
        raw_copy(i, i).start()
    enc_copy = pltpu.make_async_copy(enc, enc_v, sem_l)
    enc_copy.start()

    barrier = pltpu.get_barrier_semaphore()
    for dz in range(n):
        if dz:
            pl.semaphore_signal(barrier, inc=1, device_id={"feat": far(dz), "row": c}, device_id_type=MESH)
        pl.semaphore_signal(barrier, inc=1, device_id={"feat": far(dz), "row": other_c}, device_id_type=MESH)
    for cc in (c, other_c):
        pl.semaphore_signal(barrier, inc=1, device_id={"layer": other_x, "row": cc}, device_id_type=MESH)

    own_x = mm(pick(R, 2 * R, 2, x), res.reshape(2 * R, 2 * H)[...]).astype(BF)
    x_mine = jnp.where(c == 0, own_x[:, :H], own_x[:, H:])
    x_other = jnp.where(c == 0, own_x[:, H:], own_x[:, :H])
    for q in range(Q):
        xsend[0, q] = x_mine[:, q * HX:(q + 1) * HX]
        xsend[1, q] = x_other[:, q * HX:(q + 1) * HX]
        xg[z, c, q] = x_mine[:, q * HX:(q + 1) * HX]
    own_m = mm(pick(R, 2 * R, 2, x), mlp.reshape(2 * R, 2 * H)[...]).astype(BF)
    mlpx[c] = jnp.where(c == 0, own_m[:, :H], own_m[:, H:])
    msend[...] = jnp.where(c == 0, own_m[:, H:], own_m[:, :H])

    pl.semaphore_wait(barrier, 2 * n + 1)

    def x_copy(dz, k, q):
        return remote(xsend.at[k, q], xg.at[z, c, q], x_s.at[dz, k], x_r.at[dz, k, q],
                      feat=far(dz), row=c if k == 0 else other_c)

    x_list = [(dz, k) for dz in (2, 1, 3) for k in range(2)] + [(0, 1)]
    for q in range(Q):
        for dz, k in x_list:
            unless_ends(dz, lambda: x_copy(dz, k, q).start())

    def y_copy(k, q, to, at):
        cc = c if k == 0 else other_c
        return remote(xg.at[back(2), cc, q], xg.at[back(2), cc, q], y_s.at[k], x_r.at[at, k, q], feat=far(to))

    m_copy = remote(msend, mlpx.at[c], m_s, m_r, row=other_c)
    m_copy.start()
    d_all = jnp.where(x == 0, dbias[0:1, :], dbias[1:2, :])
    dsel[...] = jnp.where(c == 0, d_all[:, :H], d_all[:, H:])

    apart = jnp.concatenate([pick(DC, 2 * DC, 2, 0), pick(DC, 2 * DC, 2, 1)], axis=0)

    def split_body(i, carry):
        slot = lax.rem(i, slots)

        @pl.when(i + slots - 1 < nd)
        def _():
            raw_copy(i + slots - 1, lax.rem(i + slots - 1, slots)).start()

        raw_copy(i, slot).wait()
        both = mm(apart, raw[slot]).astype(BF)
        rows = pl.ds(pl.multiple_of(i * DC, DC), DC)
        dg[rows, :] = both[:DC]
        dg[pl.ds(pl.multiple_of(F + i * DC, DC), DC), :] = both[DC:]
        return carry

    def pass_on(q):
        for k in range(2):
            x_copy(2, k, q).wait_recv()
            relays(lambda to, at: y_copy(k, q, to, at).start())

    perm = (lax.broadcasted_iota(jnp.int32, (T, T), 0) == shuf[...]).astype(BF)

    def p_copy(k):
        return remote(pre.at[k, pl.ds(pl.multiple_of(other_c * T2, T2), T2)], pre_recv.at[k], p_s, p_r.at[k], row=other_c)

    mine = pl.ds(pl.multiple_of(c * T2, T2), T2)

    def f_copy(k):
        return remote(feats.at[k, mine], feats.at[k, mine], f_s, f_r, row=other_c)

    lax.fori_loop(0, nd // 2, split_body, 0)
    pass_on(0)
    lax.fori_loop(nd // 2, nd, split_body, 0)
    enc_copy.wait()
    per = 2 if nk % 2 == 0 else 1
    for q in range(Q):
        if q:
            pass_on(q)
        for dz, k in x_list:
            if dz != 2:
                x_copy(dz, k, q).wait_recv()
        lo = q * HX
        xs[:, lo:lo + HX] = dot_first(perm, xg[:, :, q].reshape(T, HX)).astype(BF)

        def pre_body(i, carry):
            rows = pl.ds(pl.multiple_of(i * per * KC, KC), per * KC)
            v = dot_last(xs[:, lo:lo + HX], enc_v[rows, lo:lo + HX])
            for h in range(per):
                part = v[:, h * KC:(h + 1) * KC]
                k = i * per + h
                pre[k] = part if q == 0 else pre[k] + part
                if q == Q - 1:
                    p_copy(k).start()
            return carry

        lax.fori_loop(0, nk // per, pre_body, 0)

    def feat_body(k, carry):
        p_copy(k).wait_recv()
        cols = pl.ds(pl.multiple_of(k * KC, KC), KC)
        v = pre[k, mine, :] + pre_recv[k] + bias[:, cols]
        feats[k, mine, :] = jnp.maximum(v, 0.0).astype(BF)
        f_copy(k).start()
        return carry

    lax.fori_loop(0, nk, feat_body, 0)

    def rows_of(k, size, base=0):
        return pl.ds(pl.multiple_of(base + k * size, KC), size)

    def zero_body(k, carry):
        gacc[:, rows_of(k, KC), :] = jnp.zeros((2, KC, T2), jnp.float32)
        return carry

    lax.fori_loop(0, nk, zero_body, 0)
    all_f = remote(feats.at[:, mine], feats.at[:, mine], f_s, f_r, row=other_c)
    all_f.wait_recv()
    m_copy.wait_recv()
    up0, up1 = spread_to(0), spread_to(1)

    def expand(b):
        rows = pl.ds(pl.multiple_of(b * 2 * DC, 2 * DC), 2 * DC)
        turned = feats[b // (KC // DC), :, pl.ds(pl.multiple_of(lax.rem(b, KC // DC) * DC, DC), DC)].T
        fx[rows, :T] = mm(up0, turned).astype(BF)

        @pl.when(x == 0)
        def _():
            fx[rows, T:] = mm(up1, turned).astype(BF)

    def n_copy(j):
        return remote(nsend.at[j], nrecv.at[j], n_s, n_r.at[j], layer=other_x)

    def right_copy(j, k, onward):
        some = pl.ds(k + 2, n - 2 - k) if onward else pl.ds(k + 1, 1)
        return remote(osend.at[j, some], rr.at[j, some], rs_s.at[0], rs_r.at[j, 0, onward], feat=k + 1)

    def left_copy(j, k, onward):
        some = pl.ds(0, k - 1) if onward else pl.ds(k - 1, 1)
        return remote(osend.at[j, some], rl.at[j, some], rs_s.at[1], rs_r.at[j, 1, onward], feat=k - 1)

    def send_right(j, k):
        for lo, hi, onward in ((k + 2, n, 1), (k + 1, k + 2, 0)):
            if lo < hi:
                v = facc[j, lo:hi]
                if k > 0:
                    v = v + rr[j, lo:hi].astype(jnp.float32)
                osend[j, lo:hi] = v.astype(BF)
                right_copy(j, k, onward).start()

    def send_left(j, k):
        for lo, hi, onward in ((0, k - 1, 1), (k - 1, k, 0)):
            if lo < hi:
                v = facc[j, lo:hi]
                if k < n - 1:
                    v = v + rl[j, lo:hi].astype(jnp.float32)
                osend[j, lo:hi] = v.astype(BF)
                left_copy(j, k, onward).start()

    def wide(j):
        return pl.ds(pl.multiple_of(j * NC, NC), NC)

    def all_feats():
        return jnp.concatenate([feats[k] for k in range(nk)], axis=1)

    def send_next(j):
        @pl.when(x == 0)
        def _():
            nsend[j] = mm(all_feats(), dg[pl.ds(F, F), wide(j)]).astype(BF)
            n_copy(j).start()

    def front(j):
        for i in range(2):
            pl.when(2 * j + i < J)(functools.partial(send_next, 2 * j + i))
        facc[j] = mm(all_feats(), dg[pl.ds(0, F), wide(j)]).reshape(n, CR, NC)

        @pl.when(x == 1)
        def _():
            n_copy(j).wait_recv()
            facc[j] = facc[j] + nrecv[j].astype(jnp.float32).reshape(n, CR, NC)

        pl.when(z == 0)(lambda: send_right(j, 0))
        pl.when(z == n - 1)(lambda: send_left(j, n - 1))

    def go_right(j, k):
        right_copy(j, k - 1, 1).wait_recv()
        send_right(j, k)

    def go_left(j, k):
        left_copy(j, k + 1, 1).wait_recv()
        send_left(j, k)

    def relay_near(j):
        pl.when(z == 1)(lambda: go_right(j, 1))
        pl.when(z == 2)(lambda: go_left(j, 2))

    def relay_far(j):
        pl.when(z == 2)(lambda: go_right(j, 2))
        pl.when(z == 1)(lambda: go_left(j, 1))

    def a_copy(j, b, way):
        to = jnp.minimum(z + 1, n - 1) if way == 0 else jnp.maximum(z - 1, 0)
        return remote(e.at[j, 0, b], e.at[j, 0, b], a_s.at[way], a_r.at[j, b], feat=to)

    def t_copy(j, b):
        return remote(e.at[j, 0, b], e.at[j, 1, b], t_s, t_r.at[j], layer=other_x)

    def final(j):
        for k in range(n):
            @pl.when(z == k)
            def _():
                if k > 0:
                    right_copy(j, k - 1, 0).wait_recv()
                if k < n - 1:
                    left_copy(j, k + 1, 0).wait_recv()

        @pl.when(z > 0)
        def _():
            facc[j, z] = facc[j, z] + rr[j, z].astype(jnp.float32)

        @pl.when(z < n - 1)
        def _():
            facc[j, z] = facc[j, z] + rl[j, z].astype(jnp.float32)

        total = facc[j, z] + dsel[:, wide(j)]
        e[j, 0, z] = (total - mlpx[:, :, wide(j)].reshape(CR, NC).astype(jnp.float32)).astype(BF)
        pl.when(z < n - 1)(lambda: a_copy(j, z, 0).start())
        pl.when(z > 0)(lambda: a_copy(j, z, 1).start())
        pl.when(x == 1)(lambda: t_copy(j, z).start())
        kept = total.astype(BF).reshape(2, R, NC)
        rc[0, j] = kept[0]
        rc[1, j] = kept[1]

    def hop(j, h):
        @pl.when(z >= h)
        def _():
            a_copy(j, z - h, 0).wait_recv()
            pl.when(z < n - 1)(lambda: a_copy(j, z - h, 0).start())
            pl.when(x == 1)(lambda: t_copy(j, z - h).start())

        @pl.when(z + h < n)
        def _():
            a_copy(j, z + h, 1).wait_recv()
            pl.when(z > 0)(lambda: a_copy(j, z + h, 1).start())
            pl.when(x == 1)(lambda: t_copy(j, z + h).start())

    def g_copy(k):
        rows = rows_of(k, GC)
        return remote(g_send.at[:, rows], g_recv.at[:, rows], g_s, g_r.at[k], row=other_c)

    def send_grads(k):
        rows = rows_of(k, GC)
        g_send[:, rows, :] = gacc[:, rows, :].astype(BF)
        g_copy(k).start()

    def grads(j):
        last = j == J - 1

        def body(k, carry):
            rows = rows_of(k, GC)
            v = dot_last(dg[rows, wide(j)], e[j, 0].reshape(T, NC))
            gacc[0, rows, :] = gacc[0, rows, :] + v[:, :T2]
            gacc[1, rows, :] = gacc[1, rows, :] + v[:, T2:]
            pl.when(last)(lambda: send_grads(k))
            return carry

        lax.fori_loop(0, F // GC, body, 0)

    def both_grads(j):
        last = j == J - 1
        remote(e.at[j, 0], e.at[j, 1], t_s, t_r.at[j], layer=other_x).wait_recv()

        def body(k, carry):
            rows, below = rows_of(k, GC), rows_of(k, GC, F)
            v = dot_last(dg[rows, wide(j)], e[j, 0].reshape(T, NC)) + dot_last(dg[below, wide(j)], e[j, 1].reshape(T, NC))
            gacc[0, rows, :] = gacc[0, rows, :] + v[:, :T2]
            gacc[1, rows, :] = gacc[1, rows, :] + v[:, T2:]
            pl.when(last)(lambda: send_grads(k))
            return carry

        lax.fori_loop(0, F // GC, body, 0)

    def weights(j):
        def body(k, carry):
            rows = rows_of(k, 2 * GC)
            dg[rows, wide(j)] = (scale * mm(fx[rows, :T], e[j, 0].reshape(T, NC))).astype(BF)
            return carry

        lax.fori_loop(0, F // GC, body, 0)

    def both_weights(j):
        def body(k, carry):
            rows = rows_of(k, 2 * GC)
            dg[rows, wide(j)] = (scale * mm(fx[rows, :], e[j].reshape(2 * T, NC))).astype(BF)
            return carry

        lax.fori_loop(0, F // GC, body, 0)

    cuts = (0, J // 3, 2 * J // 3, J)

    def b_copy(k, p):
        dx, dc = k // 2, k % 2
        to_x = other_x if dx else x
        to_c = other_c if dc else c
        some = pl.ds(0, J) if p is None else pl.ds(cuts[p], cuts[p + 1] - cuts[p])
        return remote(rc.at[to_c, some], rb.at[x, c, some], b_s.at[k], b_r.at[k], layer=to_x, row=to_c)

    def start_b(p):
        for k in range(1, 4):
            b_copy(k, p).start()

    def early_b(j):
        for p in range(2):
            pl.when(j == cuts[p + 1] - 1)(functools.partial(start_b, p))

    def late_b(j):
        pl.when(j == J - 1)(lambda: start_b(2))

    stages = (
        (0, None, front), (1, None, relay_near), (2, None, relay_far), (3, None, final), (3, None, early_b),
        (4, None, lambda j: hop(j, 1)), (5, None, lambda j: hop(j, 2)), (6, None, lambda j: hop(j, 3)), (6, None, late_b),
        (LAG1, 1, grads), (LAG1 + 1, 1, weights), (LAG0, 0, both_grads), (LAG0, 0, both_weights))
    steps = J + max(LAG0, LAG1)
    share = pl.cdiv(nd, LAG0)

    def pipe(s, carry):
        for lag, side, act in stages:
            end = J - LATE if act in (weights, both_weights) else J
            live = jnp.logical_and(s >= lag, s < end + lag)
            if side is not None:
                live = jnp.logical_and(live, x == side)
            pl.when(live)(functools.partial(act, s - lag))
        for i in range(share):
            pl.when(jnp.logical_and(x == 0, s * share + i < nd))(functools.partial(expand, s * share + i))
        return carry

    @pl.when(x == 1)
    def _():
        def body(b, carry):
            expand(b)
            return carry

        lax.fori_loop(0, nd, body, 0)

    lax.fori_loop(0, steps, pipe, 0)

    spent = (J - LATE) * NC

    def keep_fx(k, carry):
        rows = rows_of(k, GC)
        dg[rows, spent:spent + T] = fx[rows, :T]

        @pl.when(x == 0)
        def _():
            dg[rows, spent + T:spent + 2 * T] = fx[rows, T:]

        return carry

    lax.fori_loop(0, 2 * F // GC, keep_fx, 0)
    for h in range(LATE):
        dg[2 * h * T:(2 * h + 1) * T, spent + 2 * T:spent + 2 * T + NC] = e[J - LATE + h, 0].reshape(T, NC)

        @pl.when(x == 0)
        def _():
            dg[(2 * h + 1) * T:(2 * h + 2) * T, spent + 2 * T:spent + 2 * T + NC] = e[J - LATE + h, 1].reshape(T, NC)

    def mask_body(k, carry):
        g_copy(k).wait_recv()
        rows = rows_of(k, GC)
        for h in range(2):
            seen = jnp.concatenate(
                [feats[k * (GC // KC) + i, h * T2:(h + 1) * T2, :] for i in range(GC // KC)], axis=1).T
            v = (g_send[h, rows, :].astype(jnp.float32) + g_recv[h, rows, :].astype(jnp.float32)) * scale
            gt[h, rows, :] = jnp.where(seen.astype(jnp.float32) > 0, v, 0.0).astype(BF)
        return carry

    lax.fori_loop(0, F // GC, mask_body, 0)
    rb[x, c] = rc[c]
    theirs = pl.ds(pl.multiple_of(other_c * T2, T2), T2)
    remote(pre.at[:, theirs], pre_recv, p_s, p_r.at[0], row=other_c).wait_send()
    all_f.wait_send()
    m_copy.wait_send()

    def x_all(dz, k):
        return remote(xsend.at[k], xg.at[z, c], x_s.at[dz, k], x_r.at[dz, k, 0], feat=far(dz), row=other_c)

    for dz, k in x_list:
        unless_ends(dz, lambda: x_all(dz, k).wait_send())

    def y_all(k, to, at):
        cc = c if k == 0 else other_c
        return remote(xg.at[back(2), cc], xg.at[back(2), cc], y_s.at[k], x_r.at[at, k, 0], feat=far(to))

    for k in range(2):
        relays(lambda to, at: y_all(k, to, at).wait_send())

    def sent(src, sem, **where):
        remote(src, src, sem, a_r.at[0, 0], **where).wait_send()

    for k in range(n):
        @pl.when(z == k)
        def _():
            if k < n - 1:
                sent(osend.at[:, pl.ds(k + 1, n - 1 - k)], rs_s.at[0], feat=k + 1)
                sent(e.at[:, 0, pl.ds(0, k + 1)], a_s.at[0], feat=k + 1)
            if k > 0:
                sent(osend.at[:, pl.ds(0, k)], rs_s.at[1], feat=k - 1)
                sent(e.at[:, 0, pl.ds(k, n - k)], a_s.at[1], feat=k - 1)

    pl.when(x == 0)(lambda: sent(nsend, n_s, layer=other_x))
    pl.when(x == 1)(lambda: sent(e.at[:, 0], t_s, layer=other_x))
    for k in range(1, 4):
        b_copy(k, None).wait_recv()
    for h in range(2):
        for j in range(J):
            lo = h * H + j * NC
            parts[:, lo:lo + NC] = rb[:, h, j].reshape(2 * R, NC)
    for k in range(1, 4):
        b_copy(k, None).wait_send()

    sent(g_send, g_s, row=other_c)


def weight_kernel(
    dg, gt, xs, parts, enc_grad, dec_grad, bgrad, rebuilt,
    late, ebuf, bbuf, rbuf, dsem, lsem, esem, bsem, rsem,
):
    F, T2 = gt.shape[1:]
    T, H = xs.shape
    NC = KC
    R2 = parts.shape[0]
    nb, nl = F // KC, F // LC
    x = lax.axis_index("layer")
    scale = float(T) ** (-0.5)
    done = H - LATE * NC

    def rows_of(i, size):
        return pl.ds(pl.multiple_of(i * size, size), size)

    def d_copy(i):
        rows = rows_of(i, 2 * KC)
        return pltpu.make_async_copy(
            dg.at[rows, pl.ds(0, done)], dec_grad.reshape(2 * F, H).at[rows, pl.ds(0, done)], dsem.at[i])

    def l_copy(i):
        rows = rows_of(i, 2 * LC)
        return pltpu.make_async_copy(
            late.at[rows], dec_grad.reshape(2 * F, H).at[rows, pl.ds(done, LATE * NC)], lsem.at[i])

    def e_copy(i):
        slot = lax.rem(i, 4)
        return pltpu.make_async_copy(ebuf.at[slot], enc_grad.at[rows_of(i, KC)], esem.at[slot])

    b_copy = pltpu.make_async_copy(bbuf, bgrad, bsem)
    r_copy = pltpu.make_async_copy(rbuf, rebuilt.reshape(R2, 2 * H), rsem)
    for i in range(nb):
        d_copy(i).start()

    def late_block(i, carry):
        rows = rows_of(i, 2 * LC)

        def chunk(h, inner):
            cols = rows_of(h, NC)

            @pl.when(x == 0)
            def _():
                late[rows, cols] = (scale * mm(dg[rows, done:done + 2 * T], dg[rows_of(h, 2 * T), done + 2 * T:done + 2 * T + NC])).astype(BF)

            @pl.when(x == 1)
            def _():
                late[rows, cols] = (scale * mm(dg[rows, done:done + T], dg[pl.ds(pl.multiple_of(2 * h * T, T), T), done + 2 * T:done + 2 * T + NC])).astype(BF)

            return inner

        lax.fori_loop(0, LATE, chunk, 0)
        l_copy(i).start()
        return carry

    ones = jnp.ones((8, 2 * T2), BF)

    def block(i, carry):
        rows = rows_of(i, KC)
        g = jnp.concatenate([gt[0, rows, :], gt[1, rows, :]], axis=1)
        pl.when(i >= 4)(lambda: e_copy(i - 4).wait())
        ebuf[lax.rem(i, 4)] = mm(g, xs[...]).astype(BF)
        e_copy(i).start()
        bbuf[:, rows] = dot_last(ones, g)[0:1]
        return carry

    lax.fori_loop(0, nl, late_block, 0)
    i = lax.broadcasted_iota(jnp.int32, (R2, R2), 0)
    j = lax.broadcasted_iota(jnp.int32, (R2, R2), 1)
    inter = (j == (i % 2) * (R2 // 2) + i // 2).astype(BF)
    rbuf[...] = mm(inter, parts[...]).astype(BF)
    r_copy.start()
    lax.fori_loop(0, nb, block, 0)
    b_copy.start()
    for i in range(nb):
        d_copy(i).wait()
    for i in range(max(nb - 4, 0), nb):
        e_copy(i).wait()
    for i in range(nl):
        l_copy(i).wait()
    r_copy.wait()
    b_copy.wait()


def fused(resid_buf, shuffle, mlp_out, enc_weight, dec_weight, enc_bias, dec_bias):
    n = lax.axis_size("feat")
    R = resid_buf.shape[0]
    F, H = enc_weight.shape[1:]
    T = R * n * 2
    T2, CR = T // 2, 2 * R
    J = H // KC
    NC, nk = H // J, F // KC
    Q = halves_of(H)
    HX = H // Q
    f32 = jnp.float32
    vm = pl.BlockSpec(memory_space=pltpu.VMEM)
    hbm = pl.BlockSpec(memory_space=pl.ANY)
    dma = pltpu.SemaphoreType.DMA
    vmem = pltpu.VMEM
    shape = jax.ShapeDtypeStruct
    outs = ((2 * F, H), (T, H), (2, F, T2), (2 * R, 2 * H))
    held = sum(2 * math.prod(a) for a in outs)
    dg, xs, gt, parts = pl.pallas_call(
        functools.partial(step_kernel, n, J),
        out_shape=tuple(vmem(a, BF) for a in outs),
        in_specs=[vm, vm, vm, hbm, hbm, vm, vm],
        out_specs=(vm,) * 4,
        scratch_shapes=[
            vmem((2 * F, 2 * T), BF), vmem((J, 2, n, CR, NC), BF), vmem((F, H), BF), vmem((3, 2 * DC, H), BF),
            vmem((2, Q, R, HX), BF), vmem((n, 2, Q, R, HX), BF),
            vmem((2, R, H), BF), vmem((R, H), BF), vmem((1, H), f32),
            vmem((nk, T, KC), f32), vmem((nk, T2, KC), f32), vmem((nk, T, KC), BF),
            vmem((J, T, NC), BF), vmem((J, T, NC), BF), vmem((J, n, CR, NC), f32),
            vmem((J, n, CR, NC), BF), vmem((J, n, CR, NC), BF), vmem((J, n, CR, NC), BF),
            vmem((2, J, R, NC), BF), vmem((2, 2, J, R, NC), BF),
            vmem((2, F, T2), f32), vmem((2, F, T2), BF), vmem((2, F, T2), BF),
            dma, dma((4,)), dma((n, 2)), dma((n, 2, Q)), dma((2,)), dma, dma,
            dma, dma((nk,)), dma, dma, dma, dma((J,)),
            dma((2,)), dma((J, 2, 2)), dma((2,)), dma((J, n)), dma, dma((J,)),
            dma((4,)), dma((4,)), dma, dma((F // GC,)),
        ],
        compiler_params=pltpu.CompilerParams(
            collective_id=0, has_side_effects=True, vmem_limit_bytes=VMEM_LIMIT - held),
    )(resid_buf, shuffle.reshape(1, T), mlp_out, enc_weight[0], dec_weight[0], enc_bias, dec_bias)
    enc_grad, dec_grad, bgrad, rebuilt = pl.pallas_call(
        weight_kernel,
        out_shape=(
            shape((F, H), BF), shape((F, 2, H), BF), shape((1, F), f32), shape((R, 2, 2 * H), BF)),
        in_specs=[vm] * 4,
        out_specs=(hbm,) * 4,
        scratch_shapes=[
            vmem((2 * F, LATE * NC), BF), vmem((4, KC, H), BF), vmem((1, F), f32), vmem((2 * R, 2 * H), BF),
            dma((nk,)), dma((F // LC,)), dma((4,)), dma, dma],
        compiler_params=pltpu.CompilerParams(vmem_limit_bytes=VMEM_LIMIT // 4),
    )(dg, gt, xs, parts)
    return rebuilt, enc_grad[None], dec_grad[None], bgrad


def chosen(resid_buf, shuffle, mlp_out, enc_weight, dec_weight, enc_bias, dec_bias):
    args = (resid_buf, shuffle, mlp_out, enc_weight, dec_weight, enc_bias, dec_bias)
    rows, width = resid_buf.shape[0], enc_weight.shape[2]
    fits = (
        lax.axis_size("layer") == LAYERS == 2 and lax.axis_size("row") == 2
        and lax.axis_size("feat") == 4 and rows % 16 == 0
        and width % KC == 0 and width // KC > LATE
        and rows * 2 * lax.axis_size("feat") == KC and enc_weight.shape[1] % GC == 0)
    return fused(*args) if fits else on_device(*args)


def solution(mesh):
    return jax.shard_map(
        chosen,
        mesh=mesh,
        in_specs=(
            P(("groups", "feat", "row"), None, None),
            P("groups"),
            P(("groups", "feat", "row"), None, None),
            P("layer", "feat", "row"),
            P("layer", "feat", None, "row"),
            P("layer", "feat"),
            P(),
        ),
        out_specs=(
            P(("groups", "feat", "row"), None, None),
            P(("groups", "layer"), "feat", "row"),
            P(("groups", "layer"), "feat", None, "row"),
            P(("groups", "layer"), "feat"),
        ),
        check_vma=False,
    )
```

```python
import functools
import math

import jax
import jax.numpy as jnp
from jax import lax
from jax.experimental import pallas as pl
from jax.experimental.pallas import tpu as pltpu
from jax.sharding import PartitionSpec as P

LAYERS = 2


def from_behind(block, axis, distance):
    devices = range(lax.axis_size(axis))
    route = [(i - distance, i) for i in devices if i - distance in devices]
    return lax.ppermute(block, axis, route)


def dot_last(left, right):
    return lax.dot_general(
        left, right, (((1,), (1,)), ((), ())), preferred_element_type=jnp.float32
    )


def dot_first(left, right):
    return lax.dot_general(
        left, right, (((0,), (0,)), ((), ())), preferred_element_type=jnp.float32
    )


def on_device(resid_buf, shuffle, mlp_out, enc_weight, dec_weight, enc_bias, dec_bias):
    feat_count = lax.axis_size("feat")
    row_count = lax.axis_size("row")
    sub_blocks = lax.axis_size("layer") // LAYERS
    layer_pos = lax.axis_index("layer")
    row_pos = lax.axis_index("row")
    source = layer_pos // sub_blocks
    rows_each = resid_buf.shape[0]
    width = dec_bias.shape[1]
    half_width = enc_weight.shape[2]
    local_rows = rows_each * feat_count
    total_rows = local_rows * row_count
    loss_scale = float(total_rows) ** (-0.5)
    own_layer = lax.dynamic_index_in_dim(resid_buf, source, axis=1, keepdims=False)
    buffer_all = lax.all_gather(own_layer, ("feat", "row"), axis=0, tiled=True)
    batch_rows = jnp.take(buffer_all, shuffle, axis=0)
    blocks = batch_rows.reshape(feat_count, row_count, rows_each, width)
    inputs_half = lax.dynamic_slice_in_dim(
        jnp.swapaxes(blocks, 0, 1), row_pos * half_width, half_width, axis=3
    )
    inputs_half = inputs_half.reshape(total_rows, half_width)
    own_half_dec = dec_weight[0][:, 0]
    next_half_dec = dec_weight[0][:, 1]
    pre_all = lax.psum(dot_last(inputs_half, enc_weight[0]), "row") + enc_bias[0]
    features_all = jnp.maximum(pre_all, 0.0).astype(jnp.bfloat16)
    own_part = jnp.dot(features_all, own_half_dec, preferred_element_type=jnp.float32)
    next_part = jnp.dot(features_all, next_half_dec, preferred_element_type=jnp.float32)
    carried = from_behind(next_part, "layer", sub_blocks)
    spread = (own_part + carried).reshape(row_count, local_rows, half_width)
    halves = lax.psum_scatter(spread, "feat", scatter_dimension=1, tiled=True)
    joined = lax.all_to_all(halves, "row", split_axis=0, concat_axis=2, tiled=True)
    section_sum = joined.reshape(rows_each, width)
    target_ids = jnp.arange(LAYERS, dtype=jnp.int32)
    target_slots = jnp.where((target_ids == source)[:, None, None], section_sum[None], 0.0)
    totals = lax.psum(target_slots, "layer")
    recon_sum = jnp.swapaxes(totals, 0, 1) + dec_bias[None]
    errors = (recon_sum - mlp_out.astype(jnp.float32)).astype(jnp.bfloat16)
    gathered = lax.all_gather(errors, ("feat", "row"), axis=0, tiled=True)
    error_grid = gathered.reshape(feat_count, row_count, rows_each, LAYERS, width)
    errors_mine = lax.dynamic_index_in_dim(error_grid, row_pos, axis=1, keepdims=False)
    errors_mine = errors_mine.reshape(local_rows, LAYERS, width)
    errors_half = lax.dynamic_slice_in_dim(
        jnp.swapaxes(error_grid, 0, 1), row_pos * half_width, half_width, axis=4
    )
    errors_half = errors_half.reshape(total_rows, LAYERS, half_width)
    live_next = source + 1 < LAYERS
    next_index = jnp.minimum(source + 1, LAYERS - 1)
    half_own = lax.dynamic_index_in_dim(errors_half, source, axis=1, keepdims=False)
    half_next = lax.dynamic_index_in_dim(errors_half, next_index, axis=1, keepdims=False)
    half_next = jnp.where(live_next, half_next, jnp.zeros_like(half_next))
    half_terms = dot_last(half_own, own_half_dec) + dot_last(half_next, next_half_dec)
    grad_feats = lax.psum(half_terms, "row") * loss_scale
    grad_all = jnp.where(pre_all > 0, grad_feats, 0.0).astype(jnp.bfloat16)
    grad_own = loss_scale * dot_first(features_all, half_own)
    grad_next = loss_scale * dot_first(features_all, half_next)
    enc_grad = dot_first(grad_all, inputs_half).astype(jnp.bfloat16)
    dec_grad = jnp.stack([grad_own, grad_next], axis=1).astype(jnp.bfloat16)
    bias_grad = jnp.sum(grad_all.astype(jnp.float32), axis=0)
    return (recon_sum.astype(jnp.bfloat16), enc_grad[None], dec_grad[None], bias_grad[None])

KC = 256
DC = 128
GC = 2048
LC = 1024
GB = 512
LAG0 = 8
LATE = 3
LAG1 = 7
MESH = pl.DeviceIdType.MESH
VMEM_LIMIT = 67043328
BF = jnp.bfloat16


def pick(rows, cols, stride, offset):
    r = lax.broadcasted_iota(jnp.int32, (rows, cols), 0)
    c = lax.broadcasted_iota(jnp.int32, (rows, cols), 1)
    return (c == stride * r + offset).astype(BF)


def spread_to(offset):
    r = lax.broadcasted_iota(jnp.int32, (2 * DC, DC), 0)
    c = lax.broadcasted_iota(jnp.int32, (2 * DC, DC), 1)
    return (r == 2 * c + offset).astype(BF)


def mm(left, right):
    return jnp.dot(left, right, preferred_element_type=jnp.float32)


def halves_of(width):
    return next(q for q in (3, 2, 1) if width % (q * DC) == 0)


def step_kernel(
    n, J, res, shuf, mlp, enc, dec, bias, dbias,
    dg, xs, gt, rb,
    fx, e, enc_v, raw, xsend, xg, mlpx, msend, dsel, pre, pre_recv, feats,
    nsend, nrecv, facc, osend, rr, rl, rc, gacc, g_send, g_recv,
    sem_l, sem_raw, x_s, x_r, y_s, m_s, m_r, p_s, p_r, f_s, f_r, n_s, n_r,
    rs_s, rs_r, a_s, a_r, t_s, t_r, b_s, b_r, g_s, g_r,
):
    z = lax.axis_index("feat")
    x = lax.axis_index("layer")
    c = lax.axis_index("row")
    Q, R, HX = xsend.shape[1:]
    F, H = enc_v.shape
    T = xs.shape[0]
    T2, CR, NC = T // 2, 2 * R, H // J
    nk, slots = F // KC, raw.shape[0]
    scale = float(T) ** (-0.5)
    other_c, other_x = 1 - c, 1 - x

    def far(dz):
        return lax.rem(z + dz, n)

    def back(dz):
        return lax.rem(z + n - dz, n)

    def remote(src, dst, send, recv, **where):
        return pltpu.make_async_remote_copy(
            src_ref=src, dst_ref=dst, send_sem=send, recv_sem=recv,
            device_id=where, device_id_type=MESH)

    def unless_ends(dz, act):
        if dz == n - 1:
            pl.when(z != 0)(act)
        elif dz == 1:
            pl.when(z != n - 1)(act)
        else:
            act()

    def relays(act):
        pl.when(z == 2)(lambda: act(1, 3))
        pl.when(z == 1)(lambda: act(3, 1))

    def raw_copy(i, slot):
        return pltpu.make_async_copy(
            dec.reshape(2 * F, H).at[pl.ds(pl.multiple_of(i * 2 * DC, 2 * DC), 2 * DC)], raw.at[slot], sem_raw.at[slot])

    nd = F // DC
    for i in range(slots - 1):
        raw_copy(i, i).start()
    enc_copy = pltpu.make_async_copy(enc, enc_v, sem_l)
    enc_copy.start()

    barrier = pltpu.get_barrier_semaphore()
    for dz in range(n):
        if dz:
            pl.semaphore_signal(barrier, inc=1, device_id={"feat": far(dz), "row": c}, device_id_type=MESH)
        pl.semaphore_signal(barrier, inc=1, device_id={"feat": far(dz), "row": other_c}, device_id_type=MESH)
    for cc in (c, other_c):
        pl.semaphore_signal(barrier, inc=1, device_id={"layer": other_x, "row": cc}, device_id_type=MESH)

    own_x = mm(pick(R, 2 * R, 2, x), res.reshape(2 * R, 2 * H)[...]).astype(BF)
    x_mine = jnp.where(c == 0, own_x[:, :H], own_x[:, H:])
    x_other = jnp.where(c == 0, own_x[:, H:], own_x[:, :H])
    for q in range(Q):
        xsend[0, q] = x_mine[:, q * HX:(q + 1) * HX]
        xsend[1, q] = x_other[:, q * HX:(q + 1) * HX]
        xg[z, c, q] = x_mine[:, q * HX:(q + 1) * HX]
    own_m = mm(pick(R, 2 * R, 2, x), mlp.reshape(2 * R, 2 * H)[...]).astype(BF)
    mlpx[c] = jnp.where(c == 0, own_m[:, :H], own_m[:, H:])
    msend[...] = jnp.where(c == 0, own_m[:, H:], own_m[:, :H])

    pl.semaphore_wait(barrier, 2 * n + 1)

    def x_copy(dz, k, q):
        return remote(xsend.at[k, q], xg.at[z, c, q], x_s.at[dz, k], x_r.at[dz, k, q],
                      feat=far(dz), row=c if k == 0 else other_c)

    x_list = [(dz, k) for dz in (2, 1, 3) for k in range(2)] + [(0, 1)]
    for q in range(Q):
        for dz, k in x_list:
            unless_ends(dz, lambda: x_copy(dz, k, q).start())

    def y_copy(k, q, to, at):
        cc = c if k == 0 else other_c
        return remote(xg.at[back(2), cc, q], xg.at[back(2), cc, q], y_s.at[k], x_r.at[at, k, q], feat=far(to))

    m_copy = remote(msend, mlpx.at[c], m_s, m_r, row=other_c)
    m_copy.start()
    d_all = jnp.where(x == 0, dbias[0:1, :], dbias[1:2, :])
    dsel[...] = jnp.where(c == 0, d_all[:, :H], d_all[:, H:])

    apart = jnp.concatenate([pick(DC, 2 * DC, 2, 0), pick(DC, 2 * DC, 2, 1)], axis=0)

    def split_body(i, carry):
        slot = lax.rem(i, slots)

        @pl.when(i + slots - 1 < nd)
        def _():
            raw_copy(i + slots - 1, lax.rem(i + slots - 1, slots)).start()

        raw_copy(i, slot).wait()
        both = mm(apart, raw[slot]).astype(BF)
        rows = pl.ds(pl.multiple_of(i * DC, DC), DC)
        dg[rows, :] = both[:DC]
        dg[pl.ds(pl.multiple_of(F + i * DC, DC), DC), :] = both[DC:]
        return carry

    def pass_on(q):
        for k in range(2):
            x_copy(2, k, q).wait_recv()
            relays(lambda to, at: y_copy(k, q, to, at).start())

    perm = (lax.broadcasted_iota(jnp.int32, (T, T), 0) == shuf[...]).astype(BF)

    def p_copy(k):
        return remote(pre.at[k, pl.ds(pl.multiple_of(other_c * T2, T2), T2)], pre_recv.at[k], p_s, p_r.at[k], row=other_c)

    mine = pl.ds(pl.multiple_of(c * T2, T2), T2)

    def f_copy(k):
        return remote(feats.at[k, mine], feats.at[k, mine], f_s, f_r, row=other_c)

    lax.fori_loop(0, nd // 2, split_body, 0)
    pass_on(0)
    lax.fori_loop(nd // 2, nd, split_body, 0)
    def rows_of(k, size, base=0):
        return pl.ds(pl.multiple_of(base + k * size, KC), size)

    def zero_body(k, carry):
        gacc[:, rows_of(k, KC), :] = jnp.zeros((2, KC, T2), jnp.float32)
        return carry

    lax.fori_loop(0, nk, zero_body, 0)
    enc_copy.wait()
    per = 2 if nk % 2 == 0 else 1
    for q in range(Q):
        if q:
            pass_on(q)
        for dz, k in x_list:
            if dz != 2:
                x_copy(dz, k, q).wait_recv()
        lo = q * HX
        xs[:, lo:lo + HX] = dot_first(perm, xg[:, :, q].reshape(T, HX)).astype(BF)

        def pre_body(i, carry):
            rows = pl.ds(pl.multiple_of(i * per * KC, KC), per * KC)
            v = dot_last(xs[:, lo:lo + HX], enc_v[rows, lo:lo + HX])
            for h in range(per):
                part = v[:, h * KC:(h + 1) * KC]
                k = i * per + h
                pre[k] = part if q == 0 else pre[k] + part
                if q == Q - 1:
                    p_copy(k).start()
            return carry

        lax.fori_loop(0, nk // per, pre_body, 0)

    def feat_body(k, carry):
        p_copy(k).wait_recv()
        cols = pl.ds(pl.multiple_of(k * KC, KC), KC)
        v = pre[k, mine, :] + pre_recv[k] + bias[:, cols]
        feats[k, mine, :] = jnp.maximum(v, 0.0).astype(BF)
        f_copy(k).start()
        return carry

    lax.fori_loop(0, nk, feat_body, 0)

    all_f = remote(feats.at[:, mine], feats.at[:, mine], f_s, f_r, row=other_c)
    all_f.wait_recv()
    m_copy.wait_recv()
    up0, up1 = spread_to(0), spread_to(1)

    def expand(b):
        rows = pl.ds(pl.multiple_of(b * 2 * DC, 2 * DC), 2 * DC)
        turned = feats[b // (KC // DC), :, pl.ds(pl.multiple_of(lax.rem(b, KC // DC) * DC, DC), DC)].T
        fx[rows, :T] = mm(up0, turned).astype(BF)

        @pl.when(x == 0)
        def _():
            fx[rows, T:] = mm(up1, turned).astype(BF)

    def n_copy(j):
        return remote(nsend.at[j], nrecv.at[j], n_s, n_r.at[j], layer=other_x)

    def right_copy(j, k, onward):
        some = pl.ds(k + 2, n - 2 - k) if onward else pl.ds(k + 1, 1)
        return remote(osend.at[j, some], rr.at[j, some], rs_s.at[0], rs_r.at[j, 0, onward], feat=k + 1)

    def left_copy(j, k, onward):
        some = pl.ds(0, k - 1) if onward else pl.ds(k - 1, 1)
        return remote(osend.at[j, some], rl.at[j, some], rs_s.at[1], rs_r.at[j, 1, onward], feat=k - 1)

    def send_right(j, k):
        for lo, hi, onward in ((k + 2, n, 1), (k + 1, k + 2, 0)):
            if lo < hi:
                v = facc[j, lo:hi]
                if k > 0:
                    v = v + rr[j, lo:hi].astype(jnp.float32)
                osend[j, lo:hi] = v.astype(BF)
                right_copy(j, k, onward).start()

    def send_left(j, k):
        for lo, hi, onward in ((0, k - 1, 1), (k - 1, k, 0)):
            if lo < hi:
                v = facc[j, lo:hi]
                if k < n - 1:
                    v = v + rl[j, lo:hi].astype(jnp.float32)
                osend[j, lo:hi] = v.astype(BF)
                left_copy(j, k, onward).start()

    def wide(j):
        return pl.ds(pl.multiple_of(j * NC, NC), NC)

    def all_feats():
        return jnp.concatenate([feats[k] for k in range(nk)], axis=1)

    def send_next(j):
        @pl.when(x == 0)
        def _():
            nsend[j] = mm(all_feats(), dg[pl.ds(F, F), wide(j)]).astype(BF)
            n_copy(j).start()

    def front(j):
        for i in range(2):
            pl.when(2 * j + i < J)(functools.partial(send_next, 2 * j + i))
        facc[j] = mm(all_feats(), dg[pl.ds(0, F), wide(j)]).reshape(n, CR, NC)

        @pl.when(x == 1)
        def _():
            n_copy(j).wait_recv()
            facc[j] = facc[j] + nrecv[j].astype(jnp.float32).reshape(n, CR, NC)

        pl.when(z == 0)(lambda: send_right(j, 0))
        pl.when(z == n - 1)(lambda: send_left(j, n - 1))

    def go_right(j, k):
        right_copy(j, k - 1, 1).wait_recv()
        send_right(j, k)

    def go_left(j, k):
        left_copy(j, k + 1, 1).wait_recv()
        send_left(j, k)

    def relay_near(j):
        pl.when(z == 1)(lambda: go_right(j, 1))
        pl.when(z == 2)(lambda: go_left(j, 2))

    def relay_far(j):
        pl.when(z == 2)(lambda: go_right(j, 2))
        pl.when(z == 1)(lambda: go_left(j, 1))

    def a_copy(j, b, way):
        to = jnp.minimum(z + 1, n - 1) if way == 0 else jnp.maximum(z - 1, 0)
        return remote(e.at[j, 0, b], e.at[j, 0, b], a_s.at[way], a_r.at[j, b], feat=to)

    def t_copy(j, b):
        return remote(e.at[j, 0, b], e.at[j, 1, b], t_s, t_r.at[j], layer=other_x)

    def final(j):
        for k in range(n):
            @pl.when(z == k)
            def _():
                if k > 0:
                    right_copy(j, k - 1, 0).wait_recv()
                if k < n - 1:
                    left_copy(j, k + 1, 0).wait_recv()

        @pl.when(z > 0)
        def _():
            facc[j, z] = facc[j, z] + rr[j, z].astype(jnp.float32)

        @pl.when(z < n - 1)
        def _():
            facc[j, z] = facc[j, z] + rl[j, z].astype(jnp.float32)

        total = facc[j, z] + dsel[:, wide(j)]
        e[j, 0, z] = (total - mlpx[:, :, wide(j)].reshape(CR, NC).astype(jnp.float32)).astype(BF)
        pl.when(z < n - 1)(lambda: a_copy(j, z, 0).start())
        pl.when(z > 0)(lambda: a_copy(j, z, 1).start())
        pl.when(x == 1)(lambda: t_copy(j, z).start())
        kept = total.astype(BF).reshape(2, R, NC)
        rc[0, j] = kept[0]
        rc[1, j] = kept[1]

    def hop(j, h):
        @pl.when(z >= h)
        def _():
            a_copy(j, z - h, 0).wait_recv()
            pl.when(z < n - 1)(lambda: a_copy(j, z - h, 0).start())
            pl.when(x == 1)(lambda: t_copy(j, z - h).start())

        @pl.when(z + h < n)
        def _():
            a_copy(j, z + h, 1).wait_recv()
            pl.when(z > 0)(lambda: a_copy(j, z + h, 1).start())
            pl.when(x == 1)(lambda: t_copy(j, z + h).start())

    def g_copy(k):
        rows = rows_of(k, GB)
        return remote(g_send.at[:, rows], g_recv.at[:, rows], g_s, g_r.at[k], row=other_c)

    def add_grads(j, k, size, both):
        rows = rows_of(k, size)
        v = dot_last(dg[rows, wide(j)], e[j, 0].reshape(T, NC))
        if both:
            v = v + dot_last(dg[rows_of(k, size, F), wide(j)], e[j, 1].reshape(T, NC))
        gacc[0, rows, :] = gacc[0, rows, :] + v[:, :T2]
        gacc[1, rows, :] = gacc[1, rows, :] + v[:, T2:]

    def sum_grads(j, both):
        @pl.when(j < J - 1)
        def _():
            for k in range(F // GC):
                add_grads(j, k, GC, both)

        @pl.when(j == J - 1)
        def _():
            def body(k, carry):
                add_grads(j, k, GB, both)
                rows = rows_of(k, GB)
                g_send[:, rows, :] = gacc[:, rows, :].astype(BF)
                g_copy(k).start()
                return carry

            lax.fori_loop(0, F // GB, body, 0)

    def grads(j):
        sum_grads(j, False)

    def both_grads(j):
        remote(e.at[j, 0], e.at[j, 1], t_s, t_r.at[j], layer=other_x).wait_recv()
        sum_grads(j, True)

    def weights(j):
        def body(k, carry):
            rows = rows_of(k, 2 * GC)
            dg[rows, wide(j)] = (scale * mm(fx[rows, :T], e[j, 0].reshape(T, NC))).astype(BF)
            return carry

        lax.fori_loop(0, F // GC, body, 0)

    def both_weights(j):
        def body(k, carry):
            rows = rows_of(k, 2 * GC)
            dg[rows, wide(j)] = (scale * mm(fx[rows, :], e[j].reshape(2 * T, NC))).astype(BF)
            return carry

        lax.fori_loop(0, F // GC, body, 0)

    cuts = (0, J // 3, 2 * J // 3, J)

    def b_copy(k, p):
        dx, dc = k // 2, k % 2
        to_x = other_x if dx else x
        to_c = other_c if dc else c
        some = pl.ds(0, J) if p is None else pl.ds(cuts[p], cuts[p + 1] - cuts[p])
        return remote(rc.at[to_c, some], rb.at[x, c, some], b_s.at[k], b_r.at[k], layer=to_x, row=to_c)

    def start_b(p):
        for k in range(1, 4):
            b_copy(k, p).start()

    def early_b(j):
        for p in range(2):
            pl.when(j == cuts[p + 1] - 1)(functools.partial(start_b, p))

    def late_b(j):
        pl.when(j == J - 1)(lambda: start_b(2))

    stages = (
        (0, None, front), (1, None, relay_near), (2, None, relay_far), (3, None, final), (3, None, early_b),
        (4, None, lambda j: hop(j, 1)), (5, None, lambda j: hop(j, 2)), (6, None, lambda j: hop(j, 3)), (6, None, late_b),
        (LAG1, 1, grads), (LAG1 + 1, 1, weights), (LAG0, 0, both_grads), (LAG0, 0, both_weights))
    steps = J + max(LAG0, LAG1)
    share = pl.cdiv(nd, LAG0)

    def pipe(s, carry):
        for lag, side, act in stages:
            end = J - LATE if act in (weights, both_weights) else J
            live = jnp.logical_and(s >= lag, s < end + lag)
            if side is not None:
                live = jnp.logical_and(live, x == side)
            pl.when(live)(functools.partial(act, s - lag))
        for i in range(share):
            pl.when(jnp.logical_and(x == 0, s * share + i < nd))(functools.partial(expand, s * share + i))
        return carry

    @pl.when(x == 1)
    def _():
        def body(b, carry):
            expand(b)
            return carry

        lax.fori_loop(0, nd, body, 0)

    lax.fori_loop(0, steps, pipe, 0)

    spent = (J - LATE) * NC

    def keep_fx(k, carry):
        rows = rows_of(k, GC)
        dg[rows, spent:spent + T] = fx[rows, :T]

        @pl.when(x == 0)
        def _():
            dg[rows, spent + T:spent + 2 * T] = fx[rows, T:]

        return carry

    lax.fori_loop(0, 2 * F // GC, keep_fx, 0)
    for h in range(LATE):
        dg[2 * h * T:(2 * h + 1) * T, spent + 2 * T:spent + 2 * T + NC] = e[J - LATE + h, 0].reshape(T, NC)

        @pl.when(x == 0)
        def _():
            dg[(2 * h + 1) * T:(2 * h + 2) * T, spent + 2 * T:spent + 2 * T + NC] = e[J - LATE + h, 1].reshape(T, NC)

    def mask_body(k, carry):
        g_copy(k).wait_recv()
        rows = rows_of(k, GB)
        for h in range(2):
            seen = jnp.concatenate(
                [feats[k * (GB // KC) + i, h * T2:(h + 1) * T2, :] for i in range(GB // KC)], axis=1).T
            v = (g_send[h, rows, :].astype(jnp.float32) + g_recv[h, rows, :].astype(jnp.float32)) * scale
            gt[h, rows, :] = jnp.where(seen.astype(jnp.float32) > 0, v, 0.0).astype(BF)
        return carry

    lax.fori_loop(0, F // GB, mask_body, 0)
    rb[x, c] = rc[c]
    theirs = pl.ds(pl.multiple_of(other_c * T2, T2), T2)
    remote(pre.at[:, theirs], pre_recv, p_s, p_r.at[0], row=other_c).wait_send()
    all_f.wait_send()
    m_copy.wait_send()

    def x_all(dz, k):
        return remote(xsend.at[k], xg.at[z, c], x_s.at[dz, k], x_r.at[dz, k, 0], feat=far(dz), row=other_c)

    for dz, k in x_list:
        unless_ends(dz, lambda: x_all(dz, k).wait_send())

    def y_all(k, to, at):
        cc = c if k == 0 else other_c
        return remote(xg.at[back(2), cc], xg.at[back(2), cc], y_s.at[k], x_r.at[at, k, 0], feat=far(to))

    for k in range(2):
        relays(lambda to, at: y_all(k, to, at).wait_send())

    def sent(src, sem, **where):
        remote(src, src, sem, a_r.at[0, 0], **where).wait_send()

    for k in range(n):
        @pl.when(z == k)
        def _():
            if k < n - 1:
                sent(osend.at[:, pl.ds(k + 1, n - 1 - k)], rs_s.at[0], feat=k + 1)
                sent(e.at[:, 0, pl.ds(0, k + 1)], a_s.at[0], feat=k + 1)
            if k > 0:
                sent(osend.at[:, pl.ds(0, k)], rs_s.at[1], feat=k - 1)
                sent(e.at[:, 0, pl.ds(k, n - k)], a_s.at[1], feat=k - 1)

    pl.when(x == 0)(lambda: sent(nsend, n_s, layer=other_x))
    pl.when(x == 1)(lambda: sent(e.at[:, 0], t_s, layer=other_x))
    for k in range(1, 4):
        b_copy(k, None).wait_recv()
    for k in range(1, 4):
        b_copy(k, None).wait_send()

    sent(g_send, g_s, row=other_c)


def weight_kernel(
    dg, gt, xs, rb, enc_grad, dec_grad, bgrad, rebuilt,
    parts, late, ebuf, bbuf, rbuf, dsem, lsem, esem, bsem, rsem,
):
    F, T2 = gt.shape[1:]
    T, H = xs.shape
    NC = KC
    R2 = parts.shape[0]
    nb, nl = F // KC, F // LC
    x = lax.axis_index("layer")
    scale = float(T) ** (-0.5)
    done = H - LATE * NC

    def rows_of(i, size):
        return pl.ds(pl.multiple_of(i * size, size), size)

    def d_copy(i):
        rows = rows_of(i, 2 * KC)
        return pltpu.make_async_copy(
            dg.at[rows, pl.ds(0, done)], dec_grad.reshape(2 * F, H).at[rows, pl.ds(0, done)], dsem.at[i])

    def l_copy(i):
        rows = rows_of(i, 2 * LC)
        return pltpu.make_async_copy(
            late.at[rows], dec_grad.reshape(2 * F, H).at[rows, pl.ds(done, LATE * NC)], lsem.at[i])

    def e_copy(i):
        slot = lax.rem(i, 4)
        return pltpu.make_async_copy(ebuf.at[slot], enc_grad.at[rows_of(i, KC)], esem.at[slot])

    b_copy = pltpu.make_async_copy(bbuf, bgrad, bsem)
    r_copy = pltpu.make_async_copy(rbuf, rebuilt.reshape(R2, 2 * H), rsem)
    for i in range(nb):
        d_copy(i).start()

    def late_block(i, carry):
        rows = rows_of(i, 2 * LC)

        def chunk(h, inner):
            cols = rows_of(h, NC)

            @pl.when(x == 0)
            def _():
                late[rows, cols] = (scale * mm(dg[rows, done:done + 2 * T], dg[rows_of(h, 2 * T), done + 2 * T:done + 2 * T + NC])).astype(BF)

            @pl.when(x == 1)
            def _():
                late[rows, cols] = (scale * mm(dg[rows, done:done + T], dg[pl.ds(pl.multiple_of(2 * h * T, T), T), done + 2 * T:done + 2 * T + NC])).astype(BF)

            return inner

        lax.fori_loop(0, LATE, chunk, 0)
        l_copy(i).start()
        return carry

    ones = jnp.ones((8, 2 * T2), BF)

    def block(i, carry):
        rows = rows_of(i, KC)
        g = jnp.concatenate([gt[0, rows, :], gt[1, rows, :]], axis=1)
        pl.when(i >= 4)(lambda: e_copy(i - 4).wait())
        ebuf[lax.rem(i, 4)] = mm(g, xs[...]).astype(BF)
        e_copy(i).start()
        bbuf[:, rows] = dot_last(ones, g)[0:1]
        return carry

    lax.fori_loop(0, nl, late_block, 0)
    for h in range(2):
        for j in range(rb.shape[2]):
            lo = h * H + j * NC
            parts[:, lo:lo + NC] = rb[:, h, j].reshape(R2, NC)
    i = lax.broadcasted_iota(jnp.int32, (R2, R2), 0)
    j = lax.broadcasted_iota(jnp.int32, (R2, R2), 1)
    inter = (j == (i % 2) * (R2 // 2) + i // 2).astype(BF)
    rbuf[...] = mm(inter, parts[...]).astype(BF)
    r_copy.start()
    lax.fori_loop(0, nb, block, 0)
    b_copy.start()
    for i in range(nb):
        d_copy(i).wait()
    for i in range(max(nb - 4, 0), nb):
        e_copy(i).wait()
    for i in range(nl):
        l_copy(i).wait()
    r_copy.wait()
    b_copy.wait()


def fused(resid_buf, shuffle, mlp_out, enc_weight, dec_weight, enc_bias, dec_bias):
    n = lax.axis_size("feat")
    R = resid_buf.shape[0]
    F, H = enc_weight.shape[1:]
    T = R * n * 2
    T2, CR = T // 2, 2 * R
    J = H // KC
    NC, nk = H // J, F // KC
    Q = halves_of(H)
    HX = H // Q
    f32 = jnp.float32
    vm = pl.BlockSpec(memory_space=pltpu.VMEM)
    hbm = pl.BlockSpec(memory_space=pl.ANY)
    dma = pltpu.SemaphoreType.DMA
    vmem = pltpu.VMEM
    shape = jax.ShapeDtypeStruct
    outs = ((2 * F, H), (T, H), (2, F, T2), (2, 2, J, R, NC))
    held = sum(2 * math.prod(a) for a in outs)
    dg, xs, gt, rb = pl.pallas_call(
        functools.partial(step_kernel, n, J),
        out_shape=tuple(vmem(a, BF) for a in outs),
        in_specs=[vm, vm, vm, hbm, hbm, vm, vm],
        out_specs=(vm,) * 4,
        scratch_shapes=[
            vmem((2 * F, 2 * T), BF), vmem((J, 2, n, CR, NC), BF), vmem((F, H), BF), vmem((3, 2 * DC, H), BF),
            vmem((2, Q, R, HX), BF), vmem((n, 2, Q, R, HX), BF),
            vmem((2, R, H), BF), vmem((R, H), BF), vmem((1, H), f32),
            vmem((nk, T, KC), f32), vmem((nk, T2, KC), f32), vmem((nk, T, KC), BF),
            vmem((J, T, NC), BF), vmem((J, T, NC), BF), vmem((J, n, CR, NC), f32),
            vmem((J, n, CR, NC), BF), vmem((J, n, CR, NC), BF), vmem((J, n, CR, NC), BF),
            vmem((2, J, R, NC), BF),
            vmem((2, F, T2), f32), vmem((2, F, T2), BF), vmem((2, F, T2), BF),
            dma, dma((4,)), dma((n, 2)), dma((n, 2, Q)), dma((2,)), dma, dma,
            dma, dma((nk,)), dma, dma, dma, dma((J,)),
            dma((2,)), dma((J, 2, 2)), dma((2,)), dma((J, n)), dma, dma((J,)),
            dma((4,)), dma((4,)), dma, dma((F // GB,)),
        ],
        compiler_params=pltpu.CompilerParams(
            collective_id=0, has_side_effects=True, vmem_limit_bytes=VMEM_LIMIT - held),
    )(resid_buf, shuffle.reshape(1, T), mlp_out, enc_weight[0], dec_weight[0], enc_bias, dec_bias)
    enc_grad, dec_grad, bgrad, rebuilt = pl.pallas_call(
        weight_kernel,
        out_shape=(
            shape((F, H), BF), shape((F, 2, H), BF), shape((1, F), f32), shape((R, 2, 2 * H), BF)),
        in_specs=[vm] * 4,
        out_specs=(hbm,) * 4,
        scratch_shapes=[
            vmem((2 * R, 2 * H), BF), vmem((2 * F, LATE * NC), BF), vmem((4, KC, H), BF), vmem((1, F), f32), vmem((2 * R, 2 * H), BF),
            dma((nk,)), dma((F // LC,)), dma((4,)), dma, dma],
        compiler_params=pltpu.CompilerParams(vmem_limit_bytes=VMEM_LIMIT // 4),
    )(dg, gt, xs, rb)
    return rebuilt, enc_grad[None], dec_grad[None], bgrad


def chosen(resid_buf, shuffle, mlp_out, enc_weight, dec_weight, enc_bias, dec_bias):
    args = (resid_buf, shuffle, mlp_out, enc_weight, dec_weight, enc_bias, dec_bias)
    rows, width = resid_buf.shape[0], enc_weight.shape[2]
    fits = (
        lax.axis_size("layer") == LAYERS == 2 and lax.axis_size("row") == 2
        and lax.axis_size("feat") == 4 and rows % 16 == 0
        and width % KC == 0 and width // KC > LATE
        and rows * 2 * lax.axis_size("feat") == KC and enc_weight.shape[1] % GC == 0)
    return fused(*args) if fits else on_device(*args)


def solution(mesh):
    return jax.shard_map(
        chosen,
        mesh=mesh,
        in_specs=(
            P(("groups", "feat", "row"), None, None),
            P("groups"),
            P(("groups", "feat", "row"), None, None),
            P("layer", "feat", "row"),
            P("layer", "feat", None, "row"),
            P("layer", "feat"),
            P(),
        ),
        out_specs=(
            P(("groups", "feat", "row"), None, None),
            P(("groups", "layer"), "feat", "row"),
            P(("groups", "layer"), "feat", None, "row"),
            P(("groups", "layer"), "feat"),
        ),
        check_vma=False,
    )
```

```python
import functools
import math

import jax
import jax.numpy as jnp
from jax import lax
from jax.experimental import pallas as pl
from jax.experimental.pallas import tpu as pltpu
from jax.sharding import PartitionSpec as P

LAYERS = 2


def from_behind(block, axis, distance):
    devices = range(lax.axis_size(axis))
    route = [(i - distance, i) for i in devices if i - distance in devices]
    return lax.ppermute(block, axis, route)


def dot_last(left, right):
    return lax.dot_general(
        left, right, (((1,), (1,)), ((), ())), preferred_element_type=jnp.float32
    )


def dot_first(left, right):
    return lax.dot_general(
        left, right, (((0,), (0,)), ((), ())), preferred_element_type=jnp.float32
    )


def on_device(resid_buf, shuffle, mlp_out, enc_weight, dec_weight, enc_bias, dec_bias):
    feat_count = lax.axis_size("feat")
    row_count = lax.axis_size("row")
    sub_blocks = lax.axis_size("layer") // LAYERS
    layer_pos = lax.axis_index("layer")
    row_pos = lax.axis_index("row")
    source = layer_pos // sub_blocks
    rows_each = resid_buf.shape[0]
    width = dec_bias.shape[1]
    half_width = enc_weight.shape[2]
    local_rows = rows_each * feat_count
    total_rows = local_rows * row_count
    loss_scale = float(total_rows) ** (-0.5)
    own_layer = lax.dynamic_index_in_dim(resid_buf, source, axis=1, keepdims=False)
    buffer_all = lax.all_gather(own_layer, ("feat", "row"), axis=0, tiled=True)
    batch_rows = jnp.take(buffer_all, shuffle, axis=0)
    blocks = batch_rows.reshape(feat_count, row_count, rows_each, width)
    inputs_half = lax.dynamic_slice_in_dim(
        jnp.swapaxes(blocks, 0, 1), row_pos * half_width, half_width, axis=3
    )
    inputs_half = inputs_half.reshape(total_rows, half_width)
    own_half_dec = dec_weight[0][:, 0]
    next_half_dec = dec_weight[0][:, 1]
    pre_all = lax.psum(dot_last(inputs_half, enc_weight[0]), "row") + enc_bias[0]
    features_all = jnp.maximum(pre_all, 0.0).astype(jnp.bfloat16)
    own_part = jnp.dot(features_all, own_half_dec, preferred_element_type=jnp.float32)
    next_part = jnp.dot(features_all, next_half_dec, preferred_element_type=jnp.float32)
    carried = from_behind(next_part, "layer", sub_blocks)
    spread = (own_part + carried).reshape(row_count, local_rows, half_width)
    halves = lax.psum_scatter(spread, "feat", scatter_dimension=1, tiled=True)
    joined = lax.all_to_all(halves, "row", split_axis=0, concat_axis=2, tiled=True)
    section_sum = joined.reshape(rows_each, width)
    target_ids = jnp.arange(LAYERS, dtype=jnp.int32)
    target_slots = jnp.where((target_ids == source)[:, None, None], section_sum[None], 0.0)
    totals = lax.psum(target_slots, "layer")
    recon_sum = jnp.swapaxes(totals, 0, 1) + dec_bias[None]
    errors = (recon_sum - mlp_out.astype(jnp.float32)).astype(jnp.bfloat16)
    gathered = lax.all_gather(errors, ("feat", "row"), axis=0, tiled=True)
    error_grid = gathered.reshape(feat_count, row_count, rows_each, LAYERS, width)
    errors_mine = lax.dynamic_index_in_dim(error_grid, row_pos, axis=1, keepdims=False)
    errors_mine = errors_mine.reshape(local_rows, LAYERS, width)
    errors_half = lax.dynamic_slice_in_dim(
        jnp.swapaxes(error_grid, 0, 1), row_pos * half_width, half_width, axis=4
    )
    errors_half = errors_half.reshape(total_rows, LAYERS, half_width)
    live_next = source + 1 < LAYERS
    next_index = jnp.minimum(source + 1, LAYERS - 1)
    half_own = lax.dynamic_index_in_dim(errors_half, source, axis=1, keepdims=False)
    half_next = lax.dynamic_index_in_dim(errors_half, next_index, axis=1, keepdims=False)
    half_next = jnp.where(live_next, half_next, jnp.zeros_like(half_next))
    half_terms = dot_last(half_own, own_half_dec) + dot_last(half_next, next_half_dec)
    grad_feats = lax.psum(half_terms, "row") * loss_scale
    grad_all = jnp.where(pre_all > 0, grad_feats, 0.0).astype(jnp.bfloat16)
    grad_own = loss_scale * dot_first(features_all, half_own)
    grad_next = loss_scale * dot_first(features_all, half_next)
    enc_grad = dot_first(grad_all, inputs_half).astype(jnp.bfloat16)
    dec_grad = jnp.stack([grad_own, grad_next], axis=1).astype(jnp.bfloat16)
    bias_grad = jnp.sum(grad_all.astype(jnp.float32), axis=0)
    return (recon_sum.astype(jnp.bfloat16), enc_grad[None], dec_grad[None], bias_grad[None])

KC = 256
DC = 128
GC = 2048
LC = 2048
GB = 512
LAG0 = 8
LATE = 3
LAG1 = 7
MESH = pl.DeviceIdType.MESH
VMEM_LIMIT = 67043328
BF = jnp.bfloat16


def pick(rows, cols, stride, offset):
    r = lax.broadcasted_iota(jnp.int32, (rows, cols), 0)
    c = lax.broadcasted_iota(jnp.int32, (rows, cols), 1)
    return (c == stride * r + offset).astype(BF)


def spread_to(offset):
    r = lax.broadcasted_iota(jnp.int32, (2 * DC, DC), 0)
    c = lax.broadcasted_iota(jnp.int32, (2 * DC, DC), 1)
    return (r == 2 * c + offset).astype(BF)


def mm(left, right):
    return jnp.dot(left, right, preferred_element_type=jnp.float32)


def halves_of(width):
    return next(q for q in (3, 2, 1) if width % (q * DC) == 0)


def step_kernel(
    n, J, res, shuf, mlp, enc, dec, bias, dbias,
    dg, xs, gt, rb,
    fx, e, enc_v, raw, xsend, xg, mlpx, msend, dsel, pre, pre_recv, feats,
    nsend, nrecv, facc, osend, rr, rl, rc, gacc, g_send, g_recv,
    sem_l, sem_raw, x_s, x_r, y_s, m_s, m_r, p_s, p_r, f_s, f_r, n_s, n_r,
    rs_s, rs_r, a_s, a_r, t_s, t_r, b_s, b_r, g_s, g_r,
):
    z = lax.axis_index("feat")
    x = lax.axis_index("layer")
    c = lax.axis_index("row")
    Q, R, HX = xsend.shape[1:]
    F, H = enc_v.shape
    T = xs.shape[0]
    T2, CR, NC = T // 2, 2 * R, H // J
    nk, slots = F // KC, raw.shape[0]
    scale = float(T) ** (-0.5)
    other_c, other_x = 1 - c, 1 - x

    def far(dz):
        return lax.rem(z + dz, n)

    def back(dz):
        return lax.rem(z + n - dz, n)

    def remote(src, dst, send, recv, **where):
        return pltpu.make_async_remote_copy(
            src_ref=src, dst_ref=dst, send_sem=send, recv_sem=recv,
            device_id=where, device_id_type=MESH)

    def unless_ends(dz, act):
        if dz == n - 1:
            pl.when(z != 0)(act)
        elif dz == 1:
            pl.when(z != n - 1)(act)
        else:
            act()

    def relays(act):
        pl.when(z == 2)(lambda: act(1, 3))
        pl.when(z == 1)(lambda: act(3, 1))

    def raw_copy(i, slot):
        return pltpu.make_async_copy(
            dec.reshape(2 * F, H).at[pl.ds(pl.multiple_of(i * 2 * DC, 2 * DC), 2 * DC)], raw.at[slot], sem_raw.at[slot])

    nd = F // DC
    for i in range(slots - 1):
        raw_copy(i, i).start()
    enc_copy = pltpu.make_async_copy(enc, enc_v, sem_l)
    enc_copy.start()

    barrier = pltpu.get_barrier_semaphore()
    for dz in range(n):
        if dz:
            pl.semaphore_signal(barrier, inc=1, device_id={"feat": far(dz), "row": c}, device_id_type=MESH)
        pl.semaphore_signal(barrier, inc=1, device_id={"feat": far(dz), "row": other_c}, device_id_type=MESH)
    for cc in (c, other_c):
        pl.semaphore_signal(barrier, inc=1, device_id={"layer": other_x, "row": cc}, device_id_type=MESH)

    own_x = mm(pick(R, 2 * R, 2, x), res.reshape(2 * R, 2 * H)[...]).astype(BF)
    x_mine = jnp.where(c == 0, own_x[:, :H], own_x[:, H:])
    x_other = jnp.where(c == 0, own_x[:, H:], own_x[:, :H])
    for q in range(Q):
        xsend[0, q] = x_mine[:, q * HX:(q + 1) * HX]
        xsend[1, q] = x_other[:, q * HX:(q + 1) * HX]
        xg[z, c, q] = x_mine[:, q * HX:(q + 1) * HX]
    own_m = mm(pick(R, 2 * R, 2, x), mlp.reshape(2 * R, 2 * H)[...]).astype(BF)
    mlpx[c] = jnp.where(c == 0, own_m[:, :H], own_m[:, H:])
    msend[...] = jnp.where(c == 0, own_m[:, H:], own_m[:, :H])

    pl.semaphore_wait(barrier, 2 * n + 1)

    def x_copy(dz, k, q):
        return remote(xsend.at[k, q], xg.at[z, c, q], x_s.at[dz, k], x_r.at[dz, k, q],
                      feat=far(dz), row=c if k == 0 else other_c)

    x_list = [(dz, k) for dz in (2, 1, 3) for k in range(2)] + [(0, 1)]
    for q in range(Q):
        for dz, k in x_list:
            unless_ends(dz, lambda: x_copy(dz, k, q).start())

    def y_copy(k, q, to, at):
        cc = c if k == 0 else other_c
        return remote(xg.at[back(2), cc, q], xg.at[back(2), cc, q], y_s.at[k], x_r.at[at, k, q], feat=far(to))

    m_copy = remote(msend, mlpx.at[c], m_s, m_r, row=other_c)
    m_copy.start()
    d_all = jnp.where(x == 0, dbias[0:1, :], dbias[1:2, :])
    dsel[...] = jnp.where(c == 0, d_all[:, :H], d_all[:, H:])

    apart = jnp.concatenate([pick(DC, 2 * DC, 2, 0), pick(DC, 2 * DC, 2, 1)], axis=0)

    def split_body(i, carry):
        slot = lax.rem(i, slots)

        @pl.when(i + slots - 1 < nd)
        def _():
            raw_copy(i + slots - 1, lax.rem(i + slots - 1, slots)).start()

        raw_copy(i, slot).wait()
        both = mm(apart, raw[slot]).astype(BF)
        rows = pl.ds(pl.multiple_of(i * DC, DC), DC)
        dg[rows, :] = both[:DC]
        dg[pl.ds(pl.multiple_of(F + i * DC, DC), DC), :] = both[DC:]
        return carry

    def pass_on(q):
        for k in range(2):
            x_copy(2, k, q).wait_recv()
            relays(lambda to, at: y_copy(k, q, to, at).start())

    perm = (lax.broadcasted_iota(jnp.int32, (T, T), 0) == shuf[...]).astype(BF)

    def p_copy(k):
        return remote(pre.at[k, pl.ds(pl.multiple_of(other_c * T2, T2), T2)], pre_recv.at[k], p_s, p_r.at[k], row=other_c)

    mine = pl.ds(pl.multiple_of(c * T2, T2), T2)

    def f_copy(k):
        return remote(feats.at[k, mine], feats.at[k, mine], f_s, f_r, row=other_c)

    lax.fori_loop(0, nd // 2, split_body, 0)
    pass_on(0)
    lax.fori_loop(nd // 2, nd, split_body, 0)
    def rows_of(k, size, base=0):
        return pl.ds(pl.multiple_of(base + k * size, KC), size)

    def zero_body(k, carry):
        gacc[:, rows_of(k, KC), :] = jnp.zeros((2, KC, T2), jnp.float32)
        return carry

    lax.fori_loop(0, nk, zero_body, 0)
    enc_copy.wait()
    per = 2 if nk % 2 == 0 else 1
    for q in range(Q):
        if q:
            pass_on(q)
        for dz, k in x_list:
            if dz != 2:
                x_copy(dz, k, q).wait_recv()
        lo = q * HX
        xs[:, lo:lo + HX] = dot_first(perm, xg[:, :, q].reshape(T, HX)).astype(BF)

        def pre_body(i, carry):
            rows = pl.ds(pl.multiple_of(i * per * KC, KC), per * KC)
            v = dot_last(xs[:, lo:lo + HX], enc_v[rows, lo:lo + HX])
            for h in range(per):
                part = v[:, h * KC:(h + 1) * KC]
                k = i * per + h
                pre[k] = part if q == 0 else pre[k] + part
                if q == Q - 1:
                    p_copy(k).start()
            return carry

        lax.fori_loop(0, nk // per, pre_body, 0)

    def feat_body(k, carry):
        p_copy(k).wait_recv()
        cols = pl.ds(pl.multiple_of(k * KC, KC), KC)
        v = pre[k, mine, :] + pre_recv[k] + bias[:, cols]
        feats[k, mine, :] = jnp.maximum(v, 0.0).astype(BF)
        f_copy(k).start()
        return carry

    lax.fori_loop(0, nk, feat_body, 0)

    all_f = remote(feats.at[:, mine], feats.at[:, mine], f_s, f_r, row=other_c)
    all_f.wait_recv()
    m_copy.wait_recv()
    up0, up1 = spread_to(0), spread_to(1)

    def expand(b):
        rows = pl.ds(pl.multiple_of(b * 2 * DC, 2 * DC), 2 * DC)
        turned = feats[b // (KC // DC), :, pl.ds(pl.multiple_of(lax.rem(b, KC // DC) * DC, DC), DC)].T
        fx[rows, :T] = mm(up0, turned).astype(BF)

        @pl.when(x == 0)
        def _():
            fx[rows, T:] = mm(up1, turned).astype(BF)

    def n_copy(j):
        return remote(nsend.at[j], nrecv.at[j], n_s, n_r.at[j], layer=other_x)

    def right_copy(j, k, onward):
        some = pl.ds(k + 2, n - 2 - k) if onward else pl.ds(k + 1, 1)
        return remote(osend.at[j, some], rr.at[j, some], rs_s.at[0], rs_r.at[j, 0, onward], feat=k + 1)

    def left_copy(j, k, onward):
        some = pl.ds(0, k - 1) if onward else pl.ds(k - 1, 1)
        return remote(osend.at[j, some], rl.at[j, some], rs_s.at[1], rs_r.at[j, 1, onward], feat=k - 1)

    def send_right(j, k):
        for lo, hi, onward in ((k + 2, n, 1), (k + 1, k + 2, 0)):
            if lo < hi:
                v = facc[j, lo:hi]
                if k > 0:
                    v = v + rr[j, lo:hi].astype(jnp.float32)
                osend[j, lo:hi] = v.astype(BF)
                right_copy(j, k, onward).start()

    def send_left(j, k):
        for lo, hi, onward in ((0, k - 1, 1), (k - 1, k, 0)):
            if lo < hi:
                v = facc[j, lo:hi]
                if k < n - 1:
                    v = v + rl[j, lo:hi].astype(jnp.float32)
                osend[j, lo:hi] = v.astype(BF)
                left_copy(j, k, onward).start()

    def wide(j):
        return pl.ds(pl.multiple_of(j * NC, NC), NC)

    def all_feats():
        return jnp.concatenate([feats[k] for k in range(nk)], axis=1)

    def send_next(j):
        @pl.when(x == 0)
        def _():
            nsend[j] = mm(all_feats(), dg[pl.ds(F, F), wide(j)]).astype(BF)
            n_copy(j).start()

    def front(j):
        for i in range(2):
            pl.when(2 * j + i < J)(functools.partial(send_next, 2 * j + i))
        facc[j] = mm(all_feats(), dg[pl.ds(0, F), wide(j)]).reshape(n, CR, NC)

        @pl.when(x == 1)
        def _():
            n_copy(j).wait_recv()
            facc[j] = facc[j] + nrecv[j].astype(jnp.float32).reshape(n, CR, NC)

        pl.when(z == 0)(lambda: send_right(j, 0))
        pl.when(z == n - 1)(lambda: send_left(j, n - 1))

    def go_right(j, k):
        right_copy(j, k - 1, 1).wait_recv()
        send_right(j, k)

    def go_left(j, k):
        left_copy(j, k + 1, 1).wait_recv()
        send_left(j, k)

    def relay_near(j):
        pl.when(z == 1)(lambda: go_right(j, 1))
        pl.when(z == 2)(lambda: go_left(j, 2))

    def relay_far(j):
        pl.when(z == 2)(lambda: go_right(j, 2))
        pl.when(z == 1)(lambda: go_left(j, 1))

    def a_copy(j, b, way):
        to = jnp.minimum(z + 1, n - 1) if way == 0 else jnp.maximum(z - 1, 0)
        return remote(e.at[j, 0, b], e.at[j, 0, b], a_s.at[way], a_r.at[j, b], feat=to)

    def t_copy(j, b):
        return remote(e.at[j, 0, b], e.at[j, 1, b], t_s, t_r.at[j], layer=other_x)

    def final(j):
        for k in range(n):
            @pl.when(z == k)
            def _():
                if k > 0:
                    right_copy(j, k - 1, 0).wait_recv()
                if k < n - 1:
                    left_copy(j, k + 1, 0).wait_recv()

        @pl.when(z > 0)
        def _():
            facc[j, z] = facc[j, z] + rr[j, z].astype(jnp.float32)

        @pl.when(z < n - 1)
        def _():
            facc[j, z] = facc[j, z] + rl[j, z].astype(jnp.float32)

        total = facc[j, z] + dsel[:, wide(j)]
        e[j, 0, z] = (total - mlpx[:, :, wide(j)].reshape(CR, NC).astype(jnp.float32)).astype(BF)
        pl.when(z < n - 1)(lambda: a_copy(j, z, 0).start())
        pl.when(z > 0)(lambda: a_copy(j, z, 1).start())
        pl.when(x == 1)(lambda: t_copy(j, z).start())
        kept = total.astype(BF).reshape(2, R, NC)
        rc[0, j] = kept[0]
        rc[1, j] = kept[1]

    def hop(j, h):
        @pl.when(z >= h)
        def _():
            a_copy(j, z - h, 0).wait_recv()
            pl.when(z < n - 1)(lambda: a_copy(j, z - h, 0).start())
            pl.when(x == 1)(lambda: t_copy(j, z - h).start())

        @pl.when(z + h < n)
        def _():
            a_copy(j, z + h, 1).wait_recv()
            pl.when(z > 0)(lambda: a_copy(j, z + h, 1).start())
            pl.when(x == 1)(lambda: t_copy(j, z + h).start())

    def g_copy(k):
        rows = rows_of(k, GB)
        return remote(g_send.at[:, rows], g_recv.at[:, rows], g_s, g_r.at[k], row=other_c)

    def add_grads(j, k, size, both):
        rows = rows_of(k, size)
        v = dot_last(dg[rows, wide(j)], e[j, 0].reshape(T, NC))
        if both:
            v = v + dot_last(dg[rows_of(k, size, F), wide(j)], e[j, 1].reshape(T, NC))
        gacc[0, rows, :] = gacc[0, rows, :] + v[:, :T2]
        gacc[1, rows, :] = gacc[1, rows, :] + v[:, T2:]

    def sum_grads(j, both):
        @pl.when(j < J - 1)
        def _():
            for k in range(F // GC):
                add_grads(j, k, GC, both)

        @pl.when(j == J - 1)
        def _():
            def body(k, carry):
                add_grads(j, k, GB, both)
                rows = rows_of(k, GB)
                g_send[:, rows, :] = gacc[:, rows, :].astype(BF)
                g_copy(k).start()
                return carry

            lax.fori_loop(0, F // GB, body, 0)

    def grads(j):
        sum_grads(j, False)

    def both_grads(j):
        remote(e.at[j, 0], e.at[j, 1], t_s, t_r.at[j], layer=other_x).wait_recv()
        sum_grads(j, True)

    def weights(j):
        def body(k, carry):
            rows = rows_of(k, 2 * GC)
            dg[rows, wide(j)] = (scale * mm(fx[rows, :T], e[j, 0].reshape(T, NC))).astype(BF)
            return carry

        lax.fori_loop(0, F // GC, body, 0)

    def both_weights(j):
        def body(k, carry):
            rows = rows_of(k, 2 * GC)
            dg[rows, wide(j)] = (scale * mm(fx[rows, :], e[j].reshape(2 * T, NC))).astype(BF)
            return carry

        lax.fori_loop(0, F // GC, body, 0)

    cuts = (0, J // 3, 2 * J // 3, J)

    def b_copy(k, p):
        dx, dc = k // 2, k % 2
        to_x = other_x if dx else x
        to_c = other_c if dc else c
        some = pl.ds(0, J) if p is None else pl.ds(cuts[p], cuts[p + 1] - cuts[p])
        return remote(rc.at[to_c, some], rb.at[x, c, some], b_s.at[k], b_r.at[k], layer=to_x, row=to_c)

    def start_b(p):
        for k in range(1, 4):
            b_copy(k, p).start()

    def early_b(j):
        for p in range(2):
            pl.when(j == cuts[p + 1] - 1)(functools.partial(start_b, p))

    def late_b(j):
        pl.when(j == J - 1)(lambda: start_b(2))

    stages = (
        (0, None, front), (1, None, relay_near), (2, None, relay_far), (3, None, final), (3, None, early_b),
        (4, None, lambda j: hop(j, 1)), (5, None, lambda j: hop(j, 2)), (6, None, lambda j: hop(j, 3)), (6, None, late_b),
        (LAG1, 1, grads), (LAG1 + 1, 1, weights), (LAG0, 0, both_grads), (LAG0, 0, both_weights))
    steps = J + max(LAG0, LAG1)
    share = pl.cdiv(nd, LAG0)

    def pipe(s, carry):
        for lag, side, act in stages:
            end = J - LATE if act in (weights, both_weights) else J
            live = jnp.logical_and(s >= lag, s < end + lag)
            if side is not None:
                live = jnp.logical_and(live, x == side)
            pl.when(live)(functools.partial(act, s - lag))
        for i in range(share):
            pl.when(jnp.logical_and(x == 0, s * share + i < nd))(functools.partial(expand, s * share + i))
        return carry

    @pl.when(x == 1)
    def _():
        def body(b, carry):
            expand(b)
            return carry

        lax.fori_loop(0, nd, body, 0)

    lax.fori_loop(0, steps, pipe, 0)

    spent = (J - LATE) * NC

    def keep_fx(k, carry):
        rows = rows_of(k, GC)
        dg[rows, spent:spent + T] = fx[rows, :T]

        @pl.when(x == 0)
        def _():
            dg[rows, spent + T:spent + 2 * T] = fx[rows, T:]

        return carry

    lax.fori_loop(0, 2 * F // GC, keep_fx, 0)
    for h in range(LATE):
        dg[2 * h * T:(2 * h + 1) * T, spent + 2 * T:spent + 2 * T + NC] = e[J - LATE + h, 0].reshape(T, NC)

        @pl.when(x == 0)
        def _():
            dg[(2 * h + 1) * T:(2 * h + 2) * T, spent + 2 * T:spent + 2 * T + NC] = e[J - LATE + h, 1].reshape(T, NC)

    def mask_body(k, carry):
        g_copy(k).wait_recv()
        rows = rows_of(k, GB)
        for h in range(2):
            seen = jnp.concatenate(
                [feats[k * (GB // KC) + i, h * T2:(h + 1) * T2, :] for i in range(GB // KC)], axis=1).T
            v = (g_send[h, rows, :].astype(jnp.float32) + g_recv[h, rows, :].astype(jnp.float32)) * scale
            gt[h, rows, :] = jnp.where(seen.astype(jnp.float32) > 0, v, 0.0).astype(BF)
        return carry

    lax.fori_loop(0, F // GB, mask_body, 0)
    rb[x, c] = rc[c]
    theirs = pl.ds(pl.multiple_of(other_c * T2, T2), T2)
    remote(pre.at[:, theirs], pre_recv, p_s, p_r.at[0], row=other_c).wait_send()
    all_f.wait_send()
    m_copy.wait_send()

    def x_all(dz, k):
        return remote(xsend.at[k], xg.at[z, c], x_s.at[dz, k], x_r.at[dz, k, 0], feat=far(dz), row=other_c)

    for dz, k in x_list:
        unless_ends(dz, lambda: x_all(dz, k).wait_send())

    def y_all(k, to, at):
        cc = c if k == 0 else other_c
        return remote(xg.at[back(2), cc], xg.at[back(2), cc], y_s.at[k], x_r.at[at, k, 0], feat=far(to))

    for k in range(2):
        relays(lambda to, at: y_all(k, to, at).wait_send())

    def sent(src, sem, **where):
        remote(src, src, sem, a_r.at[0, 0], **where).wait_send()

    for k in range(n):
        @pl.when(z == k)
        def _():
            if k < n - 1:
                sent(osend.at[:, pl.ds(k + 1, n - 1 - k)], rs_s.at[0], feat=k + 1)
                sent(e.at[:, 0, pl.ds(0, k + 1)], a_s.at[0], feat=k + 1)
            if k > 0:
                sent(osend.at[:, pl.ds(0, k)], rs_s.at[1], feat=k - 1)
                sent(e.at[:, 0, pl.ds(k, n - k)], a_s.at[1], feat=k - 1)

    pl.when(x == 0)(lambda: sent(nsend, n_s, layer=other_x))
    pl.when(x == 1)(lambda: sent(e.at[:, 0], t_s, layer=other_x))
    for k in range(1, 4):
        b_copy(k, None).wait_recv()
    for k in range(1, 4):
        b_copy(k, None).wait_send()

    sent(g_send, g_s, row=other_c)


def weight_kernel(
    dg, gt, xs, rb, enc_grad, dec_grad, bgrad, rebuilt,
    parts, late, ebuf, bbuf, rbuf, dsem, lsem, esem, bsem, rsem,
):
    F, T2 = gt.shape[1:]
    T, H = xs.shape
    NC = KC
    R2 = parts.shape[0]
    nb, nl = F // KC, F // LC
    x = lax.axis_index("layer")
    scale = float(T) ** (-0.5)
    done = H - LATE * NC

    def rows_of(i, size):
        return pl.ds(pl.multiple_of(i * size, size), size)

    def d_copy(i):
        rows = rows_of(i, 2 * KC)
        return pltpu.make_async_copy(
            dg.at[rows, pl.ds(0, done)], dec_grad.reshape(2 * F, H).at[rows, pl.ds(0, done)], dsem.at[i])

    def l_copy(i):
        rows = rows_of(i, 2 * LC)
        return pltpu.make_async_copy(
            late.at[rows], dec_grad.reshape(2 * F, H).at[rows, pl.ds(done, LATE * NC)], lsem.at[i])

    def e_copy(i):
        slot = lax.rem(i, 4)
        return pltpu.make_async_copy(ebuf.at[slot], enc_grad.at[rows_of(i, KC)], esem.at[slot])

    b_copy = pltpu.make_async_copy(bbuf, bgrad, bsem)
    r_copy = pltpu.make_async_copy(rbuf, rebuilt.reshape(R2, 2 * H), rsem)
    for i in range(nb):
        d_copy(i).start()

    def late_block(i, carry):
        rows = rows_of(i, 2 * LC)

        def chunk(h, inner):
            cols = rows_of(h, NC)

            @pl.when(x == 0)
            def _():
                late[rows, cols] = (scale * mm(dg[rows, done:done + 2 * T], dg[rows_of(h, 2 * T), done + 2 * T:done + 2 * T + NC])).astype(BF)

            @pl.when(x == 1)
            def _():
                late[rows, cols] = (scale * mm(dg[rows, done:done + T], dg[pl.ds(pl.multiple_of(2 * h * T, T), T), done + 2 * T:done + 2 * T + NC])).astype(BF)

            return inner

        lax.fori_loop(0, LATE, chunk, 0)
        l_copy(i).start()
        return carry

    ones = jnp.ones((8, 2 * T2), BF)

    def block(i, carry):
        rows = rows_of(i, KC)
        g = jnp.concatenate([gt[0, rows, :], gt[1, rows, :]], axis=1)
        pl.when(i >= 4)(lambda: e_copy(i - 4).wait())
        ebuf[lax.rem(i, 4)] = mm(g, xs[...]).astype(BF)
        e_copy(i).start()
        bbuf[:, rows] = dot_last(ones, g)[0:1]
        return carry

    lax.fori_loop(0, nl, late_block, 0)
    for h in range(2):
        for j in range(rb.shape[2]):
            lo = h * H + j * NC
            parts[:, lo:lo + NC] = rb[:, h, j].reshape(R2, NC)
    i = lax.broadcasted_iota(jnp.int32, (R2, R2), 0)
    j = lax.broadcasted_iota(jnp.int32, (R2, R2), 1)
    inter = (j == (i % 2) * (R2 // 2) + i // 2).astype(BF)
    rbuf[...] = mm(inter, parts[...]).astype(BF)
    r_copy.start()
    lax.fori_loop(0, nb, block, 0)
    b_copy.start()
    for i in range(nb):
        d_copy(i).wait()
    for i in range(max(nb - 4, 0), nb):
        e_copy(i).wait()
    for i in range(nl):
        l_copy(i).wait()
    r_copy.wait()
    b_copy.wait()


def fused(resid_buf, shuffle, mlp_out, enc_weight, dec_weight, enc_bias, dec_bias):
    n = lax.axis_size("feat")
    R = resid_buf.shape[0]
    F, H = enc_weight.shape[1:]
    T = R * n * 2
    T2, CR = T // 2, 2 * R
    J = H // KC
    NC, nk = H // J, F // KC
    Q = halves_of(H)
    HX = H // Q
    f32 = jnp.float32
    vm = pl.BlockSpec(memory_space=pltpu.VMEM)
    hbm = pl.BlockSpec(memory_space=pl.ANY)
    dma = pltpu.SemaphoreType.DMA
    vmem = pltpu.VMEM
    shape = jax.ShapeDtypeStruct
    outs = ((2 * F, H), (T, H), (2, F, T2), (2, 2, J, R, NC))
    held = sum(2 * math.prod(a) for a in outs)
    dg, xs, gt, rb = pl.pallas_call(
        functools.partial(step_kernel, n, J),
        out_shape=tuple(vmem(a, BF) for a in outs),
        in_specs=[vm, vm, vm, hbm, hbm, vm, vm],
        out_specs=(vm,) * 4,
        scratch_shapes=[
            vmem((2 * F, 2 * T), BF), vmem((J, 2, n, CR, NC), BF), vmem((F, H), BF), vmem((3, 2 * DC, H), BF),
            vmem((2, Q, R, HX), BF), vmem((n, 2, Q, R, HX), BF),
            vmem((2, R, H), BF), vmem((R, H), BF), vmem((1, H), f32),
            vmem((nk, T, KC), f32), vmem((nk, T2, KC), f32), vmem((nk, T, KC), BF),
            vmem((J, T, NC), BF), vmem((J, T, NC), BF), vmem((J, n, CR, NC), f32),
            vmem((J, n, CR, NC), BF), vmem((J, n, CR, NC), BF), vmem((J, n, CR, NC), BF),
            vmem((2, J, R, NC), BF),
            vmem((2, F, T2), f32), vmem((2, F, T2), BF), vmem((2, F, T2), BF),
            dma, dma((4,)), dma((n, 2)), dma((n, 2, Q)), dma((2,)), dma, dma,
            dma, dma((nk,)), dma, dma, dma, dma((J,)),
            dma((2,)), dma((J, 2, 2)), dma((2,)), dma((J, n)), dma, dma((J,)),
            dma((4,)), dma((4,)), dma, dma((F // GB,)),
        ],
        compiler_params=pltpu.CompilerParams(
            collective_id=0, has_side_effects=True, vmem_limit_bytes=VMEM_LIMIT - held),
    )(resid_buf, shuffle.reshape(1, T), mlp_out, enc_weight[0], dec_weight[0], enc_bias, dec_bias)
    enc_grad, dec_grad, bgrad, rebuilt = pl.pallas_call(
        weight_kernel,
        out_shape=(
            shape((F, H), BF), shape((F, 2, H), BF), shape((1, F), f32), shape((R, 2, 2 * H), BF)),
        in_specs=[vm] * 4,
        out_specs=(hbm,) * 4,
        scratch_shapes=[
            vmem((2 * R, 2 * H), BF), vmem((2 * F, LATE * NC), BF), vmem((4, KC, H), BF), vmem((1, F), f32), vmem((2 * R, 2 * H), BF),
            dma((nk,)), dma((F // LC,)), dma((4,)), dma, dma],
        compiler_params=pltpu.CompilerParams(vmem_limit_bytes=VMEM_LIMIT // 3),
    )(dg, gt, xs, rb)
    return rebuilt, enc_grad[None], dec_grad[None], bgrad


def chosen(resid_buf, shuffle, mlp_out, enc_weight, dec_weight, enc_bias, dec_bias):
    args = (resid_buf, shuffle, mlp_out, enc_weight, dec_weight, enc_bias, dec_bias)
    rows, width = resid_buf.shape[0], enc_weight.shape[2]
    fits = (
        lax.axis_size("layer") == LAYERS == 2 and lax.axis_size("row") == 2
        and lax.axis_size("feat") == 4 and rows % 16 == 0
        and width % KC == 0 and width // KC > LATE
        and rows * 2 * lax.axis_size("feat") == KC and enc_weight.shape[1] % GC == 0)
    return fused(*args) if fits else on_device(*args)


def solution(mesh):
    return jax.shard_map(
        chosen,
        mesh=mesh,
        in_specs=(
            P(("groups", "feat", "row"), None, None),
            P("groups"),
            P(("groups", "feat", "row"), None, None),
            P("layer", "feat", "row"),
            P("layer", "feat", None, "row"),
            P("layer", "feat"),
            P(),
        ),
        out_specs=(
            P(("groups", "feat", "row"), None, None),
            P(("groups", "layer"), "feat", "row"),
            P(("groups", "layer"), "feat", None, "row"),
            P(("groups", "layer"), "feat"),
        ),
        check_vma=False,
    )
```
